32 devices in a mesh: batch: 8 (over z, y), seq: 4 (over x, core).
Axes of the slice: x: 2, y: 2, z: 4, core: 2. Of those that a mesh axis runs over, the one named last changes fastest.
Arguments:
- frames_in: bfloat16 [2048, 8, 1024], P('seq', 'batch'), may hold values from -6 to 6
- skip_in: bfloat16 [2048, 8, 1024], P('seq', 'batch'), may hold values from -6 to 6
- flow_times: float32 [8], P('batch'), may hold values from 0 to 1
- lengths: int32 [8], P('batch'), may hold values from 256 to 2048
- skip_weight: bfloat16 [2048, 1024], P(('batch', 'seq')), may hold values from -0.125 to 0.125
- qkv_weight: bfloat16 [1024, 3072], P(('batch', 'seq')), may hold values from -0.1875 to 0.1875
- output_weight: bfloat16 [1024, 1024], P(('batch', 'seq')), may hold values from -2 to 2
- up_weight: bfloat16 [1024, 4096], P(('batch', 'seq')), may hold values from -0.1875 to 0.1875
- up_bias: bfloat16 [4096], P(('batch', 'seq')), may hold values from -3 to 3
- down_weight: bfloat16 [4096, 1024], P(('batch', 'seq')), may hold values from -0.09375 to 0.09375
- down_bias: bfloat16 [1024], P(('batch', 'seq')), may hold values from -3 to 3
- modulate_weight: bfloat16 [1024, 6144], P(('batch', 'seq')), may hold values from -0.375 to 0.375
- modulate_bias: bfloat16 [6144], P(('batch', 'seq')), may hold values from -3 to 3
- output_grad: bfloat16 [2048, 8, 1024], P('seq', 'batch'), may hold values from -6 to 6
Outputs:
- layer_out: bfloat16 [2048, 8, 1024], P('seq', 'batch')
- grad_frames: float32 [2048, 8, 1024], P('seq', 'batch')
- grad_skip: float32 [2048, 8, 1024], P('seq', 'batch')
- grad_skip_weight: float32 [2048, 1024], P(('batch', 'seq'))
- grad_qkv_weight: float32 [1024, 3072], P(('batch', 'seq'))
- grad_output_weight: float32 [1024, 1024], P(('batch', 'seq'))
- grad_up_weight: float32 [1024, 4096], P(('batch', 'seq'))
- grad_up_bias: float32 [4096], P(('batch', 'seq'))
- grad_down_weight: float32 [4096, 1024], P(('batch', 'seq'))
- grad_down_bias: float32 [1024], P(('batch', 'seq'))
- grad_modulate_weight: float32 [1024, 6144], P(('batch', 'seq'))
- grad_modulate_bias: float32 [6144], P(('batch', 'seq'))
The draws below stay inside these ranges and needn't reach their ends.
Inputs may be any that keep to these rules, and one draw needn't show every extreme that they name: lengths[u] counts the real frames of utterance u; the frames from lengths[u] to 2047 are padding and never serve as keys.
All inputs are finite; a program needn't handle non-finite values.
Results may differ from the reference program's by a relative error of at most 0.02.
Values may be sent and summed in bfloat16 or wider, within the bound.
No kernel may reach another device: no remote copies, remote signals or barrier semaphores. Data moves between devices by JAX's collectives and lax.ppermute only.
A program may use at most 320 MiB of HBM per device.

```python
import math
import jax
import jax.numpy as jnp
from jax import lax

D = 1024
HEADS = 16
HEAD_DIM = 64
FF = 4096
FRAMES = 2048
UTTS = 8


def with_ends(values, rng, smallest, top_value):
    dims = values.shape
    spot = [jax.random.randint(jax.random.fold_in(rng, axis), (), 0, dims[axis]) for axis in range(len(dims))]
    values = values.at[tuple(spot)].set(smallest)
    longest = dims.index(max(dims))
    spot[longest] = (spot[longest] + 1) % dims[longest]
    return values.at[tuple(spot)].set(top_value)


def block_scale(key, extent, pieces, low, high):
    level, own = 1.0, jax.random.fold_in(key, 6)
    for position, blocks in pieces:
        draws = jnp.exp(jax.random.uniform(jax.random.fold_in(own, position), (blocks,), jnp.float32, low / len(pieces), high / len(pieces)))
        level = level * jnp.repeat(draws, extent[position] // blocks).reshape([-1 if axis == position else 1 for axis in range(len(extent))])
    return level


def scatter_about(stream_key, dims, width, bound, pieces=(), kind=jnp.bfloat16):
    values = width * jax.random.normal(stream_key, dims, jnp.float32)
    if pieces:
        values = values * block_scale(stream_key, dims, pieces, -0.22, 0.18)
    return jnp.clip(values, -bound, bound).astype(kind)


def setup_inputs(seed: int = 0) -> dict:
    arg_keys = jax.random.split(jax.random.key(seed), 15)
    frames_in = scatter_about(arg_keys[0], (FRAMES, UTTS, D), 1.0, 6.0, ((0, 4), (1, 8)))
    skip_in = scatter_about(arg_keys[1], (FRAMES, UTTS, D), 1.0, 6.0, ((0, 4), (1, 8)))
    flow_times = jnp.clip(1.0 * jax.random.uniform(arg_keys[2], (UTTS,), jnp.float32) ** block_scale(arg_keys[2], (UTTS,), ((0, 8),), -0.2, 0.2), 0.0, 1.0)
    lengths = with_ends(jax.random.randint(arg_keys[3], (UTTS,), FRAMES // 8, FRAMES + 1), jax.random.fold_in(arg_keys[3], 1), FRAMES // 8, FRAMES).astype(jnp.int32)
    skip_weight = scatter_about(arg_keys[4], (2 * D, D), (2 * D) ** -0.5, 0.125, ((0, 32),))
    qkv_weight = scatter_about(arg_keys[5], (D, 3 * D), D ** -0.5, 0.1875, ((0, 32),))
    output_weight = scatter_about(arg_keys[6], (D, D), (max(1, D * 16 // FRAMES)) ** -0.5, 2.0, ((0, 32),))
    up_weight = scatter_about(arg_keys[7], (D, FF), D ** -0.5, 0.1875, ((0, 32),))
    up_bias = scatter_about(arg_keys[8], (FF,), 0.5, 3.0, ((0, 32),))
    down_weight = scatter_about(arg_keys[9], (FF, D), FF ** -0.5, 0.09375, ((0, 32),))
    down_bias = scatter_about(arg_keys[10], (D,), 0.5, 3.0, ((0, 32),))
    modulate_weight = scatter_about(arg_keys[11], (D, 6 * D), (D // 4) ** -0.5, 0.375, ((0, 32),))
    modulate_bias = scatter_about(arg_keys[12], (6 * D,), 0.5, 3.0, ((0, 32),))
    output_grad = scatter_about(arg_keys[13], (FRAMES, UTTS, D), 1.0, 6.0, ((0, 4), (1, 8)))
    return {"frames_in": frames_in, "skip_in": skip_in, "flow_times": flow_times, "lengths": lengths, "skip_weight": skip_weight, "qkv_weight": qkv_weight, "output_weight": output_weight, "up_weight": up_weight, "up_bias": up_bias, "down_weight": down_weight, "down_bias": down_bias, "modulate_weight": modulate_weight, "modulate_bias": modulate_bias, "output_grad": output_grad}


@jax.custom_vjp
def low(v):
    return lax.optimization_barrier(v.astype(jnp.bfloat16)).astype(jnp.float32)

@jax.custom_vjp
def low_back(v):
    return v

def low_keep(v):
    return (low(v), None)

def low_pass(kept, grad):
    return (grad,)

def back_keep(v):
    return (v, None)

def back_low(kept, grad):
    return (low(grad),)
low.defvjp(low_keep, low_pass)
low_back.defvjp(back_keep, back_low)
epsilon = 1e-06
masked_score = -1e+30

def rms_norm(values):
    return values * lax.rsqrt(lax.optimization_barrier(jnp.mean(values * values, axis=-1, keepdims=True)) + epsilon)

def modulated(hidden, scale_rows, shift_rows):
    return rms_norm(hidden) * (1.0 + scale_rows[None]) + shift_rows[None]

def gelu_tanh(pre_values):
    return jax.nn.gelu(pre_values, approximate=True)

def time_embed(flow_times, embed_width):
    half_width = embed_width // 2
    frequency = jnp.exp(-math.log(10000.0) * jnp.arange(half_width, dtype=jnp.float32) / half_width)
    angles = 1000.0 * flow_times[:, None] * frequency[None, :]
    return jnp.concatenate([jnp.sin(angles), jnp.cos(angles)], axis=-1)

def rotary_tables(positions, head_size):
    half_dim = head_size // 2
    inverse = jnp.exp(-math.log(10000.0) * 2.0 * jnp.arange(half_dim, dtype=jnp.float32) / head_size)
    angles = positions.astype(jnp.float32)[:, None] * inverse[None, :]
    angles = jnp.concatenate([angles, angles], axis=-1)
    return (jnp.cos(angles), jnp.sin(angles))

def rotate(values, cosine, sine_table):
    half_dim = values.shape[-1] // 2
    turned = jnp.concatenate([-values[..., half_dim:], values[..., :half_dim]], axis=-1)
    return values * cosine + turned * sine_table

def attend(queries, keys_rot, values_cast, usable):
    frame_count = queries.shape[0]
    block_rows = math.gcd(frame_count, 512)

    def one_query(query_block):
        scores = low_back(jnp.einsum('qhd,khd->hqk', query_block, keys_rot, precision=lax.Precision.HIGHEST))
        scores = jnp.where(usable[None, None, :], scores, masked_score)
        top_score = lax.optimization_barrier(jnp.max(scores, axis=-1, keepdims=True))
        exponent = jnp.where(usable[None, None, :], jnp.exp(scores - top_score), 0.0)
        probability = exponent / lax.optimization_barrier(jnp.sum(exponent, axis=-1, keepdims=True))
        rounded = low(probability)
        mixed = jnp.einsum('hqk,khd->qhd', rounded, values_cast, precision=lax.Precision.HIGHEST)
        return low(low_back(mixed))
    blocks = queries.reshape(frame_count // block_rows, block_rows, HEADS, HEAD_DIM)
    result = lax.map(jax.checkpoint(one_query), blocks)
    return result.reshape(frame_count, HEADS, HEAD_DIM)

def layer(frames, skip_rows, silu_row, length, weights):
    skip_weight, qkv_weight, output_weight, up_weight, up_bias, down_weight, down_bias, modulate_weight, modulate_bias = weights
    highest = lax.Precision.HIGHEST
    frame_count = frames.shape[0]
    modulation = jnp.dot(silu_row[None, :], modulate_weight, precision=highest)[0] + modulate_bias
    shift_one, scale_one, gate_one, shift_two, scale_two, gate_two = jnp.split(modulation, 6, axis=-1)
    joined = jnp.concatenate([frames, skip_rows], axis=-1)
    hidden_zero = low_back(jnp.dot(joined, skip_weight, precision=highest))
    normed_one = low(modulated(hidden_zero, scale_one, shift_one))
    projected = low_back(jnp.dot(normed_one, qkv_weight, precision=highest))
    queries_raw, keys_raw, values_raw = jnp.split(projected, 3, axis=-1)
    positions = jnp.arange(frame_count, dtype=jnp.int32)
    cosine, sine_table = rotary_tables(positions, HEAD_DIM)
    cos_wide = cosine[:, None, :]
    sin_wide = sine_table[:, None, :]
    shape_three = (frame_count, HEADS, HEAD_DIM)
    queries = low(rotate(queries_raw.reshape(shape_three), cos_wide, sin_wide) * HEAD_DIM ** (-0.5))
    keys_rot = low(rotate(keys_raw.reshape(shape_three), cos_wide, sin_wide))
    values_cast = low(values_raw.reshape(shape_three))
    usable = positions < length
    attended = attend(queries, keys_rot, values_cast, usable).reshape(frame_count, D)
    attn_proj = low_back(jnp.dot(attended, output_weight, precision=highest))
    hidden_one = hidden_zero + gate_one[None, :] * attn_proj
    normed_two = low(modulated(hidden_one, scale_two, shift_two))
    pre_act = low_back(jnp.dot(normed_two, up_weight, precision=highest)) + up_bias[None, :]
    activated = low(gelu_tanh(pre_act))
    ffn_out = low_back(jnp.dot(activated, down_weight, precision=highest)) + down_bias[None, :]
    return hidden_one + gate_two[None, :] * ffn_out

def reference(frames_in, skip_in, flow_times, lengths, skip_weight, qkv_weight, output_weight, up_weight, up_bias, down_weight, down_bias, modulate_weight, modulate_bias, output_grad):
    weight_set = tuple((matrix.astype(jnp.float32) for matrix in (skip_weight, qkv_weight, output_weight, up_weight, up_bias, down_weight, down_bias, modulate_weight, modulate_bias)))
    silu_rows = low(jax.nn.silu(time_embed(flow_times.astype(jnp.float32), D)))
    frame_major = jnp.swapaxes(frames_in.astype(jnp.float32), 0, 1)
    skip_major = jnp.swapaxes(skip_in.astype(jnp.float32), 0, 1)
    grad_major = jnp.swapaxes(output_grad.astype(jnp.float32), 0, 1)
    zeros = tuple((jnp.zeros_like(matrix) for matrix in weight_set))

    def utterance_step(totals, current):
        frame_rows, skip_rows, silu_row, length, grad_rows = current

        def forward_one(frame_part, skip_part, weights):
            return layer(frame_part, skip_part, silu_row, length, weights)
        layer_value, pullback = jax.vjp(forward_one, frame_rows, skip_rows, weight_set)
        grad_frame, grad_skip_rows, grad_weights = pullback(grad_rows)
        totals = jax.tree.map(jnp.add, totals, grad_weights)
        return (totals, (layer_value.astype(jnp.bfloat16), grad_frame, grad_skip_rows))
    totals, (outputs, grad_frame_all, grad_skip_all) = lax.scan(utterance_step, zeros, (frame_major, skip_major, silu_rows, lengths, grad_major))
    return (jnp.swapaxes(outputs, 0, 1), jnp.swapaxes(grad_frame_all, 0, 1), jnp.swapaxes(grad_skip_all, 0, 1), totals[0], totals[1], totals[2], totals[3], totals[4], totals[5], totals[6], totals[7], totals[8])
```

```python
import functools
import math

import jax
import jax.numpy as jnp
from jax import lax
from jax.experimental import pallas as pl
from jax.experimental.pallas import tpu as pltpu
from jax.sharding import PartitionSpec as P

HEADS = 16
HEAD_DIM = 64
epsilon = 1e-06
masked_score = -1e30
f32 = jnp.float32
bf16 = jnp.bfloat16
ALL = ("batch", "seq")


def rms_norm(values):
    return values * lax.rsqrt(jnp.mean(values * values, axis=-1, keepdims=True) + epsilon)


def modulated(hidden, scale_rows, shift_rows):
    return rms_norm(hidden) * (1.0 + scale_rows) + shift_rows


def gelu_tanh(pre_values):
    return jax.nn.gelu(pre_values, approximate=True)


def time_embed(flow_times, embed_width):
    half_width = embed_width // 2
    frequency = jnp.exp(-math.log(10000.0) * jnp.arange(half_width, dtype=f32) / half_width)
    angles = 1000.0 * flow_times[:, None] * frequency[None, :]
    return jnp.concatenate([jnp.sin(angles), jnp.cos(angles)], axis=-1)


def params(semantics=None):
    return pltpu.CompilerParams(dimension_semantics=semantics, vmem_limit_bytes=60 * 1024 * 1024)


class Net:
    def __init__(self, batch, seq):
        self.batch, self.seq, self.n = batch, seq, batch * seq
        self.d = lax.axis_index("batch") * seq + lax.axis_index("seq")
        self.b = lax.axis_index("batch")
        self.s = lax.axis_index("seq")
        self.core = self.d & 1

    def swap(self, value, offset):
        return lax.ppermute(value, ALL, [(i, i ^ offset) for i in range(self.n)])

    def swap_by_core(self, value, even, odd):
        pairs = [(i, i ^ (odd if i & 1 else even)) for i in range(self.n)]
        return lax.ppermute(value, ALL, pairs)

    def sum_all(self, value):
        bit = 1
        while bit < self.n:
            value = value + self.swap(value, bit)
            bit *= 2
        return value


def after(value, *others):
    return lax.optimization_barrier((value,) + tuple(others))[0]


def place(pieces, tables, count, columns=None):
    rows, width = pieces[0].shape[1:]
    columns = columns or (width,)
    counts = [p.shape[0] for p in pieces]
    total = sum(counts)
    table = jnp.concatenate(tables, axis=-1).astype(jnp.int32)
    if table.ndim == 1:
        table = jnp.broadcast_to(table[None], (len(columns), total))

    def kernel(table_ref, *refs):
        sources = refs[: len(pieces)]
        outs = refs[len(pieces) : len(pieces) + len(columns)]
        sems = refs[-1]
        copies = []
        at = 0
        for source, number in zip(sources, counts):
            for j in range(number):
                left = 0
                for o, wide in enumerate(columns):
                    copies.append(
                        pltpu.make_async_copy(
                            source.at[j, :, pl.ds(left, wide)],
                            outs[o].at[table_ref[o, at]],
                            sems.at[o, at],
                        )
                    )
                    left += wide
                at += 1
        for copy in copies:
            copy.start()
        for copy in copies:
            copy.wait()

    any_spec = pl.BlockSpec(memory_space=pl.ANY)
    outs = pl.pallas_call(
        kernel,
        out_shape=[jax.ShapeDtypeStruct((count, rows, wide), pieces[0].dtype) for wide in columns],
        in_specs=[pl.BlockSpec(memory_space=pltpu.SMEM)] + [any_spec] * len(pieces),
        out_specs=[any_spec] * len(columns),
        scratch_shapes=[pltpu.SemaphoreType.DMA((len(columns), total))],
        compiler_params=params(),
    )(table, *pieces)
    return [out.reshape(count * rows, wide) for out, wide in zip(outs, columns)]


def combine(inputs, tables, dtype):
    rows, width = inputs[0].shape[1:]
    count = tables[0].shape[0]
    table = jnp.stack([jnp.asarray(t, jnp.int32) for t in tables])

    def kernel(table_ref, *refs):
        total = refs[0][...].astype(f32)
        for ref in refs[1:-1]:
            total = total + ref[...].astype(f32)
        refs[-1][...] = total.astype(dtype)

    def spec(j):
        return pl.BlockSpec((1, rows, width), lambda i, t: (t[j, i], 0, 0))

    return pl.pallas_call(
        kernel,
        out_shape=jax.ShapeDtypeStruct((count, rows, width), dtype),
        grid_spec=pltpu.PrefetchScalarGridSpec(
            num_scalar_prefetch=1,
            grid=(count,),
            in_specs=[spec(j) for j in range(len(inputs))],
            out_specs=pl.BlockSpec((1, rows, width), lambda i, t: (i, 0, 0)),
        ),
        compiler_params=params(("arbitrary",)),
    )(table, *inputs)


def gather_start(net, shard):
    return jnp.stack([shard] + [net.swap(shard, k << 3) for k in (1, 2, 3)])


def gather_finish(net, near):
    d, c = net.d, net.core
    z = jnp.arange(4, dtype=jnp.int32) << 3
    second = jnp.where(c == 0, 2, 4)
    third = 6 - second
    far = net.swap_by_core(near, 2, 4)
    half = jnp.concatenate([near, far], axis=0)
    other = net.swap_by_core(half, 4, 2)
    own = jnp.concatenate([d ^ z, d ^ z ^ second])
    last = own ^ third
    mate = d ^ 1
    mate_own = jnp.concatenate([mate ^ z, mate ^ z ^ third])
    mate_last = mate_own ^ second
    return (
        [half, other, net.swap(half, 1), net.swap(other, 1)],
        [own, last, mate_own, mate_last],
    )


def scatter_sum(net, grads, spot):
    d, c = net.d, net.core
    first = jnp.where(c == 0, 4, 2)
    second = 6 - first
    j = jnp.arange(16, dtype=jnp.int32)
    r1 = net.swap(combine([grads], [spot(d ^ 1 ^ (j << 1))], bf16), 1)
    t = jnp.arange(8, dtype=jnp.int32)
    off = first ^ ((t >> 1) << 3) ^ ((t & 1) * second)
    r2 = net.swap_by_core(combine([grads, r1], [spot(d ^ off), off >> 1], bf16), 4, 2)
    z = jnp.arange(4, dtype=jnp.int32)
    off = second ^ (z << 3)
    r3 = net.swap_by_core(
        combine([grads, r1, r2], [spot(d ^ off), off >> 1, z * 2 + 1], bf16), 2, 4
    )
    z = z[1:]
    parts = combine([grads, r1, r2, r3], [spot(d ^ (z << 3)), z << 2, z * 2, z], bf16)
    zs = [net.swap(parts[k - 1 : k], k << 3) for k in (1, 2, 3)]
    zero = jnp.zeros((1,), jnp.int32)
    own = combine(
        [grads, r1, r2, r3] + zs, [spot(d + zero), zero, zero, zero, zero, zero, zero], f32
    )
    return own[0]


def rope(values, cosine, sine, back):
    width = values.shape[-1]
    lane = lax.broadcasted_iota(jnp.int32, values.shape, 1)
    early = (lane & (HEAD_DIM - 1)) < HEAD_DIM // 2
    source = values * sine if back else values
    ahead = pltpu.roll(source, width - HEAD_DIM // 2, 1)
    behind = pltpu.roll(source, HEAD_DIM // 2, 1)
    if back:
        turned = jnp.where(early, ahead, -behind)
        return values * cosine + turned
    turned = jnp.where(early, -ahead, behind)
    return values * cosine + turned * sine


def wide_tables(cos_ref, sin_ref, width):
    reps = width // cos_ref.shape[-1]
    cosine = jnp.concatenate([cos_ref[...]] * reps, axis=-1)
    sine = jnp.concatenate([sin_ref[...]] * reps, axis=-1)
    return cosine, sine


def qkv_kernel(x_ref, w_ref, cos_ref, sin_ref, q_ref, k_ref, v_ref):
    width = q_ref.shape[-1]
    result = jnp.dot(x_ref[...], w_ref[...], preferred_element_type=f32)
    cosine, sine = wide_tables(cos_ref, sin_ref, width)
    scale = HEAD_DIM ** (-0.5)
    q_ref[...] = (rope(result[:, :width], cosine, sine, False) * scale).astype(bf16)
    k_ref[...] = rope(result[:, width : 2 * width], cosine, sine, False).astype(bf16)
    v_ref[...] = result[:, 2 * width :].astype(bf16)


def qkv_project(x, w, cosine, sine):
    rows, depth = x.shape
    width = w.shape[1] // 3
    block = min(512, rows)
    row = lambda wide: pl.BlockSpec((block, wide), lambda i: (i, 0))
    return pl.pallas_call(
        qkv_kernel,
        grid=(rows // block,),
        out_shape=[jax.ShapeDtypeStruct((rows, width), bf16)] * 3,
        in_specs=[row(depth), pl.BlockSpec(w.shape, lambda i: (0, 0)), row(128), row(128)],
        out_specs=[row(width)] * 3,
        compiler_params=params(("arbitrary",)),
    )(x, w, cosine, sine)


def attend_kernel(heads, q_ref, k_ref, v_ref, bias_ref, o_ref, lse_ref):
    q = q_ref[...]
    k = k_ref[...]
    v = v_ref[...]
    bias = bias_ref[...]
    lane = lax.broadcasted_iota(jnp.int32, q.shape, 1) // HEAD_DIM
    spot = lax.broadcasted_iota(jnp.int32, lse_ref.shape, 1)
    out = jnp.zeros(q.shape, f32)
    lse = jnp.zeros(lse_ref.shape, f32)
    for h in range(heads):
        mine = lane == h
        qh = jnp.where(mine, q, jnp.zeros_like(q))
        s = lax.dot_general(qh, k, (((1,), (1,)), ((), ())), preferred_element_type=f32) + bias
        top = jnp.max(s, axis=-1, keepdims=True)
        p = jnp.exp(s - top)
        total = jnp.sum(p, axis=-1, keepdims=True)
        o = jnp.dot(p.astype(bf16), v, preferred_element_type=f32) / total
        out = jnp.where(mine, o, out)
        lse = jnp.where(spot == h, top + jnp.log(total), lse)
    o_ref[...] = out.astype(bf16)
    lse_ref[...] = lse


def attend(q, k, v, bias, heads):
    rows, width = q.shape
    block = 256
    row = lambda wide: pl.BlockSpec((block, wide), lambda i: (i, 0))
    whole = pl.BlockSpec((rows, width), lambda i: (0, 0))
    return pl.pallas_call(
        functools.partial(attend_kernel, heads),
        grid=(rows // block,),
        out_shape=[jax.ShapeDtypeStruct((rows, width), bf16), jax.ShapeDtypeStruct((rows, 128), f32)],
        in_specs=[row(width), whole, whole, pl.BlockSpec((1, rows), lambda i: (0, 0))],
        out_specs=[row(width), row(128)],
        compiler_params=params(("arbitrary",)),
    )(q, k, v, bias)


def attend_back_kernel(
    heads,
    q_ref,
    do_ref,
    o_ref,
    lse_ref,
    k_ref,
    v_ref,
    kt_ref,
    bias_ref,
    cosq_ref,
    sinq_ref,
    cosk_ref,
    sink_ref,
    dq_ref,
    dk_ref,
    dv_ref,
    p_all,
    ds_all,
    dk_acc,
    dv_acc,
):
    step = pl.program_id(0)
    q = q_ref[...]
    do = do_ref[...]
    k = k_ref[...]
    v = v_ref[...]
    block, width = q.shape
    lane = lax.broadcasted_iota(jnp.int32, q.shape, 1) // HEAD_DIM
    product = (do.astype(f32) * o_ref[...].astype(f32)).T
    lse_t = lse_ref[...].T
    bias = bias_ref[...]
    contract = (((1,), (1,)), ((), ()))
    q_parts, do_parts, dq_parts = [], [], []
    for h in range(heads):
        mine = lane == h
        qh = jnp.where(mine, q, jnp.zeros_like(q))
        doh = jnp.where(mine, do, jnp.zeros_like(do))
        q_parts.append(qh)
        do_parts.append(doh)
        row_dot = jnp.sum(product[h * HEAD_DIM : (h + 1) * HEAD_DIM], axis=0, keepdims=True)
        s = lax.dot_general(k, qh, contract, preferred_element_type=f32)
        p = jnp.exp(s + bias - lse_t[h : h + 1])
        dp = lax.dot_general(v, doh, contract, preferred_element_type=f32)
        ds = (p * (dp - row_dot)).astype(bf16)
        p_all[:, h * block : (h + 1) * block] = p.astype(bf16)
        ds_all[:, h * block : (h + 1) * block] = ds
        dq_parts.append(
            jnp.dot(kt_ref[h * HEAD_DIM : (h + 1) * HEAD_DIM, :], ds, preferred_element_type=f32)
        )
    dv = jnp.dot(p_all[...], jnp.concatenate(do_parts, axis=0), preferred_element_type=f32)
    dk = jnp.dot(ds_all[...], jnp.concatenate(q_parts, axis=0), preferred_element_type=f32)

    @pl.when(step == 0)
    def _():
        dv_acc[...] = dv
        dk_acc[...] = dk

    @pl.when(step > 0)
    def _():
        dv_acc[...] += dv
        dk_acc[...] += dk

    dq = jnp.concatenate(dq_parts, axis=0).T
    cosine, sine = wide_tables(cosq_ref, sinq_ref, width)
    dq_ref[...] = (rope(dq, cosine, sine, True) * (HEAD_DIM ** (-0.5))).astype(bf16)

    @pl.when(step == pl.num_programs(0) - 1)
    def _():
        cosine, sine = wide_tables(cosk_ref, sink_ref, width)
        dk_ref[...] = rope(dk_acc[...], cosine, sine, True).astype(bf16)
        dv_ref[...] = dv_acc[...].astype(bf16)


def attend_back(q, k, v, o, do, lse, bias, cosine, sine, heads):
    rows, width = q.shape
    block = 256
    row = lambda wide: pl.BlockSpec((block, wide), lambda i: (i, 0))
    whole = lambda wide: pl.BlockSpec((rows, wide), lambda i: (0, 0))
    return pl.pallas_call(
        functools.partial(attend_back_kernel, heads),
        grid=(rows // block,),
        out_shape=[jax.ShapeDtypeStruct((rows, width), bf16)] * 3,
        in_specs=[
            row(width),
            row(width),
            row(width),
            row(128),
            whole(width),
            whole(width),
            pl.BlockSpec((width, rows), lambda i: (0, 0)),
            whole(block),
            row(128),
            row(128),
            whole(128),
            whole(128),
        ],
        out_specs=[row(width), whole(width), whole(width)],
        scratch_shapes=[
            pltpu.VMEM((rows, heads * block), bf16),
            pltpu.VMEM((rows, heads * block), bf16),
            pltpu.VMEM((rows, width), f32),
            pltpu.VMEM((rows, width), f32),
        ],
        compiler_params=params(("arbitrary",)),
    )(
        q,
        do,
        o,
        lse,
        k,
        v,
        k.T,
        jnp.broadcast_to(bias.reshape(rows, 1), (rows, block)),
        cosine,
        sine,
        cosine,
        sine,
    )


def body(
    mesh_sizes,
    frames_in,
    skip_in,
    flow_times,
    lengths,
    skip_weight,
    qkv_weight,
    output_weight,
    up_weight,
    up_bias,
    down_weight,
    down_bias,
    modulate_weight,
    modulate_bias,
    output_grad,
):
    batch, seq = mesh_sizes
    net = Net(batch, seq)
    n, d, s = net.n, net.d, net.s
    local, utts, width = frames_in.shape
    frames = frames_in.reshape(local, width)
    skips = skip_in.reshape(local, width)
    out_grad = output_grad.reshape(local, width).astype(f32)
    heads = HEADS // seq
    part = heads * HEAD_DIM
    rows = local * seq
    built = n == 32 and seq == 4
    wrow = width // n
    ff = up_weight.shape[1]

    seq_order = s ^ jnp.arange(seq, dtype=jnp.int32)
    by_part = qkv_weight.reshape(wrow, 3, seq, part)
    pieces = [
        lax.dynamic_index_in_dim(by_part, s ^ k, 2, keepdims=False).reshape(wrow, 3 * part)
        for k in range(seq)
    ]
    pieces = [p if k == 0 else net.swap(p, k) for k, p in enumerate(pieces)]
    if built:
        near = gather_start(net, skip_weight)
        got, spots = gather_finish(net, near)
        (full_skip,) = place(got, spots, n)
        qkv_four = jnp.stack(pieces)
        qkv_four = after(qkv_four, near)
        qkv_z = jnp.concatenate([qkv_four] + [net.swap(qkv_four, k << 3) for k in (1, 2, 3)])
        qkv_y = net.swap(qkv_z, 4)
        k16 = jnp.arange(16, dtype=jnp.int32)
        z_spots = d ^ (((k16 >> 2) << 3) | (k16 & 3))
        (full_qkv,) = place([qkv_z, qkv_y], [z_spots, z_spots ^ 4], n)
        ou = after(jnp.concatenate([output_weight, up_weight], axis=1), qkv_z)
        near_ou = gather_start(net, ou)
        got, spots = gather_finish(net, near_ou)
        spots = jnp.concatenate(spots)
        turned = spots ^ (s * (n // seq))
        full_output, full_up = place(
            got, [jnp.stack([turned, spots])], n, (width, ff)
        )
        near_down = gather_start(net, after(down_weight, near_ou))
        got, spots = gather_finish(net, near_down)
        (full_down,) = place(got, spots, n)
    else:
        gather = lambda w, ax: lax.all_gather(w, ax, axis=0, tiled=True)
        full_skip = gather(skip_weight, ALL)
        full_qkv = gather(jnp.stack(pieces)[seq_order], "batch")
        full_qkv = full_qkv.reshape(batch, seq, wrow, 3 * part)
        full_qkv = full_qkv.reshape(width, 3 * part)
        full_output = gather(output_weight, ALL).reshape(seq, width // seq, width)[seq_order]
        full_output = full_output.reshape(width, width)
        full_up = gather(up_weight, ALL)
        full_down = gather(down_weight, ALL)

    urow, drow = up_bias.shape[0], down_bias.shape[0]
    small = jnp.concatenate([up_bias.astype(f32), down_bias.astype(f32), flow_times])
    small_width = -(-small.shape[0] // 128) * 128
    small = jnp.pad(small, (0, small_width - small.shape[0]))
    slots = lax.broadcasted_iota(jnp.int32, (n, small_width), 0)
    small = net.sum_all(jnp.where(slots == d, small[None], 0.0))
    full_up_bias = small[:, :urow].reshape(1, ff)
    full_down_bias = small[:, urow : urow + drow].reshape(1, width)
    all_times = small.reshape(batch, seq, small_width)[:, 0, urow + drow]

    feat = jax.nn.silu(time_embed(all_times, width)).astype(bf16)
    feat_own = lax.dynamic_slice_in_dim(feat, d * wrow, wrow, 1)
    modulation = jnp.dot(feat_own, modulate_weight, preferred_element_type=f32)
    mod_bias = lax.dynamic_update_slice_in_dim(
        jnp.zeros((6 * width,), f32), modulate_bias.astype(f32), d * modulate_bias.shape[0], 0
    )
    modulation = modulation + mod_bias[None]
    bit = batch // 2
    while bit:
        high = (net.b & bit) // bit
        sent = lax.dynamic_slice_in_dim(modulation, (1 - high) * bit, bit, 0)
        kept = lax.dynamic_slice_in_dim(modulation, high * bit, bit, 0)
        modulation = kept + net.swap(sent, bit * seq)
        bit //= 2
    bit = 1
    while bit < seq:
        modulation = modulation + net.swap(modulation, bit)
        bit *= 2
    shift_one, scale_one, gate_one, shift_two, scale_two, gate_two = jnp.split(modulation, 6, -1)

    half_dim = HEAD_DIM // 2
    inverse = jnp.exp(-math.log(10000.0) * 2.0 * jnp.arange(half_dim, dtype=f32) / HEAD_DIM)
    positions = (
        seq_order[:, None] * local + jnp.arange(local, dtype=jnp.int32)[None]
    ).reshape(rows)
    angles = positions.astype(f32)[:, None] * jnp.tile(inverse, 128 // half_dim)[None]
    cosine, sine = jnp.cos(angles), jnp.sin(angles)
    key_bias = jnp.where(positions < lengths[0], 0.0, masked_score).astype(f32)[None]

    joined = jnp.concatenate([frames, skips], axis=-1)
    hidden_zero = jnp.dot(joined, full_skip, preferred_element_type=f32)
    normed_one = modulated(hidden_zero, scale_one, shift_one).astype(bf16)
    across = {0: normed_one}
    bit = seq // 2
    while bit:
        across.update({i | bit: net.swap(a, bit) for i, a in list(across.items())})
        bit //= 2
    normed_all = jnp.concatenate([across[i] for i in range(seq)])
    q, k, v = qkv_project(normed_all, full_qkv, cosine, sine)
    att, lse = attend(q, k, v, key_bias, heads)
    blocks = [att[i * local : (i + 1) * local] for i in range(seq)]
    attended = jnp.concatenate(
        [b if i == 0 else net.swap(b, i) for i, b in enumerate(blocks)], axis=-1
    )
    attn_proj = jnp.dot(attended, full_output, preferred_element_type=f32)
    hidden_one = hidden_zero + gate_one * attn_proj
    normed_two = modulated(hidden_one, scale_two, shift_two).astype(bf16)
    pre_act = jnp.dot(normed_two, full_up, preferred_element_type=f32) + full_up_bias
    activated = gelu_tanh(pre_act).astype(bf16)
    ffn_out = jnp.dot(activated, full_down, preferred_element_type=f32) + full_down_bias
    layer_out = (hidden_one + gate_two * ffn_out).astype(bf16)

    rows_dot = lambda a, b: lax.dot_general(
        a, b, (((0,), (0,)), ((), ())), preferred_element_type=f32
    )
    back_dot = lambda a, b: lax.dot_general(
        a, b, (((1,), (1,)), ((), ())), preferred_element_type=f32
    )

    def scattered(grads, block_rows, turn=False):
        if built:
            blocks = grads.reshape(n, block_rows, grads.shape[-1])
            spot = (lambda i: i ^ (s * (n // seq))) if turn else (lambda i: i)
            return scatter_sum(net, blocks, spot)
        if turn:
            grads = grads.reshape(seq, width // seq, -1)[seq_order].reshape(grads.shape)
        return lax.psum_scatter(grads, ALL, scatter_dimension=0, tiled=True).astype(f32)

    ffn_grad = out_grad * gate_two
    down_bias_term = jnp.sum(ffn_grad, axis=0)
    ffn_grad_low = ffn_grad.astype(bf16)
    grad_down_weight = scattered(rows_dot(activated, ffn_grad_low).astype(bf16), ff // n)
    act_grad = back_dot(ffn_grad_low, full_down)
    pre_grad = jax.vjp(gelu_tanh, pre_act)[1](act_grad)[0]
    up_bias_term = jnp.sum(pre_grad, axis=0)
    pre_grad_low = pre_grad.astype(bf16)
    normed_two_grad = back_dot(pre_grad_low, full_up)
    pull_two = jax.vjp(modulated, hidden_one, scale_two, shift_two)[1]
    hidden_grad_two, scale_two_grad, shift_two_grad = pull_two(normed_two_grad)
    gate_two_grad = jnp.sum(out_grad * ffn_out, axis=0)
    hidden_one_grad = out_grad + hidden_grad_two
    gate_one_grad = jnp.sum(hidden_one_grad * attn_proj, axis=0)
    proj_grad_low = (hidden_one_grad * gate_one).astype(bf16)
    attended_grad = back_dot(proj_grad_low, full_output).astype(bf16)
    pieces = [attended_grad[:, i * part : (i + 1) * part] for i in range(seq)]
    grad_all = jnp.concatenate([p if i == 0 else net.swap(p, i) for i, p in enumerate(pieces)])
    up_out = jnp.concatenate(
        [rows_dot(normed_two, pre_grad_low).astype(bf16)], axis=1
    )
    grad_up_weight = scattered(up_out, wrow)
    grad_output_weight = scattered(rows_dot(attended, proj_grad_low).astype(bf16), wrow, True)
    dq, dk, dv = attend_back(q, k, v, att, grad_all, lse, key_bias, cosine, sine, heads)
    qkv_grad = jnp.concatenate([dq, dk, dv], axis=-1)

    odd = jnp.concatenate([qkv_grad[i * local : (i + 1) * local] for i in range(1, seq, 2)])
    even = [qkv_grad[i * local : (i + 1) * local] for i in range(0, seq, 2)]
    sent = net.swap(back_dot(odd, full_qkv).astype(bf16), 1).astype(f32)
    halves = [
        back_dot(e, full_qkv) + sent[i * local : (i + 1) * local] for i, e in enumerate(even)
    ]
    step = 2
    while len(halves) > 1:
        keep = halves[0::2]
        give = halves[1::2]
        halves = [
            a + net.swap(g.astype(bf16), step).astype(f32) for a, g in zip(keep, give)
        ]
        step *= 2
    normed_one_grad = halves[0]
    qkv_part = rows_dot(normed_all, qkv_grad).astype(bf16)
    if built:
        units = qkv_part.reshape(batch, seq * wrow, 3 * part)
        z = jnp.arange(4, dtype=jnp.int32)
        r1 = net.swap(combine([units], [net.b ^ 1 ^ (z << 1)], bf16), 4)
        parts = combine([units, r1], [net.b ^ (z[1:] << 1), z[1:]], bf16)
        zs = [net.swap(parts[i - 1 : i], i << 3) for i in (1, 2, 3)]
        zero = jnp.zeros((1,), jnp.int32)
        own = combine([units, r1] + zs, [net.b + zero] + [zero] * 4, f32)[0]
    else:
        own = lax.psum_scatter(qkv_part, "batch", scatter_dimension=0, tiled=True).astype(f32)
    own = own.reshape(seq, wrow, 3, part)
    cols = [
        lax.dynamic_index_in_dim(own, s ^ i, 0, keepdims=False) for i in range(seq)
    ]
    cols = jnp.stack([c if i == 0 else net.swap(c, i) for i, c in enumerate(cols)], axis=2)
    bit = 1
    while bit < seq:
        swapped = cols.reshape(wrow, 3, seq // (2 * bit), 2, bit, part)[:, :, :, ::-1]
        cols = jnp.where((s & bit) > 0, swapped.reshape(cols.shape), cols)
        bit *= 2
    grad_qkv_weight = cols.reshape(wrow, 3 * width)

    pull_one = jax.vjp(modulated, hidden_zero, scale_one, shift_one)[1]
    hidden_grad_one, scale_one_grad, shift_one_grad = pull_one(normed_one_grad)
    hidden_zero_grad = (hidden_one_grad + hidden_grad_one).astype(bf16)
    grad_skip_weight = scattered(
        rows_dot(joined, hidden_zero_grad).astype(bf16), 2 * width // n
    )
    grad_frames = back_dot(hidden_zero_grad, full_skip[:width])
    grad_skip = back_dot(hidden_zero_grad, full_skip[width:])

    def by_utterance(*vectors):
        row = jnp.concatenate([vec.reshape(1, -1) for vec in vectors], axis=1)
        place_row = lax.broadcasted_iota(jnp.int32, (batch, row.shape[1]), 0)
        return jnp.where(place_row == net.b, row, 0.0)

    early = by_utterance(gate_one_grad, shift_two_grad, scale_two_grad, gate_two_grad)
    flat = jnp.concatenate([early.reshape(-1), up_bias_term, down_bias_term])
    flat = net.sum_all(flat.reshape(-1, 128)).reshape(-1)
    early = flat[: batch * 4 * width].reshape(batch, 4 * width)
    up_sum = flat[batch * 4 * width : batch * 4 * width + ff]
    down_sum = flat[batch * 4 * width + ff :]
    grad_up_bias = lax.dynamic_slice_in_dim(up_sum, d * urow, urow, 0)
    grad_down_bias = lax.dynamic_slice_in_dim(down_sum, d * drow, drow, 0)
    late = net.sum_all(by_utterance(shift_one_grad, scale_one_grad))
    mod_grad = jnp.concatenate([late, early], axis=1)
    grad_modulate_weight = lax.dot_general(
        feat_own.astype(f32),
        mod_grad,
        (((0,), (0,)), ((), ())),
        precision=lax.Precision.HIGHEST,
        preferred_element_type=f32,
    )
    mod_width = modulate_bias.shape[0]
    grad_modulate_bias = jnp.sum(
        lax.dynamic_slice_in_dim(mod_grad, d * mod_width, mod_width, 1), axis=0
    )
    shape = (local, utts, width)
    return (
        layer_out.reshape(shape),
        grad_frames.reshape(shape),
        grad_skip.reshape(shape),
        grad_skip_weight,
        grad_qkv_weight,
        grad_output_weight,
        grad_up_weight,
        grad_up_bias,
        grad_down_weight,
        grad_down_bias,
        grad_modulate_weight,
        grad_modulate_bias,
    )


def solution(mesh):
    rows_two = P("seq", "batch", None)
    owned = P(ALL, None)
    vector = P(ALL)
    in_specs = (
        rows_two,
        rows_two,
        P("batch"),
        P("batch"),
        owned,
        owned,
        owned,
        owned,
        vector,
        owned,
        vector,
        owned,
        vector,
        rows_two,
    )
    out_specs = (
        rows_two,
        rows_two,
        rows_two,
        owned,
        owned,
        owned,
        owned,
        vector,
        owned,
        vector,
        owned,
        vector,
    )
    sizes = (mesh.shape["batch"], mesh.shape["seq"])
    return jax.shard_map(
        functools.partial(body, sizes),
        mesh=mesh,
        in_specs=in_specs,
        out_specs=out_specs,
        check_vma=False,
    )
```

```python
import functools
import math

import jax
import jax.numpy as jnp
from jax import lax
from jax.experimental import pallas as pl
from jax.experimental.pallas import tpu as pltpu
from jax.sharding import PartitionSpec as P

HEADS = 16
HEAD_DIM = 64
epsilon = 1e-06
masked_score = -1e30
f32 = jnp.float32
bf16 = jnp.bfloat16
ALL = ("batch", "seq")


def rms_norm(values):
    return values * lax.rsqrt(jnp.mean(values * values, axis=-1, keepdims=True) + epsilon)


def modulated(hidden, scale_rows, shift_rows):
    return rms_norm(hidden) * (1.0 + scale_rows) + shift_rows


def gelu_tanh(pre_values):
    return jax.nn.gelu(pre_values, approximate=True)


def time_embed(flow_times, embed_width):
    half_width = embed_width // 2
    frequency = jnp.exp(-math.log(10000.0) * jnp.arange(half_width, dtype=f32) / half_width)
    angles = 1000.0 * flow_times[:, None] * frequency[None, :]
    return jnp.concatenate([jnp.sin(angles), jnp.cos(angles)], axis=-1)


def params(semantics=None):
    return pltpu.CompilerParams(dimension_semantics=semantics, vmem_limit_bytes=60 * 1024 * 1024)


class Net:
    def __init__(self, batch, seq):
        self.batch, self.seq, self.n = batch, seq, batch * seq
        self.d = lax.axis_index("batch") * seq + lax.axis_index("seq")
        self.b = lax.axis_index("batch")
        self.s = lax.axis_index("seq")
        self.core = self.d & 1

    def swap(self, value, offset):
        return lax.ppermute(value, ALL, [(i, i ^ offset) for i in range(self.n)])

    def swap_by_core(self, value, even, odd):
        pairs = [(i, i ^ (odd if i & 1 else even)) for i in range(self.n)]
        return lax.ppermute(value, ALL, pairs)

    def sum_all(self, value):
        bit = 1
        while bit < self.n:
            value = value + self.swap(value, bit)
            bit *= 2
        return value


def after(value, *others):
    return lax.optimization_barrier((value,) + tuple(others))[0]


def place(pieces, tables, count, columns=None):
    rows, width = pieces[0].shape[1:]
    columns = columns or (width,)
    counts = [p.shape[0] for p in pieces]
    total = sum(counts)
    table = jnp.concatenate(tables, axis=-1).astype(jnp.int32)
    if table.ndim == 1:
        table = jnp.broadcast_to(table[None], (len(columns), total))

    def kernel(table_ref, *refs):
        sources = refs[: len(pieces)]
        outs = refs[len(pieces) : len(pieces) + len(columns)]
        sems = refs[-1]
        copies = []
        at = 0
        for source, number in zip(sources, counts):
            for j in range(number):
                left = 0
                for o, wide in enumerate(columns):
                    copies.append(
                        pltpu.make_async_copy(
                            source.at[j, :, pl.ds(left, wide)],
                            outs[o].at[table_ref[o, at]],
                            sems.at[o, at],
                        )
                    )
                    left += wide
                at += 1
        for copy in copies:
            copy.start()
        for copy in copies:
            copy.wait()

    any_spec = pl.BlockSpec(memory_space=pl.ANY)
    outs = pl.pallas_call(
        kernel,
        out_shape=[jax.ShapeDtypeStruct((count, rows, wide), pieces[0].dtype) for wide in columns],
        in_specs=[pl.BlockSpec(memory_space=pltpu.SMEM)] + [any_spec] * len(pieces),
        out_specs=[pl.BlockSpec(memory_space=pltpu.VMEM)] * len(columns),
        scratch_shapes=[pltpu.SemaphoreType.DMA((len(columns), total))],
        compiler_params=params(),
    )(table, *pieces)
    return [out.reshape(count * rows, wide) for out, wide in zip(outs, columns)]


def combine(inputs, tables, dtype):
    rows, width = inputs[0].shape[1:]
    count = tables[0].shape[0]
    table = jnp.stack([jnp.asarray(t, jnp.int32) for t in tables])

    def kernel(table_ref, *refs):
        total = refs[0][...].astype(f32)
        for ref in refs[1:-1]:
            total = total + ref[...].astype(f32)
        refs[-1][...] = total.astype(dtype)

    def spec(j):
        return pl.BlockSpec((1, rows, width), lambda i, t: (t[j, i], 0, 0))

    return pl.pallas_call(
        kernel,
        out_shape=jax.ShapeDtypeStruct((count, rows, width), dtype),
        grid_spec=pltpu.PrefetchScalarGridSpec(
            num_scalar_prefetch=1,
            grid=(count,),
            in_specs=[spec(j) for j in range(len(inputs))],
            out_specs=pl.BlockSpec((1, rows, width), lambda i, t: (i, 0, 0)),
        ),
        compiler_params=params(("arbitrary",)),
    )(table, *inputs)


def gather_start(net, shard):
    return jnp.stack([shard] + [net.swap(shard, k << 3) for k in (1, 2, 3)])


def gather_finish(net, near):
    d, c = net.d, net.core
    z = jnp.arange(4, dtype=jnp.int32) << 3
    second = jnp.where(c == 0, 2, 4)
    third = 6 - second
    far = net.swap_by_core(near, 2, 4)
    half = jnp.concatenate([near, far], axis=0)
    other = net.swap_by_core(half, 4, 2)
    own = jnp.concatenate([d ^ z, d ^ z ^ second])
    last = own ^ third
    mate = d ^ 1
    mate_own = jnp.concatenate([mate ^ z, mate ^ z ^ third])
    mate_last = mate_own ^ second
    return (
        [half, other, net.swap(half, 1), net.swap(other, 1)],
        [own, last, mate_own, mate_last],
    )


def scatter_sum(net, grads, spot):
    d, c = net.d, net.core
    first = jnp.where(c == 0, 4, 2)
    second = 6 - first
    j = jnp.arange(16, dtype=jnp.int32)
    r1 = net.swap(combine([grads], [spot(d ^ 1 ^ (j << 1))], bf16), 1)
    t = jnp.arange(8, dtype=jnp.int32)
    off = first ^ ((t >> 1) << 3) ^ ((t & 1) * second)
    r2 = net.swap_by_core(combine([grads, r1], [spot(d ^ off), off >> 1], bf16), 4, 2)
    z = jnp.arange(4, dtype=jnp.int32)
    off = second ^ (z << 3)
    r3 = net.swap_by_core(
        combine([grads, r1, r2], [spot(d ^ off), off >> 1, z * 2 + 1], bf16), 2, 4
    )
    z = z[1:]
    parts = combine([grads, r1, r2, r3], [spot(d ^ (z << 3)), z << 2, z * 2, z], bf16)
    zs = [net.swap(parts[k - 1 : k], k << 3) for k in (1, 2, 3)]
    zero = jnp.zeros((1,), jnp.int32)
    own = combine(
        [grads, r1, r2, r3] + zs, [spot(d + zero), zero, zero, zero, zero, zero, zero], f32
    )
    return own[0]


def rope(values, cosine, sine, back):
    width = values.shape[-1]
    lane = lax.broadcasted_iota(jnp.int32, values.shape, 1)
    early = (lane & (HEAD_DIM - 1)) < HEAD_DIM // 2
    source = values * sine if back else values
    ahead = pltpu.roll(source, width - HEAD_DIM // 2, 1)
    behind = pltpu.roll(source, HEAD_DIM // 2, 1)
    if back:
        turned = jnp.where(early, ahead, -behind)
        return values * cosine + turned
    turned = jnp.where(early, -ahead, behind)
    return values * cosine + turned * sine


def wide_tables(cos_ref, sin_ref, width):
    reps = width // cos_ref.shape[-1]
    cosine = jnp.concatenate([cos_ref[...]] * reps, axis=-1)
    sine = jnp.concatenate([sin_ref[...]] * reps, axis=-1)
    return cosine, sine


def qkv_kernel(x_ref, w_ref, cos_ref, sin_ref, q_ref, k_ref, v_ref):
    width = q_ref.shape[-1]
    result = jnp.dot(x_ref[...], w_ref[...], preferred_element_type=f32)
    cosine, sine = wide_tables(cos_ref, sin_ref, width)
    scale = HEAD_DIM ** (-0.5)
    q_ref[...] = (rope(result[:, :width], cosine, sine, False) * scale).astype(bf16)
    k_ref[...] = rope(result[:, width : 2 * width], cosine, sine, False).astype(bf16)
    v_ref[...] = result[:, 2 * width :].astype(bf16)


def qkv_project(x, w, cosine, sine):
    rows, depth = x.shape
    width = w.shape[1] // 3
    block = min(512, rows)
    row = lambda wide: pl.BlockSpec((block, wide), lambda i: (i, 0))
    return pl.pallas_call(
        qkv_kernel,
        grid=(rows // block,),
        out_shape=[jax.ShapeDtypeStruct((rows, width), bf16)] * 3,
        in_specs=[row(depth), pl.BlockSpec(w.shape, lambda i: (0, 0)), row(128), row(128)],
        out_specs=[row(width)] * 3,
        compiler_params=params(("arbitrary",)),
    )(x, w, cosine, sine)


def attend_kernel(heads, q_ref, k_ref, v_ref, bias_ref, o_ref, lse_ref):
    q = q_ref[...]
    k = k_ref[...]
    v = v_ref[...]
    bias = bias_ref[...]
    lane = lax.broadcasted_iota(jnp.int32, q.shape, 1) // HEAD_DIM
    spot = lax.broadcasted_iota(jnp.int32, lse_ref.shape, 1)
    out = jnp.zeros(q.shape, f32)
    lse = jnp.zeros(lse_ref.shape, f32)
    for h in range(heads):
        mine = lane == h
        qh = jnp.where(mine, q, jnp.zeros_like(q))
        s = lax.dot_general(qh, k, (((1,), (1,)), ((), ())), preferred_element_type=f32) + bias
        top = jnp.max(s, axis=-1, keepdims=True)
        p = jnp.exp(s - top)
        total = jnp.sum(p, axis=-1, keepdims=True)
        o = jnp.dot(p.astype(bf16), v, preferred_element_type=f32) / total
        out = jnp.where(mine, o, out)
        lse = jnp.where(spot == h, top + jnp.log(total), lse)
    o_ref[...] = out.astype(bf16)
    lse_ref[...] = lse


def attend(q, k, v, bias, heads):
    rows, width = q.shape
    block = 256
    row = lambda wide: pl.BlockSpec((block, wide), lambda i: (i, 0))
    whole = pl.BlockSpec((rows, width), lambda i: (0, 0))
    return pl.pallas_call(
        functools.partial(attend_kernel, heads),
        grid=(rows // block,),
        out_shape=[jax.ShapeDtypeStruct((rows, width), bf16), jax.ShapeDtypeStruct((rows, 128), f32)],
        in_specs=[row(width), whole, whole, pl.BlockSpec((1, rows), lambda i: (0, 0))],
        out_specs=[row(width), row(128)],
        compiler_params=params(("arbitrary",)),
    )(q, k, v, bias)


def attend_back_kernel(
    heads,
    q_ref,
    do_ref,
    o_ref,
    lse_ref,
    k_ref,
    v_ref,
    kt_ref,
    bias_ref,
    cosq_ref,
    sinq_ref,
    cosk_ref,
    sink_ref,
    dq_ref,
    dk_ref,
    dv_ref,
    p_all,
    ds_all,
    dk_acc,
    dv_acc,
):
    step = pl.program_id(0)
    q = q_ref[...]
    do = do_ref[...]
    k = k_ref[...]
    v = v_ref[...]
    block, width = q.shape
    lane = lax.broadcasted_iota(jnp.int32, q.shape, 1) // HEAD_DIM
    product = (do.astype(f32) * o_ref[...].astype(f32)).T
    lse_t = lse_ref[...].T
    bias = bias_ref[...]
    contract = (((1,), (1,)), ((), ()))
    q_parts, do_parts, dq_parts = [], [], []
    for h in range(heads):
        mine = lane == h
        qh = jnp.where(mine, q, jnp.zeros_like(q))
        doh = jnp.where(mine, do, jnp.zeros_like(do))
        q_parts.append(qh)
        do_parts.append(doh)
        row_dot = jnp.sum(product[h * HEAD_DIM : (h + 1) * HEAD_DIM], axis=0, keepdims=True)
        s = lax.dot_general(k, qh, contract, preferred_element_type=f32)
        p = jnp.exp(s + bias - lse_t[h : h + 1])
        dp = lax.dot_general(v, doh, contract, preferred_element_type=f32)
        ds = (p * (dp - row_dot)).astype(bf16)
        p_all[:, h * block : (h + 1) * block] = p.astype(bf16)
        ds_all[:, h * block : (h + 1) * block] = ds
        dq_parts.append(
            jnp.dot(kt_ref[h * HEAD_DIM : (h + 1) * HEAD_DIM, :], ds, preferred_element_type=f32)
        )
    dv = jnp.dot(p_all[...], jnp.concatenate(do_parts, axis=0), preferred_element_type=f32)
    dk = jnp.dot(ds_all[...], jnp.concatenate(q_parts, axis=0), preferred_element_type=f32)

    @pl.when(step == 0)
    def _():
        dv_acc[...] = dv
        dk_acc[...] = dk

    @pl.when(step > 0)
    def _():
        dv_acc[...] += dv
        dk_acc[...] += dk

    dq = jnp.concatenate(dq_parts, axis=0).T
    cosine, sine = wide_tables(cosq_ref, sinq_ref, width)
    dq_ref[...] = (rope(dq, cosine, sine, True) * (HEAD_DIM ** (-0.5))).astype(bf16)

    @pl.when(step == pl.num_programs(0) - 1)
    def _():
        cosine, sine = wide_tables(cosk_ref, sink_ref, width)
        dk_ref[...] = rope(dk_acc[...], cosine, sine, True).astype(bf16)
        dv_ref[...] = dv_acc[...].astype(bf16)


def attend_back(q, k, v, o, do, lse, bias, cosine, sine, heads):
    rows, width = q.shape
    block = 256
    row = lambda wide: pl.BlockSpec((block, wide), lambda i: (i, 0))
    whole = lambda wide: pl.BlockSpec((rows, wide), lambda i: (0, 0))
    return pl.pallas_call(
        functools.partial(attend_back_kernel, heads),
        grid=(rows // block,),
        out_shape=[jax.ShapeDtypeStruct((rows, width), bf16)] * 3,
        in_specs=[
            row(width),
            row(width),
            row(width),
            row(128),
            whole(width),
            whole(width),
            pl.BlockSpec((width, rows), lambda i: (0, 0)),
            whole(block),
            row(128),
            row(128),
            whole(128),
            whole(128),
        ],
        out_specs=[row(width), whole(width), whole(width)],
        scratch_shapes=[
            pltpu.VMEM((rows, heads * block), bf16),
            pltpu.VMEM((rows, heads * block), bf16),
            pltpu.VMEM((rows, width), f32),
            pltpu.VMEM((rows, width), f32),
        ],
        compiler_params=params(("arbitrary",)),
    )(
        q,
        do,
        o,
        lse,
        k,
        v,
        k.T,
        jnp.broadcast_to(bias.reshape(rows, 1), (rows, block)),
        cosine,
        sine,
        cosine,
        sine,
    )


def body(
    mesh_sizes,
    frames_in,
    skip_in,
    flow_times,
    lengths,
    skip_weight,
    qkv_weight,
    output_weight,
    up_weight,
    up_bias,
    down_weight,
    down_bias,
    modulate_weight,
    modulate_bias,
    output_grad,
):
    batch, seq = mesh_sizes
    net = Net(batch, seq)
    n, d, s = net.n, net.d, net.s
    local, utts, width = frames_in.shape
    frames = frames_in.reshape(local, width)
    skips = skip_in.reshape(local, width)
    out_grad = output_grad.reshape(local, width).astype(f32)
    heads = HEADS // seq
    part = heads * HEAD_DIM
    rows = local * seq
    built = n == 32 and seq == 4
    wrow = width // n
    ff = up_weight.shape[1]

    seq_order = s ^ jnp.arange(seq, dtype=jnp.int32)
    by_part = qkv_weight.reshape(wrow, 3, seq, part)
    pieces = [
        lax.dynamic_index_in_dim(by_part, s ^ k, 2, keepdims=False).reshape(wrow, 3 * part)
        for k in range(seq)
    ]
    pieces = [p if k == 0 else net.swap(p, k) for k, p in enumerate(pieces)]
    if built:
        near = gather_start(net, skip_weight)
        got, spots = gather_finish(net, near)
        (full_skip,) = place(got, spots, n)
        qkv_four = jnp.stack(pieces)
        qkv_four = after(qkv_four, near)
        qkv_z = jnp.concatenate([qkv_four] + [net.swap(qkv_four, k << 3) for k in (1, 2, 3)])
        qkv_y = net.swap(qkv_z, 4)
        k16 = jnp.arange(16, dtype=jnp.int32)
        z_spots = d ^ (((k16 >> 2) << 3) | (k16 & 3))
        (full_qkv,) = place([qkv_z, qkv_y], [z_spots, z_spots ^ 4], n)
        ou = after(jnp.concatenate([output_weight, up_weight], axis=1), qkv_z)
        near_ou = gather_start(net, ou)
        got, spots = gather_finish(net, near_ou)
        spots = jnp.concatenate(spots)
        turned = spots ^ (s * (n // seq))
        full_output, full_up = place(
            got, [jnp.stack([turned, spots])], n, (width, ff)
        )
        near_down = gather_start(net, after(down_weight, near_ou))
        got, spots = gather_finish(net, near_down)
        (full_down,) = place(got, spots, n)
    else:
        gather = lambda w, ax: lax.all_gather(w, ax, axis=0, tiled=True)
        full_skip = gather(skip_weight, ALL)
        full_qkv = gather(jnp.stack(pieces)[seq_order], "batch")
        full_qkv = full_qkv.reshape(batch, seq, wrow, 3 * part)
        full_qkv = full_qkv.reshape(width, 3 * part)
        full_output = gather(output_weight, ALL).reshape(seq, width // seq, width)[seq_order]
        full_output = full_output.reshape(width, width)
        full_up = gather(up_weight, ALL)
        full_down = gather(down_weight, ALL)

    urow, drow = up_bias.shape[0], down_bias.shape[0]
    small = jnp.concatenate([up_bias.astype(f32), down_bias.astype(f32), flow_times])
    small_width = -(-small.shape[0] // 128) * 128
    small = jnp.pad(small, (0, small_width - small.shape[0]))
    slots = lax.broadcasted_iota(jnp.int32, (n, small_width), 0)
    small = net.sum_all(jnp.where(slots == d, small[None], 0.0))
    full_up_bias = small[:, :urow].reshape(1, ff)
    full_down_bias = small[:, urow : urow + drow].reshape(1, width)
    all_times = small.reshape(batch, seq, small_width)[:, 0, urow + drow]

    feat = jax.nn.silu(time_embed(all_times, width)).astype(bf16)
    feat_own = lax.dynamic_slice_in_dim(feat, d * wrow, wrow, 1)
    modulation = jnp.dot(feat_own, modulate_weight, preferred_element_type=f32)
    mod_bias = lax.dynamic_update_slice_in_dim(
        jnp.zeros((6 * width,), f32), modulate_bias.astype(f32), d * modulate_bias.shape[0], 0
    )
    modulation = modulation + mod_bias[None]
    bit = batch // 2
    while bit:
        high = (net.b & bit) // bit
        sent = lax.dynamic_slice_in_dim(modulation, (1 - high) * bit, bit, 0)
        kept = lax.dynamic_slice_in_dim(modulation, high * bit, bit, 0)
        modulation = kept + net.swap(sent, bit * seq)
        bit //= 2
    bit = 1
    while bit < seq:
        modulation = modulation + net.swap(modulation, bit)
        bit *= 2
    shift_one, scale_one, gate_one, shift_two, scale_two, gate_two = jnp.split(modulation, 6, -1)

    half_dim = HEAD_DIM // 2
    inverse = jnp.exp(-math.log(10000.0) * 2.0 * jnp.arange(half_dim, dtype=f32) / HEAD_DIM)
    positions = (
        seq_order[:, None] * local + jnp.arange(local, dtype=jnp.int32)[None]
    ).reshape(rows)
    angles = positions.astype(f32)[:, None] * jnp.tile(inverse, 128 // half_dim)[None]
    cosine, sine = jnp.cos(angles), jnp.sin(angles)
    key_bias = jnp.where(positions < lengths[0], 0.0, masked_score).astype(f32)[None]

    joined = jnp.concatenate([frames, skips], axis=-1)
    hidden_zero = jnp.dot(joined, full_skip, preferred_element_type=f32)
    normed_one = modulated(hidden_zero, scale_one, shift_one).astype(bf16)
    across = {0: normed_one}
    bit = seq // 2
    while bit:
        across.update({i | bit: net.swap(a, bit) for i, a in list(across.items())})
        bit //= 2
    normed_all = jnp.concatenate([across[i] for i in range(seq)])
    q, k, v = qkv_project(normed_all, full_qkv, cosine, sine)
    att, lse = attend(q, k, v, key_bias, heads)
    blocks = [att[i * local : (i + 1) * local] for i in range(seq)]
    attended = jnp.concatenate(
        [b if i == 0 else net.swap(b, i) for i, b in enumerate(blocks)], axis=-1
    )
    attn_proj = jnp.dot(attended, full_output, preferred_element_type=f32)
    hidden_one = hidden_zero + gate_one * attn_proj
    normed_two = modulated(hidden_one, scale_two, shift_two).astype(bf16)
    pre_act = jnp.dot(normed_two, full_up, preferred_element_type=f32) + full_up_bias
    activated = gelu_tanh(pre_act).astype(bf16)
    ffn_out = jnp.dot(activated, full_down, preferred_element_type=f32) + full_down_bias
    layer_out = (hidden_one + gate_two * ffn_out).astype(bf16)

    rows_dot = lambda a, b: lax.dot_general(
        a, b, (((0,), (0,)), ((), ())), preferred_element_type=f32
    )
    back_dot = lambda a, b: lax.dot_general(
        a, b, (((1,), (1,)), ((), ())), preferred_element_type=f32
    )

    def scattered(grads, block_rows, turn=False):
        if built:
            blocks = grads.reshape(n, block_rows, grads.shape[-1])
            spot = (lambda i: i ^ (s * (n // seq))) if turn else (lambda i: i)
            return scatter_sum(net, blocks, spot)
        if turn:
            grads = grads.reshape(seq, width // seq, -1)[seq_order].reshape(grads.shape)
        return lax.psum_scatter(grads, ALL, scatter_dimension=0, tiled=True).astype(f32)

    ffn_grad = out_grad * gate_two
    down_bias_term = jnp.sum(ffn_grad, axis=0)
    ffn_grad_low = ffn_grad.astype(bf16)
    grad_down_weight = scattered(rows_dot(activated, ffn_grad_low).astype(bf16), ff // n)
    act_grad = back_dot(ffn_grad_low, full_down)
    pre_grad = jax.vjp(gelu_tanh, pre_act)[1](act_grad)[0]
    up_bias_term = jnp.sum(pre_grad, axis=0)
    pre_grad_low = pre_grad.astype(bf16)
    normed_two_grad = back_dot(pre_grad_low, full_up)
    pull_two = jax.vjp(modulated, hidden_one, scale_two, shift_two)[1]
    hidden_grad_two, scale_two_grad, shift_two_grad = pull_two(normed_two_grad)
    gate_two_grad = jnp.sum(out_grad * ffn_out, axis=0)
    hidden_one_grad = out_grad + hidden_grad_two
    gate_one_grad = jnp.sum(hidden_one_grad * attn_proj, axis=0)
    proj_grad_low = (hidden_one_grad * gate_one).astype(bf16)
    attended_grad = back_dot(proj_grad_low, full_output).astype(bf16)
    pieces = [attended_grad[:, i * part : (i + 1) * part] for i in range(seq)]
    grad_all = jnp.concatenate([p if i == 0 else net.swap(p, i) for i, p in enumerate(pieces)])
    up_out = jnp.concatenate(
        [rows_dot(normed_two, pre_grad_low).astype(bf16)], axis=1
    )
    grad_up_weight = scattered(up_out, wrow)
    grad_output_weight = scattered(rows_dot(attended, proj_grad_low).astype(bf16), wrow, True)
    dq, dk, dv = attend_back(q, k, v, att, grad_all, lse, key_bias, cosine, sine, heads)
    qkv_grad = jnp.concatenate([dq, dk, dv], axis=-1)

    odd = jnp.concatenate([qkv_grad[i * local : (i + 1) * local] for i in range(1, seq, 2)])
    even = [qkv_grad[i * local : (i + 1) * local] for i in range(0, seq, 2)]
    sent = net.swap(back_dot(odd, full_qkv).astype(bf16), 1).astype(f32)
    halves = [
        back_dot(e, full_qkv) + sent[i * local : (i + 1) * local] for i, e in enumerate(even)
    ]
    step = 2
    while len(halves) > 1:
        keep = halves[0::2]
        give = halves[1::2]
        halves = [
            a + net.swap(g.astype(bf16), step).astype(f32) for a, g in zip(keep, give)
        ]
        step *= 2
    normed_one_grad = halves[0]
    qkv_part = rows_dot(normed_all, qkv_grad).astype(bf16)
    if built:
        units = qkv_part.reshape(batch, seq * wrow, 3 * part)
        z = jnp.arange(4, dtype=jnp.int32)
        r1 = net.swap(combine([units], [net.b ^ 1 ^ (z << 1)], bf16), 4)
        parts = combine([units, r1], [net.b ^ (z[1:] << 1), z[1:]], bf16)
        zs = [net.swap(parts[i - 1 : i], i << 3) for i in (1, 2, 3)]
        zero = jnp.zeros((1,), jnp.int32)
        own = combine([units, r1] + zs, [net.b + zero] + [zero] * 4, f32)[0]
    else:
        own = lax.psum_scatter(qkv_part, "batch", scatter_dimension=0, tiled=True).astype(f32)
    own = own.reshape(seq, wrow, 3, part)
    cols = [
        lax.dynamic_index_in_dim(own, s ^ i, 0, keepdims=False) for i in range(seq)
    ]
    cols = jnp.stack([c if i == 0 else net.swap(c, i) for i, c in enumerate(cols)], axis=2)
    bit = 1
    while bit < seq:
        swapped = cols.reshape(wrow, 3, seq // (2 * bit), 2, bit, part)[:, :, :, ::-1]
        cols = jnp.where((s & bit) > 0, swapped.reshape(cols.shape), cols)
        bit *= 2
    grad_qkv_weight = cols.reshape(wrow, 3 * width)

    pull_one = jax.vjp(modulated, hidden_zero, scale_one, shift_one)[1]
    hidden_grad_one, scale_one_grad, shift_one_grad = pull_one(normed_one_grad)
    hidden_zero_grad = (hidden_one_grad + hidden_grad_one).astype(bf16)
    grad_skip_weight = scattered(
        rows_dot(joined, hidden_zero_grad).astype(bf16), 2 * width // n
    )
    grad_frames = back_dot(hidden_zero_grad, full_skip[:width])
    grad_skip = back_dot(hidden_zero_grad, full_skip[width:])

    def by_utterance(*vectors):
        row = jnp.concatenate([vec.reshape(1, -1) for vec in vectors], axis=1)
        place_row = lax.broadcasted_iota(jnp.int32, (batch, row.shape[1]), 0)
        return jnp.where(place_row == net.b, row, 0.0)

    early = by_utterance(gate_one_grad, shift_two_grad, scale_two_grad, gate_two_grad)
    flat = jnp.concatenate([early.reshape(-1), up_bias_term, down_bias_term])
    flat = net.sum_all(flat.reshape(-1, 128)).reshape(-1)
    early = flat[: batch * 4 * width].reshape(batch, 4 * width)
    up_sum = flat[batch * 4 * width : batch * 4 * width + ff]
    down_sum = flat[batch * 4 * width + ff :]
    grad_up_bias = lax.dynamic_slice_in_dim(up_sum, d * urow, urow, 0)
    grad_down_bias = lax.dynamic_slice_in_dim(down_sum, d * drow, drow, 0)
    late = net.sum_all(by_utterance(shift_one_grad, scale_one_grad))
    mod_grad = jnp.concatenate([late, early], axis=1)
    grad_modulate_weight = lax.dot_general(
        feat_own.astype(f32),
        mod_grad,
        (((0,), (0,)), ((), ())),
        precision=lax.Precision.HIGHEST,
        preferred_element_type=f32,
    )
    mod_width = modulate_bias.shape[0]
    grad_modulate_bias = jnp.sum(
        lax.dynamic_slice_in_dim(mod_grad, d * mod_width, mod_width, 1), axis=0
    )
    shape = (local, utts, width)
    return (
        layer_out.reshape(shape),
        grad_frames.reshape(shape),
        grad_skip.reshape(shape),
        grad_skip_weight,
        grad_qkv_weight,
        grad_output_weight,
        grad_up_weight,
        grad_up_bias,
        grad_down_weight,
        grad_down_bias,
        grad_modulate_weight,
        grad_modulate_bias,
    )


def solution(mesh):
    rows_two = P("seq", "batch", None)
    owned = P(ALL, None)
    vector = P(ALL)
    in_specs = (
        rows_two,
        rows_two,
        P("batch"),
        P("batch"),
        owned,
        owned,
        owned,
        owned,
        vector,
        owned,
        vector,
        owned,
        vector,
        rows_two,
    )
    out_specs = (
        rows_two,
        rows_two,
        rows_two,
        owned,
        owned,
        owned,
        owned,
        vector,
        owned,
        vector,
        owned,
        vector,
    )
    sizes = (mesh.shape["batch"], mesh.shape["seq"])
    return jax.shard_map(
        functools.partial(body, sizes),
        mesh=mesh,
        in_specs=in_specs,
        out_specs=out_specs,
        check_vma=False,
    )
```

```python
import functools
import math

import jax
import jax.numpy as jnp
from jax import lax
from jax.experimental import pallas as pl
from jax.experimental.pallas import tpu as pltpu
from jax.sharding import PartitionSpec as P

HEADS = 16
HEAD_DIM = 64
epsilon = 1e-06
masked_score = -1e30
f32 = jnp.float32
bf16 = jnp.bfloat16
ALL = ("batch", "seq")


def rms_norm(values):
    return values * lax.rsqrt(jnp.mean(values * values, axis=-1, keepdims=True) + epsilon)


def modulated(hidden, scale_rows, shift_rows):
    return rms_norm(hidden) * (1.0 + scale_rows) + shift_rows


def gelu_tanh(pre_values):
    return jax.nn.gelu(pre_values, approximate=True)


def time_embed(flow_times, embed_width):
    half_width = embed_width // 2
    frequency = jnp.exp(-math.log(10000.0) * jnp.arange(half_width, dtype=f32) / half_width)
    angles = 1000.0 * flow_times[:, None] * frequency[None, :]
    return jnp.concatenate([jnp.sin(angles), jnp.cos(angles)], axis=-1)


def params(semantics=None):
    return pltpu.CompilerParams(dimension_semantics=semantics, vmem_limit_bytes=60 * 1024 * 1024)


class Net:
    def __init__(self, batch, seq):
        self.batch, self.seq, self.n = batch, seq, batch * seq
        self.d = lax.axis_index("batch") * seq + lax.axis_index("seq")
        self.b = lax.axis_index("batch")
        self.s = lax.axis_index("seq")
        self.core = self.d & 1

    def swap(self, value, offset):
        return lax.ppermute(value, ALL, [(i, i ^ offset) for i in range(self.n)])

    def swap_by_core(self, value, even, odd):
        pairs = [(i, i ^ (odd if i & 1 else even)) for i in range(self.n)]
        return lax.ppermute(value, ALL, pairs)

    def sum_all(self, value):
        bit = 1
        while bit < self.n:
            value = value + self.swap(value, bit)
            bit *= 2
        return value


def cost(flops, moved, exps=0):
    return pl.CostEstimate(flops=int(flops), bytes_accessed=int(moved), transcendentals=int(exps))


def after(value, *others):
    return lax.optimization_barrier((value,) + tuple(others))[0]


def place(pieces, tables, count, columns=None):
    rows, width = pieces[0].shape[1:]
    columns = columns or (width,)
    counts = [p.shape[0] for p in pieces]
    total = sum(counts)
    table = jnp.concatenate(tables, axis=-1).astype(jnp.int32)
    if table.ndim == 1:
        table = jnp.broadcast_to(table[None], (len(columns), total))

    def kernel(table_ref, *refs):
        sources = refs[: len(pieces)]
        outs = refs[len(pieces) : len(pieces) + len(columns)]
        sems = refs[-1]
        copies = []
        at = 0
        for source, number in zip(sources, counts):
            for j in range(number):
                left = 0
                for o, wide in enumerate(columns):
                    copies.append(
                        pltpu.make_async_copy(
                            source.at[j, :, pl.ds(left, wide)],
                            outs[o].at[table_ref[o, at]],
                            sems.at[o, at],
                        )
                    )
                    left += wide
                at += 1
        for copy in copies:
            copy.start()
        for copy in copies:
            copy.wait()

    any_spec = pl.BlockSpec(memory_space=pl.ANY)
    outs = pl.pallas_call(
        kernel,
        out_shape=[jax.ShapeDtypeStruct((count, rows, wide), pieces[0].dtype) for wide in columns],
        in_specs=[pl.BlockSpec(memory_space=pltpu.SMEM)] + [any_spec] * len(pieces),
        out_specs=[pl.BlockSpec(memory_space=pltpu.VMEM)] * len(columns),
        scratch_shapes=[pltpu.SemaphoreType.DMA((len(columns), total))],
        compiler_params=params(),
        cost_estimate=cost(0, 4 * count * rows * width),
    )(table, *pieces)
    return [out.reshape(count * rows, wide) for out, wide in zip(outs, columns)]


def combine(inputs, tables, dtype):
    rows, width = inputs[0].shape[1:]
    count = tables[0].shape[0]
    table = jnp.stack([jnp.asarray(t, jnp.int32) for t in tables])

    def kernel(table_ref, *refs):
        total = refs[0][...].astype(f32)
        for ref in refs[1:-1]:
            total = total + ref[...].astype(f32)
        refs[-1][...] = total.astype(dtype)

    def spec(j):
        return pl.BlockSpec((1, rows, width), lambda i, t: (t[j, i], 0, 0))

    return pl.pallas_call(
        kernel,
        out_shape=jax.ShapeDtypeStruct((count, rows, width), dtype),
        grid_spec=pltpu.PrefetchScalarGridSpec(
            num_scalar_prefetch=1,
            grid=(count,),
            in_specs=[spec(j) for j in range(len(inputs))],
            out_specs=pl.BlockSpec((1, rows, width), lambda i, t: (i, 0, 0)),
        ),
        compiler_params=params(("arbitrary",)),
    )(table, *inputs)


def gather_start(net, shard):
    return jnp.stack([shard] + [net.swap(shard, k << 3) for k in (1, 2, 3)])


def gather_finish(net, near):
    d, c = net.d, net.core
    z = jnp.arange(4, dtype=jnp.int32) << 3
    second = jnp.where(c == 0, 2, 4)
    third = 6 - second
    far = net.swap_by_core(near, 2, 4)
    half = jnp.concatenate([near, far], axis=0)
    other = net.swap_by_core(half, 4, 2)
    own = jnp.concatenate([d ^ z, d ^ z ^ second])
    last = own ^ third
    mate = d ^ 1
    mate_own = jnp.concatenate([mate ^ z, mate ^ z ^ third])
    mate_last = mate_own ^ second
    return (
        [half, other, net.swap(half, 1), net.swap(other, 1)],
        [own, last, mate_own, mate_last],
    )


def grad_blocks(net, lefts, rights, segments, packed_rows, turns=None):
    depth = lefts[0].shape[0]
    tile = 1024
    piece = 32
    chip = net.d >> 1
    rel = jnp.arange(16, dtype=jnp.int32) ^ chip
    x_bit, y_bit, z = rel & 1, (rel >> 1) & 1, rel >> 2
    even = y_bit * 8 + x_bit * 4 + z
    odd = x_bit * 8 + y_bit * 4 + z
    mine = jnp.where(net.core == 0, even, odd)
    other = jnp.where(net.core == 0, odd, even)
    extra = jnp.stack([net.core] + (turns or [net.core * 0] * len(segments)))
    extra = jnp.pad(extra, (0, 16 - extra.shape[0]))
    table = jnp.stack([mine, other, extra]).astype(jnp.int32)
    starts = [0]
    for seg in segments:
        starts.append(starts[-1] + seg[0])
    steps = starts[-1]
    number = len(segments)

    def kernel(table_ref, *refs):
        left_refs, right_refs = refs[:number], refs[number : 2 * number]
        keep, send, scratch, sems = refs[2 * number :]
        t = pl.program_id(0)
        slot = t % 2
        core = table_ref[2, 0]

        def copy(v, p, at_slot, source_row, pos, dest_row):
            dest = send if p else keep
            return pltpu.make_async_copy(
                scratch.at[at_slot, pl.ds(pl.multiple_of(source_row, piece), piece)],
                dest.at[pos, pl.ds(pl.multiple_of(dest_row, piece), piece)],
                sems.at[at_slot, p, v],
            )

        def wait_slot(at_slot):
            for v in range(16):
                for p in range(2):
                    copy(v, p, at_slot, 0, 0, 0).wait()

        @pl.when(t >= 2)
        def _():
            wait_slot(slot)

        left, right = left_refs[-1][...], right_refs[-1][...]
        for i in range(number - 2, -1, -1):
            early = t < starts[i + 1]
            left = jnp.where(early, left_refs[i][...], left)
            right = jnp.where(early, right_refs[i][...], right)
        scratch[slot] = lax.dot_general(
            left, right, (((0,), (0,)), ((), ())), preferred_element_type=f32
        ).astype(bf16)
        for v in range(16):
            for p in range(2):
                side = core ^ p
                chip_at = source = dest_row = jnp.int32(0)
                for i, (_, subs, base, rise) in reversed(list(enumerate(segments))):
                    local = t - starts[i]
                    here = (
                        (local * (16 // subs) % 16 + v // subs) ^ table_ref[2, 1 + i],
                        (2 * (v // subs) + side) * subs * piece + (v % subs) * piece,
                        base + local * rise + (v % subs) * piece,
                    )
                    if i == number - 1:
                        chip_at, source, dest_row = here
                    else:
                        early = t < starts[i + 1]
                        chip_at = jnp.where(early, here[0], chip_at)
                        source = jnp.where(early, here[1], source)
                        dest_row = jnp.where(early, here[2], dest_row)
                copy(v, p, slot, source, table_ref[p, chip_at], dest_row).start()

        @pl.when(t == steps - 1)
        def _():
            wait_slot(slot)
            if steps > 1:
                wait_slot(1 - slot)

    def spec(array, i):
        count = array.shape[1] // tile
        if count == 1:
            return pl.BlockSpec((depth, tile), lambda t, table: (0, 0))
        return pl.BlockSpec(
            (depth, tile), lambda t, table: (0, jnp.clip(t - starts[i], 0, count - 1))
        )

    any_spec = pl.BlockSpec(memory_space=pl.ANY)
    shape = jax.ShapeDtypeStruct((16, packed_rows, tile), bf16)
    return pl.pallas_call(
        kernel,
        out_shape=[shape, shape],
        grid_spec=pltpu.PrefetchScalarGridSpec(
            num_scalar_prefetch=1,
            grid=(steps,),
            in_specs=[spec(a, i) for i, a in enumerate(lefts)]
            + [spec(a, i) for i, a in enumerate(rights)],
            out_specs=[any_spec, any_spec],
            scratch_shapes=[
                pltpu.VMEM((2, tile, tile), bf16),
                pltpu.SemaphoreType.DMA((2, 2, 16)),
            ],
        ),
        compiler_params=params(("arbitrary",)),
        cost_estimate=cost(2 * steps * depth * tile * tile, 3 * steps * tile * tile * 2),
    )(table, *lefts, *rights)


def total(*parts):
    result = parts[0].astype(f32)
    for part in parts[1:]:
        result = result + part.astype(f32)
    return result


class Scatter:
    def __init__(self, net, keep, send):
        self.net, self.parts = net, [keep]
        self.parts.append(net.swap(send, 1))

    def halve(self, low, high, even, odd):
        out = total(*[p[low:high] for p in self.parts]).astype(bf16)
        self.out = out
        self.pair = (even, odd)
        return out

    def push(self, out):
        self.parts.append(self.net.swap_by_core(out, *self.pair))

    def finish(self):
        outs = [total(*[p[k : k + 1] for p in self.parts]).astype(bf16) for k in (1, 2, 3)]
        zs = [self.net.swap(o, (k + 1) << 3) for k, o in enumerate(outs)]
        return total(*[p[0:1] for p in self.parts], *zs)[0]


def rope(values, cosine, sine, back):
    width = values.shape[-1]
    lane = lax.broadcasted_iota(jnp.int32, values.shape, 1)
    early = (lane & (HEAD_DIM - 1)) < HEAD_DIM // 2
    source = values * sine if back else values
    ahead = pltpu.roll(source, width - HEAD_DIM // 2, 1)
    behind = pltpu.roll(source, HEAD_DIM // 2, 1)
    if back:
        turned = jnp.where(early, ahead, -behind)
        return values * cosine + turned
    turned = jnp.where(early, -ahead, behind)
    return values * cosine + turned * sine


def wide_tables(cos_ref, sin_ref, width):
    reps = width // cos_ref.shape[-1]
    cosine = jnp.concatenate([cos_ref[...]] * reps, axis=-1)
    sine = jnp.concatenate([sin_ref[...]] * reps, axis=-1)
    return cosine, sine


def qkv_kernel(x_ref, w_ref, cos_ref, sin_ref, q_ref, k_ref, v_ref):
    width = q_ref.shape[-1]
    result = jnp.dot(x_ref[...], w_ref[...], preferred_element_type=f32)
    cosine, sine = wide_tables(cos_ref, sin_ref, width)
    scale = HEAD_DIM ** (-0.5)
    q_ref[...] = (rope(result[:, :width], cosine, sine, False) * scale).astype(bf16)
    k_ref[...] = rope(result[:, width : 2 * width], cosine, sine, False).astype(bf16)
    v_ref[...] = result[:, 2 * width :].astype(bf16)


def qkv_project(x, w, cosine, sine):
    rows, depth = x.shape
    width = w.shape[1] // 3
    block = min(512, rows)
    row = lambda wide: pl.BlockSpec((block, wide), lambda i: (i, 0))
    return pl.pallas_call(
        qkv_kernel,
        grid=(rows // block,),
        out_shape=[jax.ShapeDtypeStruct((rows, width), bf16)] * 3,
        in_specs=[row(depth), pl.BlockSpec(w.shape, lambda i: (0, 0)), row(128), row(128)],
        out_specs=[row(width)] * 3,
        compiler_params=params(("arbitrary",)),
        cost_estimate=cost(2 * rows * depth * 3 * width, 2 * rows * (depth + 3 * width)),
    )(x, w, cosine, sine)


def attend_kernel(heads, q_ref, k_ref, v_ref, bias_ref, o_ref, lse_ref):
    q = q_ref[...]
    k = k_ref[...]
    v = v_ref[...]
    bias = bias_ref[...]
    lane = lax.broadcasted_iota(jnp.int32, q.shape, 1) // HEAD_DIM
    spot = lax.broadcasted_iota(jnp.int32, lse_ref.shape, 1)
    out = jnp.zeros(q.shape, f32)
    lse = jnp.zeros(lse_ref.shape, f32)
    for h in range(heads):
        mine = lane == h
        qh = jnp.where(mine, q, jnp.zeros_like(q))
        s = lax.dot_general(qh, k, (((1,), (1,)), ((), ())), preferred_element_type=f32) + bias
        top = jnp.max(s, axis=-1, keepdims=True)
        p = jnp.exp(s - top)
        total = jnp.sum(p, axis=-1, keepdims=True)
        o = jnp.dot(p.astype(bf16), v, preferred_element_type=f32) / total
        out = jnp.where(mine, o, out)
        lse = jnp.where(spot == h, top + jnp.log(total), lse)
    o_ref[...] = out.astype(bf16)
    lse_ref[...] = lse


def attend(q, k, v, bias, heads):
    rows, width = q.shape
    block = 256
    row = lambda wide: pl.BlockSpec((block, wide), lambda i: (i, 0))
    whole = pl.BlockSpec((rows, width), lambda i: (0, 0))
    return pl.pallas_call(
        functools.partial(attend_kernel, heads),
        grid=(rows // block,),
        out_shape=[jax.ShapeDtypeStruct((rows, width), bf16), jax.ShapeDtypeStruct((rows, 128), f32)],
        in_specs=[row(width), whole, whole, pl.BlockSpec((1, rows), lambda i: (0, 0))],
        out_specs=[row(width), row(128)],
        compiler_params=params(("arbitrary",)),
        cost_estimate=cost(
            16 * rows * rows * heads * HEAD_DIM, 8 * rows * width, rows * rows * heads
        ),
    )(q, k, v, bias)


def attend_back_kernel(
    heads,
    first,
    q_ref,
    do_ref,
    o_ref,
    lse_ref,
    k_ref,
    v_ref,
    kt_ref,
    bias_ref,
    cosq_ref,
    sinq_ref,
    cosk_ref,
    sink_ref,
    dq_ref,
    dk_ref,
    dv_ref,
    p_all,
    ds_all,
    dk_acc,
    dv_acc,
):
    step = pl.program_id(0)
    q = q_ref[...]
    do = do_ref[...]
    k = k_ref[...]
    v = v_ref[...]
    block, width = q.shape
    lane = lax.broadcasted_iota(jnp.int32, q.shape, 1) // HEAD_DIM
    product = (do.astype(f32) * o_ref[...].astype(f32)).T
    lse_t = lse_ref[...].T
    bias = bias_ref[...]
    contract = (((1,), (1,)), ((), ()))
    q_parts, do_parts, dq_parts = [], [], []
    for h in range(heads):
        mine = lane == h
        qh = jnp.where(mine, q, jnp.zeros_like(q))
        doh = jnp.where(mine, do, jnp.zeros_like(do))
        q_parts.append(qh)
        do_parts.append(doh)
        row_dot = jnp.sum(product[h * HEAD_DIM : (h + 1) * HEAD_DIM], axis=0, keepdims=True)
        s = lax.dot_general(k, qh, contract, preferred_element_type=f32)
        p = jnp.exp(s + bias - lse_t[first + h : first + h + 1])
        dp = lax.dot_general(v, doh, contract, preferred_element_type=f32)
        ds = (p * (dp - row_dot)).astype(bf16)
        p_all[:, h * block : (h + 1) * block] = p.astype(bf16)
        ds_all[:, h * block : (h + 1) * block] = ds
        dq_parts.append(
            jnp.dot(kt_ref[h * HEAD_DIM : (h + 1) * HEAD_DIM, :], ds, preferred_element_type=f32)
        )
    dv = jnp.dot(p_all[...], jnp.concatenate(do_parts, axis=0), preferred_element_type=f32)
    dk = jnp.dot(ds_all[...], jnp.concatenate(q_parts, axis=0), preferred_element_type=f32)

    @pl.when(step == 0)
    def _():
        dv_acc[...] = dv
        dk_acc[...] = dk

    @pl.when(step > 0)
    def _():
        dv_acc[...] += dv
        dk_acc[...] += dk

    dq = jnp.concatenate(dq_parts, axis=0).T
    cosine, sine = wide_tables(cosq_ref, sinq_ref, width)
    dq_ref[...] = (rope(dq, cosine, sine, True) * (HEAD_DIM ** (-0.5))).astype(bf16)

    @pl.when(step == pl.num_programs(0) - 1)
    def _():
        cosine, sine = wide_tables(cosk_ref, sink_ref, width)
        dk_ref[...] = rope(dk_acc[...], cosine, sine, True).astype(bf16)
        dv_ref[...] = dv_acc[...].astype(bf16)


def attend_back(q, k, v, o, do, lse, bias, cosine, sine, heads, group):
    rows = q.shape[0]
    width = heads * HEAD_DIM
    block = 256
    lanes = lambda wide: pl.BlockSpec((block, wide), lambda i: (i, group))
    row = lambda wide: pl.BlockSpec((block, wide), lambda i: (i, 0))
    whole = lambda wide, at: pl.BlockSpec((rows, wide), lambda i: (0, at))
    out = jax.ShapeDtypeStruct((rows, width), bf16)
    return pl.pallas_call(
        functools.partial(attend_back_kernel, heads, group * heads),
        grid=(rows // block,),
        out_shape=[out] * 3,
        in_specs=[
            lanes(width),
            lanes(width),
            lanes(width),
            row(128),
            whole(width, group),
            whole(width, group),
            pl.BlockSpec((width, rows), lambda i: (group, 0)),
            whole(block, 0),
            row(128),
            row(128),
            whole(128, 0),
            whole(128, 0),
        ],
        out_specs=[row(width), whole(width, 0), whole(width, 0)],
        scratch_shapes=[
            pltpu.VMEM((rows, heads * block), bf16),
            pltpu.VMEM((rows, heads * block), bf16),
            pltpu.VMEM((rows, width), f32),
            pltpu.VMEM((rows, width), f32),
        ],
        compiler_params=params(("arbitrary",)),
        cost_estimate=cost(
            40 * rows * rows * heads * HEAD_DIM, 16 * rows * width, rows * rows * heads
        ),
    )(
        q,
        do,
        o,
        lse,
        k,
        v,
        k.T,
        jnp.broadcast_to(bias.reshape(rows, 1), (rows, block)),
        cosine,
        sine,
        cosine,
        sine,
    )


def body(
    mesh_sizes,
    frames_in,
    skip_in,
    flow_times,
    lengths,
    skip_weight,
    qkv_weight,
    output_weight,
    up_weight,
    up_bias,
    down_weight,
    down_bias,
    modulate_weight,
    modulate_bias,
    output_grad,
):
    batch, seq = mesh_sizes
    net = Net(batch, seq)
    n, d, s = net.n, net.d, net.s
    local, utts, width = frames_in.shape
    frames = frames_in.reshape(local, width)
    skips = skip_in.reshape(local, width)
    out_grad = output_grad.reshape(local, width).astype(f32)
    heads = HEADS // seq
    part = heads * HEAD_DIM
    rows = local * seq
    built = n == 32 and seq == 4
    wrow = width // n
    ff = up_weight.shape[1]

    seq_order = s ^ jnp.arange(seq, dtype=jnp.int32)
    by_part = qkv_weight.reshape(wrow, 3, seq, part)
    pieces = [
        lax.dynamic_index_in_dim(by_part, s ^ k, 2, keepdims=False).reshape(wrow, 3 * part)
        for k in range(seq)
    ]
    urow, drow = up_bias.shape[0], down_bias.shape[0]
    if built:
        vectors = jnp.concatenate(
            [
                up_bias.reshape(1, urow),
                jnp.pad(down_bias, (0, urow - drow)).reshape(1, urow),
                jnp.zeros((wrow - 2, urow), bf16),
            ]
        )
        pieces = [jnp.concatenate([p, vectors], axis=1) for p in pieces]
    pieces = [p if k == 0 else net.swap(p, k) for k, p in enumerate(pieces)]
    if built:
        near = gather_start(net, skip_weight)
        got, spots = gather_finish(net, near)
        (full_skip,) = place(got, spots, n)
        qkv_four = jnp.stack(pieces)
        qkv_four = after(qkv_four, near)
        qkv_z = jnp.concatenate([qkv_four] + [net.swap(qkv_four, k << 3) for k in (1, 2, 3)])
        qkv_y = net.swap(qkv_z, 4)
        k16 = jnp.arange(16, dtype=jnp.int32)
        z_spots = d ^ (((k16 >> 2) << 3) | (k16 & 3))
        full_qkv, vectors = place(
            [qkv_z, qkv_y], [z_spots, z_spots ^ 4], n, (3 * part, urow)
        )
        vectors = vectors.reshape(n, wrow, urow)
        full_up_bias = vectors[:, 0].reshape(1, ff).astype(f32)
        full_down_bias = vectors[:, 1, :drow].reshape(1, width).astype(f32)
        ou = after(jnp.concatenate([output_weight, up_weight], axis=1), qkv_z)
        near_ou = gather_start(net, ou)
        got, spots = gather_finish(net, near_ou)
        spots = jnp.concatenate(spots)
        turned = spots ^ (s * (n // seq))
        full_output, full_up = place(
            got, [jnp.stack([turned, spots])], n, (width, ff)
        )
        near_down = gather_start(net, after(down_weight, near_ou))
        got, spots = gather_finish(net, near_down)
        (full_down,) = place(got, spots, n)
    else:
        gather = lambda w, ax: lax.all_gather(w, ax, axis=0, tiled=True)
        full_skip = gather(skip_weight, ALL)
        full_qkv = gather(jnp.stack(pieces)[seq_order], "batch")
        full_qkv = full_qkv.reshape(batch, seq, wrow, 3 * part)
        full_qkv = full_qkv.reshape(width, 3 * part)
        full_output = gather(output_weight, ALL).reshape(seq, width // seq, width)[seq_order]
        full_output = full_output.reshape(width, width)
        full_up = gather(up_weight, ALL)
        full_down = gather(down_weight, ALL)

    mod_bias = lax.dynamic_update_slice_in_dim(
        jnp.zeros((6 * width,), f32), modulate_bias.astype(f32), d * modulate_bias.shape[0], 0
    )
    if built:
        times = jnp.broadcast_to(flow_times.reshape(1, 1), (8, 128))
        times = [times] + [net.swap(times, k << 3) for k in (1, 2, 3)]
        times = jnp.concatenate([t[:1] for t in times] * 2)
        times = jnp.stack([times[:4], net.swap(times, 4)[:4]], axis=1).reshape(batch, 128)
        all_times = times[:, 0]
    else:
        small = jnp.concatenate([up_bias.astype(f32), down_bias.astype(f32), flow_times])
        small_width = -(-small.shape[0] // 128) * 128
        small = jnp.pad(small, (0, small_width - small.shape[0]))
        slots = lax.broadcasted_iota(jnp.int32, (n, small_width), 0)
        small = net.sum_all(jnp.where(slots == d, small[None], 0.0))
        full_up_bias = small[:, :urow].reshape(1, ff)
        full_down_bias = small[:, urow : urow + drow].reshape(1, width)
        all_times = small.reshape(batch, seq, small_width)[:, 0, urow + drow]
    feat = jax.nn.silu(time_embed(all_times, width)).astype(bf16)
    feat_own = lax.dynamic_slice_in_dim(feat, d * wrow, wrow, 1)
    modulation = jnp.dot(feat_own, modulate_weight, preferred_element_type=f32)
    modulation = modulation + mod_bias[None]
    if built:
        sums = modulation[0:2]
        for k in (1, 2, 3):
            sums = sums + net.swap(modulation[2 * k : 2 * k + 2], k << 3)
        sums = sums[0:1] + net.swap(sums[1:2], 4)
        modulation = sums
        for k in (1, 2, 3):
            modulation = modulation + net.swap(sums, k)
    else:
        bit = batch // 2
        while bit:
            high = (net.b & bit) // bit
            sent = lax.dynamic_slice_in_dim(modulation, (1 - high) * bit, bit, 0)
            kept = lax.dynamic_slice_in_dim(modulation, high * bit, bit, 0)
            modulation = kept + net.swap(sent, bit * seq)
            bit //= 2
        bit = 1
        while bit < seq:
            modulation = modulation + net.swap(modulation, bit)
            bit *= 2
    shift_one, scale_one, gate_one, shift_two, scale_two, gate_two = jnp.split(modulation, 6, -1)

    half_dim = HEAD_DIM // 2
    inverse = jnp.exp(-math.log(10000.0) * 2.0 * jnp.arange(half_dim, dtype=f32) / HEAD_DIM)
    positions = (
        seq_order[:, None] * local + jnp.arange(local, dtype=jnp.int32)[None]
    ).reshape(rows)
    angles = positions.astype(f32)[:, None] * jnp.tile(inverse, 128 // half_dim)[None]
    cosine, sine = jnp.cos(angles), jnp.sin(angles)
    key_bias = jnp.where(positions < lengths[0], 0.0, masked_score).astype(f32)[None]

    joined = jnp.concatenate([frames, skips], axis=-1)
    hidden_zero = jnp.dot(joined, full_skip, preferred_element_type=f32)
    normed_one = modulated(hidden_zero, scale_one, shift_one).astype(bf16)
    across = {0: normed_one}
    bit = seq // 2
    while bit:
        across.update({i | bit: net.swap(a, bit) for i, a in list(across.items())})
        bit //= 2
    normed_all = jnp.concatenate([across[i] for i in range(seq)])
    q, k, v = qkv_project(normed_all, full_qkv, cosine, sine)
    att, lse = attend(q, k, v, key_bias, heads)
    blocks = [att[i * local : (i + 1) * local] for i in range(seq)]
    attended = jnp.concatenate(
        [b if i == 0 else net.swap(b, i) for i, b in enumerate(blocks)], axis=-1
    )
    attn_proj = jnp.dot(attended, full_output, preferred_element_type=f32)
    hidden_one = hidden_zero + gate_one * attn_proj
    normed_two = modulated(hidden_one, scale_two, shift_two).astype(bf16)
    pre_act = jnp.dot(normed_two, full_up, preferred_element_type=f32) + full_up_bias
    activated = gelu_tanh(pre_act).astype(bf16)
    ffn_out = jnp.dot(activated, full_down, preferred_element_type=f32) + full_down_bias
    layer_out = (hidden_one + gate_two * ffn_out).astype(bf16)

    rows_dot = lambda a, b: lax.dot_general(
        a, b, (((0,), (0,)), ((), ())), preferred_element_type=f32
    )
    back_dot = lambda a, b: lax.dot_general(
        a, b, (((1,), (1,)), ((), ())), preferred_element_type=f32
    )

    def scattered(grads, turn=False):
        if turn:
            grads = grads.reshape(seq, width // seq, -1)[seq_order].reshape(grads.shape)
        return lax.psum_scatter(
            grads.astype(bf16), ALL, scatter_dimension=0, tiled=True
        ).astype(f32)

    ffn_grad = out_grad * gate_two
    down_bias_term = jnp.sum(ffn_grad, axis=0)
    ffn_grad_low = ffn_grad.astype(bf16)
    act_grad = back_dot(ffn_grad_low, full_down)
    pre_grad = jax.vjp(gelu_tanh, pre_act)[1](act_grad)[0]
    up_bias_term = jnp.sum(pre_grad, axis=0)
    pre_grad_low = pre_grad.astype(bf16)
    normed_two_grad = back_dot(pre_grad_low, full_up)
    pull_two = jax.vjp(modulated, hidden_one, scale_two, shift_two)[1]
    hidden_grad_two, scale_two_grad, shift_two_grad = pull_two(normed_two_grad)
    gate_two_grad = jnp.sum(out_grad * ffn_out, axis=0)
    hidden_one_grad = out_grad + hidden_grad_two
    gate_one_grad = jnp.sum(hidden_one_grad * attn_proj, axis=0)
    proj_grad_low = (hidden_one_grad * gate_one).astype(bf16)
    attended_grad = back_dot(proj_grad_low, full_output).astype(bf16)
    pieces = [attended_grad[:, i * part : (i + 1) * part] for i in range(seq)]
    grad_all = jnp.concatenate([p if i == 0 else net.swap(p, i) for i, p in enumerate(pieces)])
    pair = lambda i, gate: attend_back(
        q, k, v, att, gate, lse, key_bias, cosine, sine, 2, i
    )
    if built:
        down = Scatter(net, *grad_blocks(net, [activated], [ffn_grad_low], [(4, 4, 0, 0)], 128))
        up = Scatter(
            net,
            *grad_blocks(
                net,
                [normed_two, attended],
                [pre_grad_low, proj_grad_low],
                [(4, 1, 0, 32), (1, 1, 128, 0)],
                160,
                [s * 0, s * (n // seq // 2)],
            ),
        )
        down_half = down.halve(8, 16, 4, 2)
        up_half = up.halve(8, 16, 4, 2)
        grad_all, down_half, up_half = lax.optimization_barrier((grad_all, down_half, up_half))
        down.push(down_half)
        up.push(up_half)
        results = []
        for i in range(heads // 2):
            if i == 1:
                down_half = down.halve(4, 8, 2, 4)
                grad_all, down_half, _ = lax.optimization_barrier((grad_all, down_half, results))
                down.push(down_half)
            results.append(pair(i, grad_all))
        up.push(up.halve(4, 8, 2, 4))
        grad_down_weight = down.finish()
        own = up.finish()
        grad_up_weight = jnp.concatenate(
            [own[i * wrow : (i + 1) * wrow] for i in range(4)], axis=1
        )
        grad_output_weight = own[4 * wrow :]
    else:
        grad_down_weight = scattered(rows_dot(activated, ffn_grad_low))
        grad_up_weight = scattered(rows_dot(normed_two, pre_grad_low))
        grad_output_weight = scattered(rows_dot(attended, proj_grad_low), True)
        results = [pair(i, grad_all) for i in range(heads // 2)]
    qkv_grad = jnp.concatenate([r[i] for i in range(3) for r in results], axis=-1)

    odd = jnp.concatenate([qkv_grad[i * local : (i + 1) * local] for i in range(1, seq, 2)])
    even = [qkv_grad[i * local : (i + 1) * local] for i in range(0, seq, 2)]
    sent = net.swap(back_dot(odd, full_qkv).astype(bf16), 1).astype(f32)
    halves = [
        back_dot(e, full_qkv) + sent[i * local : (i + 1) * local] for i, e in enumerate(even)
    ]
    step = 2
    while len(halves) > 1:
        keep = halves[0::2]
        give = halves[1::2]
        halves = [
            a + net.swap(g.astype(bf16), step).astype(f32) for a, g in zip(keep, give)
        ]
        step *= 2
    normed_one_grad = halves[0]
    qkv_part = rows_dot(normed_all, qkv_grad).astype(bf16)
    if built:
        units = qkv_part.reshape(batch, seq * wrow, 3 * part)
        z = jnp.arange(4, dtype=jnp.int32)
        r1 = net.swap(combine([units], [net.b ^ 1 ^ (z << 1)], bf16), 4)
        parts = combine([units, r1], [net.b ^ (z[1:] << 1), z[1:]], bf16)
        zs = [net.swap(parts[i - 1 : i], i << 3) for i in (1, 2, 3)]
        zero = jnp.zeros((1,), jnp.int32)
        own = combine([units, r1] + zs, [net.b + zero] + [zero] * 4, f32)[0]
    else:
        own = lax.psum_scatter(qkv_part, "batch", scatter_dimension=0, tiled=True).astype(f32)
    own = own.reshape(seq, wrow, 3, part)
    cols = [
        lax.dynamic_index_in_dim(own, s ^ i, 0, keepdims=False) for i in range(seq)
    ]
    cols = jnp.stack([c if i == 0 else net.swap(c, i) for i, c in enumerate(cols)], axis=2)
    bit = 1
    while bit < seq:
        swapped = cols.reshape(wrow, 3, seq // (2 * bit), 2, bit, part)[:, :, :, ::-1]
        cols = jnp.where((s & bit) > 0, swapped.reshape(cols.shape), cols)
        bit *= 2
    grad_qkv_weight = cols.reshape(wrow, 3 * width)

    pull_one = jax.vjp(modulated, hidden_zero, scale_one, shift_one)[1]
    hidden_grad_one, scale_one_grad, shift_one_grad = pull_one(normed_one_grad)
    hidden_zero_grad = (hidden_one_grad + hidden_grad_one).astype(bf16)
    if built:
        skip = Scatter(
            net, *grad_blocks(net, [joined], [hidden_zero_grad], [(2, 2, 0, 0)], 64)
        )
        skip.push(skip.halve(8, 16, 4, 2))
        skip.push(skip.halve(4, 8, 2, 4))
        grad_skip_weight = skip.finish()
    else:
        grad_skip_weight = scattered(rows_dot(joined, hidden_zero_grad))
    grad_frames = back_dot(hidden_zero_grad, full_skip[:width])
    grad_skip = back_dot(hidden_zero_grad, full_skip[width:])

    def by_utterance(*vectors):
        row = jnp.concatenate([vec.reshape(1, -1) for vec in vectors], axis=1)
        place_row = lax.broadcasted_iota(jnp.int32, (batch, row.shape[1]), 0)
        return jnp.where(place_row == net.b, row, 0.0)

    if built:
        order = net.b ^ jnp.arange(batch, dtype=jnp.int32)
        feat_own = feat_own[order]

    early = by_utterance(gate_one_grad, shift_two_grad, scale_two_grad, gate_two_grad)
    flat = jnp.concatenate([early.reshape(-1), up_bias_term, down_bias_term])
    flat = net.sum_all(flat.reshape(-1, 128)).reshape(-1)
    early = flat[: batch * 4 * width].reshape(batch, 4 * width)
    up_sum = flat[batch * 4 * width : batch * 4 * width + ff]
    down_sum = flat[batch * 4 * width + ff :]
    grad_up_bias = lax.dynamic_slice_in_dim(up_sum, d * urow, urow, 0)
    grad_down_bias = lax.dynamic_slice_in_dim(down_sum, d * drow, drow, 0)
    late = net.sum_all(by_utterance(shift_one_grad, scale_one_grad))
    mod_grad = jnp.concatenate([late, early], axis=1)
    grad_modulate_weight = lax.dot_general(
        feat_own.astype(f32),
        mod_grad,
        (((0,), (0,)), ((), ())),
        precision=lax.Precision.HIGHEST,
        preferred_element_type=f32,
    )
    mod_width = modulate_bias.shape[0]
    grad_modulate_bias = jnp.sum(
        lax.dynamic_slice_in_dim(mod_grad, d * mod_width, mod_width, 1), axis=0
    )
    shape = (local, utts, width)
    return (
        layer_out.reshape(shape),
        grad_frames.reshape(shape),
        grad_skip.reshape(shape),
        grad_skip_weight,
        grad_qkv_weight,
        grad_output_weight,
        grad_up_weight,
        grad_up_bias,
        grad_down_weight,
        grad_down_bias,
        grad_modulate_weight,
        grad_modulate_bias,
    )


def solution(mesh):
    rows_two = P("seq", "batch", None)
    owned = P(ALL, None)
    vector = P(ALL)
    in_specs = (
        rows_two,
        rows_two,
        P("batch"),
        P("batch"),
        owned,
        owned,
        owned,
        owned,
        vector,
        owned,
        vector,
        owned,
        vector,
        rows_two,
    )
    out_specs = (
        rows_two,
        rows_two,
        rows_two,
        owned,
        owned,
        owned,
        owned,
        vector,
        owned,
        vector,
        owned,
        vector,
    )
    sizes = (mesh.shape["batch"], mesh.shape["seq"])
    return jax.shard_map(
        functools.partial(body, sizes),
        mesh=mesh,
        in_specs=in_specs,
        out_specs=out_specs,
        check_vma=False,
    )
```

```python
import functools
import math

import jax
import jax.numpy as jnp
from jax import lax
from jax.experimental import pallas as pl
from jax.experimental.pallas import tpu as pltpu
from jax.sharding import PartitionSpec as P

HEADS = 16
HEAD_DIM = 64
epsilon = 1e-06
masked_score = -1e30
f32 = jnp.float32
bf16 = jnp.bfloat16
ALL = ("batch", "seq")


def rms_norm(values):
    return values * lax.rsqrt(jnp.mean(values * values, axis=-1, keepdims=True) + epsilon)


def modulated(hidden, scale_rows, shift_rows):
    return rms_norm(hidden) * (1.0 + scale_rows) + shift_rows


def gelu_tanh(pre_values):
    return jax.nn.gelu(pre_values, approximate=True)


def time_embed(flow_times, embed_width):
    half_width = embed_width // 2
    frequency = jnp.exp(-math.log(10000.0) * jnp.arange(half_width, dtype=f32) / half_width)
    angles = 1000.0 * flow_times[:, None] * frequency[None, :]
    return jnp.concatenate([jnp.sin(angles), jnp.cos(angles)], axis=-1)


def params(semantics=None):
    return pltpu.CompilerParams(dimension_semantics=semantics, vmem_limit_bytes=60 * 1024 * 1024)


class Net:
    def __init__(self, batch, seq):
        self.batch, self.seq, self.n = batch, seq, batch * seq
        self.d = lax.axis_index("batch") * seq + lax.axis_index("seq")
        self.b = lax.axis_index("batch")
        self.s = lax.axis_index("seq")
        self.core = self.d & 1

    def swap(self, value, offset):
        return lax.ppermute(value, ALL, [(i, i ^ offset) for i in range(self.n)])

    def swap_by_core(self, value, even, odd):
        pairs = [(i, i ^ (odd if i & 1 else even)) for i in range(self.n)]
        return lax.ppermute(value, ALL, pairs)

    def sum_all(self, value):
        bit = 1
        while bit < self.n:
            value = value + self.swap(value, bit)
            bit *= 2
        return value


def cost(flops, moved, exps=0):
    return pl.CostEstimate(flops=int(flops), bytes_accessed=int(moved), transcendentals=int(exps))


def after(value, *others):
    return lax.optimization_barrier((value,) + tuple(others))[0]


def place(pieces, tables, count, columns=None):
    rows, width = pieces[0].shape[1:]
    columns = columns or (width,)
    counts = [p.shape[0] for p in pieces]
    total = sum(counts)
    table = jnp.concatenate(tables, axis=-1).astype(jnp.int32)
    if table.ndim == 1:
        table = jnp.broadcast_to(table[None], (len(columns), total))

    def kernel(table_ref, *refs):
        sources = refs[: len(pieces)]
        outs = refs[len(pieces) : len(pieces) + len(columns)]
        sems = refs[-1]
        copies = []
        at = 0
        for source, number in zip(sources, counts):
            for j in range(number):
                left = 0
                for o, wide in enumerate(columns):
                    copies.append(
                        pltpu.make_async_copy(
                            source.at[j, :, pl.ds(left, wide)],
                            outs[o].at[table_ref[o, at]],
                            sems.at[o, at],
                        )
                    )
                    left += wide
                at += 1
        for copy in copies:
            copy.start()
        for copy in copies:
            copy.wait()

    any_spec = pl.BlockSpec(memory_space=pl.ANY)
    outs = pl.pallas_call(
        kernel,
        out_shape=[jax.ShapeDtypeStruct((count, rows, wide), pieces[0].dtype) for wide in columns],
        in_specs=[pl.BlockSpec(memory_space=pltpu.SMEM)] + [any_spec] * len(pieces),
        out_specs=[pl.BlockSpec(memory_space=pltpu.VMEM)] * len(columns),
        scratch_shapes=[pltpu.SemaphoreType.DMA((len(columns), total))],
        compiler_params=params(),
        cost_estimate=cost(0, 4 * count * rows * width),
    )(table, *pieces)
    return [out.reshape(count * rows, wide) for out, wide in zip(outs, columns)]


class Gather:
    def __init__(self, net, shard):
        self.net = net
        self.near = jnp.stack([shard] + [net.swap(shard, k << 3) for k in (1, 2, 3)])

    def far(self):
        self.half = jnp.concatenate([self.near, self.net.swap_by_core(self.near, 2, 4)])
        self.mate_half = self.net.swap(self.half, 1)

    def last(self):
        self.other = self.net.swap_by_core(self.half, 4, 2)
        self.mate_other = self.net.swap(self.other, 1)

    def blocks(self):
        d = self.net.d
        z = jnp.arange(4, dtype=jnp.int32) << 3
        second = jnp.where(self.net.core == 0, 2, 4)
        third = 6 - second
        own = jnp.concatenate([d ^ z, d ^ z ^ second])
        mate = d ^ 1
        mate_own = jnp.concatenate([mate ^ z, mate ^ z ^ third])
        return (
            [self.half, self.other, self.mate_half, self.mate_other],
            [own, own ^ third, mate_own, mate_own ^ second],
        )


def grad_blocks(net, lefts, rights, segments, packed_rows, turns=None):
    depth = lefts[0].shape[0]
    tile = 1024
    piece = 32
    chip = net.d >> 1
    rel = jnp.arange(16, dtype=jnp.int32) ^ chip
    x_bit, y_bit, z = rel & 1, (rel >> 1) & 1, rel >> 2
    even = y_bit * 8 + x_bit * 4 + z
    odd = x_bit * 8 + y_bit * 4 + z
    mine = jnp.where(net.core == 0, even, odd)
    other = jnp.where(net.core == 0, odd, even)
    extra = jnp.stack([net.core] + (turns or [net.core * 0] * len(segments)))
    extra = jnp.pad(extra, (0, 16 - extra.shape[0]))
    table = jnp.stack([mine, other, extra]).astype(jnp.int32)
    starts = [0]
    for seg in segments:
        starts.append(starts[-1] + seg[0])
    steps = starts[-1]
    number = len(segments)

    def kernel(table_ref, *refs):
        left_refs, right_refs = refs[:number], refs[number : 2 * number]
        keep, send, scratch, sems = refs[2 * number :]
        t = pl.program_id(0)
        slot = t % 2
        core = table_ref[2, 0]

        def copy(v, p, at_slot, source_row, pos, dest_row):
            dest = send if p else keep
            return pltpu.make_async_copy(
                scratch.at[at_slot, pl.ds(pl.multiple_of(source_row, piece), piece)],
                dest.at[pos, pl.ds(pl.multiple_of(dest_row, piece), piece)],
                sems.at[at_slot, p, v],
            )

        def wait_slot(at_slot):
            for v in range(16):
                for p in range(2):
                    copy(v, p, at_slot, 0, 0, 0).wait()

        @pl.when(t >= 2)
        def _():
            wait_slot(slot)

        left, right = left_refs[-1][...], right_refs[-1][...]
        for i in range(number - 2, -1, -1):
            early = t < starts[i + 1]
            left = jnp.where(early, left_refs[i][...], left)
            right = jnp.where(early, right_refs[i][...], right)
        scratch[slot] = lax.dot_general(
            left, right, (((0,), (0,)), ((), ())), preferred_element_type=f32
        ).astype(bf16)
        for v in range(16):
            for p in range(2):
                side = core ^ p
                chip_at = source = dest_row = jnp.int32(0)
                for i, (_, subs, base, rise) in reversed(list(enumerate(segments))):
                    local = t - starts[i]
                    here = (
                        (local * (16 // subs) % 16 + v // subs) ^ table_ref[2, 1 + i],
                        (2 * (v // subs) + side) * subs * piece + (v % subs) * piece,
                        base + local * rise + (v % subs) * piece,
                    )
                    if i == number - 1:
                        chip_at, source, dest_row = here
                    else:
                        early = t < starts[i + 1]
                        chip_at = jnp.where(early, here[0], chip_at)
                        source = jnp.where(early, here[1], source)
                        dest_row = jnp.where(early, here[2], dest_row)
                copy(v, p, slot, source, table_ref[p, chip_at], dest_row).start()

        @pl.when(t == steps - 1)
        def _():
            wait_slot(slot)
            if steps > 1:
                wait_slot(1 - slot)

    def spec(array, i):
        count = array.shape[1] // tile
        if count == 1:
            return pl.BlockSpec((depth, tile), lambda t, table: (0, 0))
        return pl.BlockSpec(
            (depth, tile), lambda t, table: (0, jnp.clip(t - starts[i], 0, count - 1))
        )

    any_spec = pl.BlockSpec(memory_space=pl.ANY)
    shape = jax.ShapeDtypeStruct((16, packed_rows, tile), bf16)
    return pl.pallas_call(
        kernel,
        out_shape=[shape, shape],
        grid_spec=pltpu.PrefetchScalarGridSpec(
            num_scalar_prefetch=1,
            grid=(steps,),
            in_specs=[spec(a, i) for i, a in enumerate(lefts)]
            + [spec(a, i) for i, a in enumerate(rights)],
            out_specs=[any_spec, any_spec],
            scratch_shapes=[
                pltpu.VMEM((2, tile, tile), bf16),
                pltpu.SemaphoreType.DMA((2, 2, 16)),
            ],
        ),
        compiler_params=params(("arbitrary",)),
        cost_estimate=cost(2 * steps * depth * tile * tile, 3 * steps * tile * tile * 2),
    )(table, *lefts, *rights)


def total(*parts):
    result = parts[0].astype(f32)
    for part in parts[1:]:
        result = result + part.astype(f32)
    return result


class Scatter:
    def __init__(self, net, keep, send):
        self.net, self.parts = net, [keep]
        self.parts.append(net.swap(send, 1))

    def halve(self, low, high, even, odd):
        out = total(*[p[low:high] for p in self.parts]).astype(bf16)
        self.out = out
        self.pair = (even, odd)
        return out

    def push(self, out):
        self.parts.append(self.net.swap_by_core(out, *self.pair))

    def finish(self):
        outs = [total(*[p[k : k + 1] for p in self.parts]).astype(bf16) for k in (1, 2, 3)]
        zs = [self.net.swap(o, (k + 1) << 3) for k, o in enumerate(outs)]
        return total(*[p[0:1] for p in self.parts], *zs)[0]


def utterance_rows(net, row):
    for part in [net.swap(row, k) for k in (1, 2, 3)]:
        row = row + part
    near = jnp.concatenate([row] + [net.swap(row, k << 3) for k in (1, 2, 3)])
    return jnp.stack([near, net.swap(near, 4)], axis=1).reshape(8, row.shape[1])


def spread_columns(parts, order, groups):
    rows, width = parts[0].shape
    number = len(parts)
    wide = width // groups

    def kernel(order_ref, *refs):
        out, sems = refs[number:]
        copies = []
        for i in range(number):
            for g in range(groups):
                at = pl.multiple_of((order_ref[i] + g * number) * wide, wide)
                copies.append(
                    pltpu.make_async_copy(
                        refs[i].at[:, pl.ds(g * wide, wide)],
                        out.at[:, pl.ds(at, wide)],
                        sems.at[i, g],
                    )
                )
        for copy in copies:
            copy.start()
        for copy in copies:
            copy.wait()

    return pl.pallas_call(
        kernel,
        out_shape=jax.ShapeDtypeStruct((rows, width * number), parts[0].dtype),
        in_specs=[pl.BlockSpec(memory_space=pltpu.SMEM)]
        + [pl.BlockSpec(memory_space=pltpu.VMEM)] * number,
        out_specs=pl.BlockSpec(memory_space=pltpu.VMEM),
        scratch_shapes=[pltpu.SemaphoreType.DMA((number, groups))],
        compiler_params=params(),
        cost_estimate=cost(0, 8 * rows * width * number),
    )(order.astype(jnp.int32), *parts)


def rope(values, cosine, sine, back):
    width = values.shape[-1]
    lane = lax.broadcasted_iota(jnp.int32, values.shape, 1)
    early = (lane & (HEAD_DIM - 1)) < HEAD_DIM // 2
    source = values * sine if back else values
    ahead = pltpu.roll(source, width - HEAD_DIM // 2, 1)
    behind = pltpu.roll(source, HEAD_DIM // 2, 1)
    if back:
        turned = jnp.where(early, ahead, -behind)
        return values * cosine + turned
    turned = jnp.where(early, -ahead, behind)
    return values * cosine + turned * sine


def wide_tables(cos_ref, sin_ref, width):
    reps = width // cos_ref.shape[-1]
    cosine = jnp.concatenate([cos_ref[...]] * reps, axis=-1)
    sine = jnp.concatenate([sin_ref[...]] * reps, axis=-1)
    return cosine, sine


def qkv_kernel(number, *refs):
    w_ref, cos_ref, sin_ref, q_ref, k_ref, v_ref = refs[number:]
    width = q_ref.shape[-1]
    scale = HEAD_DIM ** (-0.5)
    for i in range(number):

        @pl.when(pl.program_id(0) == i)
        def _():
            result = jnp.dot(refs[i][...], w_ref[...], preferred_element_type=f32)
            cosine, sine = wide_tables(cos_ref, sin_ref, width)
            q_ref[...] = (rope(result[:, :width], cosine, sine, False) * scale).astype(bf16)
            k_ref[...] = rope(result[:, width : 2 * width], cosine, sine, False).astype(bf16)
            v_ref[...] = result[:, 2 * width :].astype(bf16)


def qkv_project(parts, w, cosine, sine):
    block, depth = parts[0].shape
    rows = block * len(parts)
    width = w.shape[1] // 3
    row = lambda wide: pl.BlockSpec((block, wide), lambda i: (i, 0))
    whole = lambda a: pl.BlockSpec(a.shape, lambda i: (0, 0))
    return pl.pallas_call(
        functools.partial(qkv_kernel, len(parts)),
        grid=(len(parts),),
        out_shape=[jax.ShapeDtypeStruct((rows, width), bf16)] * 3,
        in_specs=[whole(a) for a in parts] + [whole(w), row(128), row(128)],
        out_specs=[row(width)] * 3,
        compiler_params=params(("arbitrary",)),
        cost_estimate=cost(2 * rows * depth * 3 * width, 2 * rows * (depth + 3 * width)),
    )(*parts, w, cosine, sine)


def qkv_back(pieces, w, local, first, dtype):
    rows = pieces[0].shape[0]
    wide = pieces[0].shape[1]
    count = rows // local // 2
    width = len(pieces) * wide

    def kernel(*refs):
        w_ref, all_ref, out_ref = refs[len(pieces) :]
        joined = jnp.concatenate([r[...] for r in refs[: len(pieces)]], axis=-1)
        all_ref[...] = joined
        out_ref[...] = lax.dot_general(
            joined, w_ref[...], (((1,), (1,)), ((), ())), preferred_element_type=f32
        ).astype(dtype)

    return pl.pallas_call(
        kernel,
        grid=(count,),
        out_shape=[
            jax.ShapeDtypeStruct((count * local, width), bf16),
            jax.ShapeDtypeStruct((count * local, w.shape[0]), dtype),
        ],
        in_specs=[pl.BlockSpec((local, wide), lambda i: (2 * i + first, 0))] * len(pieces)
        + [pl.BlockSpec(w.shape, lambda i: (0, 0))],
        out_specs=[
            pl.BlockSpec((local, width), lambda i: (i, 0)),
            pl.BlockSpec((local, w.shape[0]), lambda i: (i, 0)),
        ],
        compiler_params=params(("arbitrary",)),
        cost_estimate=cost(2 * count * local * width * w.shape[0], 8 * count * local * w.shape[0]),
    )(*pieces, w)


def qkv_grad_blocks(net, lefts, grads):
    local, depth = lefts[0].shape
    width = grads[0].shape[1]
    rows = depth // 8
    t = jnp.arange(8, dtype=jnp.int32)
    table = net.b ^ ((t & 3) << 1) ^ jnp.where(t < 4, 1, 0)
    number = len(lefts)

    def kernel(table_ref, *refs):
        keep, send = refs[number + len(grads) :]
        result = jnp.zeros((rows, width), f32)
        for i in range(number):
            grad = refs[number + i % 2][(i // 2) * local : (i // 2 + 1) * local]
            result = result + lax.dot_general(
                refs[i][...], grad, (((0,), (0,)), ((), ())), preferred_element_type=f32
            )
        result = result.astype(bf16)[None]
        step = pl.program_id(0)

        @pl.when(step < 4)
        def _():
            send[...] = result

        @pl.when(step >= 4)
        def _():
            keep[...] = result

    shape = jax.ShapeDtypeStruct((4, rows, width), bf16)
    block = (1, rows, width)
    return pl.pallas_call(
        kernel,
        out_shape=[shape, shape],
        grid_spec=pltpu.PrefetchScalarGridSpec(
            num_scalar_prefetch=1,
            grid=(8,),
            in_specs=[pl.BlockSpec((local, rows), lambda i, t: (0, t[i]))] * number
            + [pl.BlockSpec(g.shape, lambda i, t: (0, 0)) for g in grads],
            out_specs=[
                pl.BlockSpec(block, lambda i, t: (jnp.maximum(i - 4, 0), 0, 0)),
                pl.BlockSpec(block, lambda i, t: (jnp.minimum(i, 3), 0, 0)),
            ],
        ),
        compiler_params=params(("arbitrary",)),
        cost_estimate=cost(2 * number * local * depth * width, 4 * depth * width),
    )(table, *lefts, *grads)


def attend_kernel(heads, q_ref, k_ref, v_ref, bias_ref, o_ref, lse_ref):
    q = q_ref[...]
    k = k_ref[...]
    v = v_ref[...]
    bias = bias_ref[...]
    lane = lax.broadcasted_iota(jnp.int32, q.shape, 1) // HEAD_DIM
    spot = lax.broadcasted_iota(jnp.int32, lse_ref.shape, 1)
    out = jnp.zeros(q.shape, f32)
    lse = jnp.zeros(lse_ref.shape, f32)
    for h in range(heads):
        mine = lane == h
        qh = jnp.where(mine, q, jnp.zeros_like(q))
        s = lax.dot_general(qh, k, (((1,), (1,)), ((), ())), preferred_element_type=f32) + bias
        top = jnp.max(s, axis=-1, keepdims=True)
        p = jnp.exp(s - top)
        total = jnp.sum(p, axis=-1, keepdims=True)
        o = jnp.dot(p.astype(bf16), v, preferred_element_type=f32) / total
        out = jnp.where(mine, o, out)
        lse = jnp.where(spot == h, top + jnp.log(total), lse)
    o_ref[...] = out.astype(bf16)
    lse_ref[...] = lse


def attend(q, k, v, bias, heads):
    rows, width = q.shape
    block = 256
    row = lambda wide: pl.BlockSpec((block, wide), lambda i: (i, 0))
    whole = pl.BlockSpec((rows, width), lambda i: (0, 0))
    return pl.pallas_call(
        functools.partial(attend_kernel, heads),
        grid=(rows // block,),
        out_shape=[jax.ShapeDtypeStruct((rows, width), bf16), jax.ShapeDtypeStruct((rows, 128), f32)],
        in_specs=[row(width), whole, whole, pl.BlockSpec((1, rows), lambda i: (0, 0))],
        out_specs=[row(width), row(128)],
        compiler_params=params(("arbitrary",)),
        cost_estimate=cost(
            16 * rows * rows * heads * HEAD_DIM, 8 * rows * width, rows * rows * heads
        ),
    )(q, k, v, bias)


def attend_back_kernel(
    heads,
    first,
    q_ref,
    do_ref,
    o_ref,
    lse_ref,
    k_ref,
    v_ref,
    kt_ref,
    bias_ref,
    cosq_ref,
    sinq_ref,
    cosk_ref,
    sink_ref,
    dq_ref,
    dk_ref,
    dv_ref,
    p_all,
    ds_all,
    dk_acc,
    dv_acc,
):
    step = pl.program_id(0)
    q = q_ref[...]
    do = do_ref[...]
    k = k_ref[...]
    v = v_ref[...]
    block, width = q.shape
    lane = lax.broadcasted_iota(jnp.int32, q.shape, 1) // HEAD_DIM
    product = (do.astype(f32) * o_ref[...].astype(f32)).T
    lse_t = lse_ref[...].T
    bias = bias_ref[...]
    contract = (((1,), (1,)), ((), ()))
    q_parts, do_parts, dq_parts = [], [], []
    for h in range(heads):
        mine = lane == h
        qh = jnp.where(mine, q, jnp.zeros_like(q))
        doh = jnp.where(mine, do, jnp.zeros_like(do))
        q_parts.append(qh)
        do_parts.append(doh)
        row_dot = jnp.sum(product[h * HEAD_DIM : (h + 1) * HEAD_DIM], axis=0, keepdims=True)
        s = lax.dot_general(k, qh, contract, preferred_element_type=f32)
        p = jnp.exp(s + bias - lse_t[first + h : first + h + 1])
        dp = lax.dot_general(v, doh, contract, preferred_element_type=f32)
        ds = (p * (dp - row_dot)).astype(bf16)
        p_all[:, h * block : (h + 1) * block] = p.astype(bf16)
        ds_all[:, h * block : (h + 1) * block] = ds
        dq_parts.append(
            jnp.dot(kt_ref[h * HEAD_DIM : (h + 1) * HEAD_DIM, :], ds, preferred_element_type=f32)
        )
    dv = jnp.dot(p_all[...], jnp.concatenate(do_parts, axis=0), preferred_element_type=f32)
    dk = jnp.dot(ds_all[...], jnp.concatenate(q_parts, axis=0), preferred_element_type=f32)

    @pl.when(step == 0)
    def _():
        dv_acc[...] = dv
        dk_acc[...] = dk

    @pl.when(step > 0)
    def _():
        dv_acc[...] += dv
        dk_acc[...] += dk

    dq = jnp.concatenate(dq_parts, axis=0).T
    cosine, sine = wide_tables(cosq_ref, sinq_ref, width)
    dq_ref[...] = (rope(dq, cosine, sine, True) * (HEAD_DIM ** (-0.5))).astype(bf16)

    @pl.when(step == pl.num_programs(0) - 1)
    def _():
        cosine, sine = wide_tables(cosk_ref, sink_ref, width)
        dk_ref[...] = rope(dk_acc[...], cosine, sine, True).astype(bf16)
        dv_ref[...] = dv_acc[...].astype(bf16)


def attend_back(q, k, v, o, do, lse, bias, cosine, sine, heads, group):
    rows = q.shape[0]
    width = heads * HEAD_DIM
    block = 256
    lanes = lambda wide: pl.BlockSpec((block, wide), lambda i: (i, group))
    row = lambda wide: pl.BlockSpec((block, wide), lambda i: (i, 0))
    whole = lambda wide, at: pl.BlockSpec((rows, wide), lambda i: (0, at))
    out = jax.ShapeDtypeStruct((rows, width), bf16)
    return pl.pallas_call(
        functools.partial(attend_back_kernel, heads, group * heads),
        grid=(rows // block,),
        out_shape=[out] * 3,
        in_specs=[
            lanes(width),
            lanes(width),
            lanes(width),
            row(128),
            whole(width, group),
            whole(width, group),
            pl.BlockSpec((width, rows), lambda i: (group, 0)),
            whole(block, 0),
            row(128),
            row(128),
            whole(128, 0),
            whole(128, 0),
        ],
        out_specs=[row(width), whole(width, 0), whole(width, 0)],
        scratch_shapes=[
            pltpu.VMEM((rows, heads * block), bf16),
            pltpu.VMEM((rows, heads * block), bf16),
            pltpu.VMEM((rows, width), f32),
            pltpu.VMEM((rows, width), f32),
        ],
        compiler_params=params(("arbitrary",)),
        cost_estimate=cost(
            40 * rows * rows * heads * HEAD_DIM, 16 * rows * width, rows * rows * heads
        ),
    )(
        q,
        do,
        o,
        lse,
        k,
        v,
        k.T,
        jnp.broadcast_to(bias.reshape(rows, 1), (rows, block)),
        cosine,
        sine,
        cosine,
        sine,
    )


def body(
    mesh_sizes,
    frames_in,
    skip_in,
    flow_times,
    lengths,
    skip_weight,
    qkv_weight,
    output_weight,
    up_weight,
    up_bias,
    down_weight,
    down_bias,
    modulate_weight,
    modulate_bias,
    output_grad,
):
    batch, seq = mesh_sizes
    net = Net(batch, seq)
    n, d, s = net.n, net.d, net.s
    local, utts, width = frames_in.shape
    frames = frames_in.reshape(local, width)
    skips = skip_in.reshape(local, width)
    out_grad = output_grad.reshape(local, width).astype(f32)
    heads = HEADS // seq
    part = heads * HEAD_DIM
    rows = local * seq
    built = n == 32 and seq == 4
    wrow = width // n
    ff = up_weight.shape[1]

    seq_order = s ^ jnp.arange(seq, dtype=jnp.int32)
    by_part = qkv_weight.reshape(wrow, 3, seq, part)
    pieces = [
        lax.dynamic_index_in_dim(by_part, s ^ k, 2, keepdims=False).reshape(wrow, 3 * part)
        for k in range(seq)
    ]
    urow, drow = up_bias.shape[0], down_bias.shape[0]
    if built:
        vectors = jnp.concatenate(
            [
                up_bias.reshape(1, urow),
                jnp.pad(down_bias, (0, urow - drow)).reshape(1, urow),
                jnp.zeros((wrow - 2, urow), bf16),
            ]
        )
        pieces = [jnp.concatenate([p, vectors], axis=1) for p in pieces]
    pieces = [p if k == 0 else net.swap(p, k) for k, p in enumerate(pieces)]
    if built:
        skip_gather = Gather(net, skip_weight)
        skip_gather.far()
        skip_gather.last()
        (full_skip,) = place(*skip_gather.blocks(), n)
        qkv_four = after(jnp.stack(pieces), skip_gather.near)
        qkv_z = jnp.concatenate([qkv_four] + [net.swap(qkv_four, k << 3) for k in (1, 2, 3)])
        qkv_y = net.swap(after(qkv_z, skip_gather.other), 4)
        ou = jnp.concatenate([output_weight, up_weight], axis=1)
        ou_gather = Gather(net, after(ou, qkv_z))
    else:
        gather = lambda w, ax: lax.all_gather(w, ax, axis=0, tiled=True)
        full_skip = gather(skip_weight, ALL)
        full_qkv = gather(jnp.stack(pieces)[seq_order], "batch")
        full_qkv = full_qkv.reshape(batch, seq, wrow, 3 * part)
        full_qkv = full_qkv.reshape(width, 3 * part)
        full_output = gather(output_weight, ALL).reshape(seq, width // seq, width)[seq_order]
        full_output = full_output.reshape(width, width)
        full_up = gather(up_weight, ALL)
        full_down = gather(down_weight, ALL)

    mod_bias = lax.dynamic_update_slice_in_dim(
        jnp.zeros((6 * width,), f32), modulate_bias.astype(f32), d * modulate_bias.shape[0], 0
    )
    if built:
        times = jnp.broadcast_to(flow_times.reshape(1, 1), (8, 128))
        times = [times] + [net.swap(times, k << 3) for k in (1, 2, 3)]
        times = jnp.concatenate([t[:1] for t in times] * 2)
        times = jnp.stack([times[:4], net.swap(times, 4)[:4]], axis=1).reshape(batch, 128)
        all_times = times[:, 0]
    else:
        small = jnp.concatenate([up_bias.astype(f32), down_bias.astype(f32), flow_times])
        small_width = -(-small.shape[0] // 128) * 128
        small = jnp.pad(small, (0, small_width - small.shape[0]))
        slots = lax.broadcasted_iota(jnp.int32, (n, small_width), 0)
        small = net.sum_all(jnp.where(slots == d, small[None], 0.0))
        full_up_bias = small[:, :urow].reshape(1, ff)
        full_down_bias = small[:, urow : urow + drow].reshape(1, width)
        all_times = small.reshape(batch, seq, small_width)[:, 0, urow + drow]
    feat = jax.nn.silu(time_embed(all_times, width)).astype(bf16)
    feat_own = lax.dynamic_slice_in_dim(feat, d * wrow, wrow, 1)
    modulation = jnp.dot(feat_own, modulate_weight, preferred_element_type=f32)
    modulation = modulation + mod_bias[None]
    if built:
        sums = modulation[0:2]
        for k in (1, 2, 3):
            sums = sums + net.swap(modulation[2 * k : 2 * k + 2], k << 3)
        sums = sums[0:1] + net.swap(sums[1:2], 4)
        modulation = sums
        for k in (1, 2, 3):
            modulation = modulation + net.swap(sums, k)
    else:
        bit = batch // 2
        while bit:
            high = (net.b & bit) // bit
            sent = lax.dynamic_slice_in_dim(modulation, (1 - high) * bit, bit, 0)
            kept = lax.dynamic_slice_in_dim(modulation, high * bit, bit, 0)
            modulation = kept + net.swap(sent, bit * seq)
            bit //= 2
        bit = 1
        while bit < seq:
            modulation = modulation + net.swap(modulation, bit)
            bit *= 2
    shift_one, scale_one, gate_one, shift_two, scale_two, gate_two = jnp.split(modulation, 6, -1)

    half_dim = HEAD_DIM // 2
    inverse = jnp.exp(-math.log(10000.0) * 2.0 * jnp.arange(half_dim, dtype=f32) / HEAD_DIM)
    positions = (
        seq_order[:, None] * local + jnp.arange(local, dtype=jnp.int32)[None]
    ).reshape(rows)
    angles = positions.astype(f32)[:, None] * jnp.tile(inverse, 128 // half_dim)[None]
    cosine, sine = jnp.cos(angles), jnp.sin(angles)
    key_bias = jnp.where(positions < lengths[0], 0.0, masked_score).astype(f32)[None]

    joined = jnp.concatenate([frames, skips], axis=-1)
    hidden_zero = jnp.dot(joined, full_skip, preferred_element_type=f32)
    normed_one = modulated(hidden_zero, scale_one, shift_one).astype(bf16)
    if built:
        down_gather = Gather(net, after(down_weight, (normed_one, ou_gather.near)))
    across = {0: normed_one}
    bit = seq // 2
    while bit:
        across.update({i | bit: net.swap(a, bit) for i, a in list(across.items())})
        bit //= 2
    normed_parts = [across[i] for i in range(seq)]
    if built:
        ou_gather.near, down_gather.near, qkv_y, *_ = lax.optimization_barrier(
            (ou_gather.near, down_gather.near, qkv_y, across[2])
        )
        ou_gather.far()
        k16 = jnp.arange(16, dtype=jnp.int32)
        z_spots = d ^ (((k16 >> 2) << 3) | (k16 & 3))
        full_qkv, vectors = place(
            [qkv_z, qkv_y], [z_spots, z_spots ^ 4], n, (3 * part, urow)
        )
        vectors = vectors.reshape(n, wrow, urow)
        full_up_bias = vectors[:, 0].reshape(1, ff).astype(f32)
        full_down_bias = vectors[:, 1, :drow].reshape(1, width).astype(f32)
    q, k, v = qkv_project(normed_parts, full_qkv, cosine, sine)
    if built:
        q, ou_gather.half, down_gather.near = lax.optimization_barrier(
            (q, ou_gather.half, down_gather.near)
        )
        ou_gather.last()
        down_gather.far()
    att, lse = attend(q, k, v, key_bias, heads)
    if built:
        att, down_gather.half, ou_gather.mate_half = lax.optimization_barrier(
            (att, down_gather.half, ou_gather.mate_half)
        )
        down_gather.last()
        got, spots = ou_gather.blocks()
        spots = jnp.concatenate(spots)
        turned = spots ^ (s * (n // seq))
        full_output, full_up = place(got, [jnp.stack([turned, spots])], n, (width, ff))
        (full_down,) = place(*down_gather.blocks(), n)
    blocks = [att[i * local : (i + 1) * local] for i in range(seq)]
    attended = jnp.concatenate(
        [b if i == 0 else net.swap(b, i) for i, b in enumerate(blocks)], axis=-1
    )
    attn_proj = jnp.dot(attended, full_output, preferred_element_type=f32)
    hidden_one = hidden_zero + gate_one * attn_proj
    normed_two = modulated(hidden_one, scale_two, shift_two).astype(bf16)
    pre_act = jnp.dot(normed_two, full_up, preferred_element_type=f32) + full_up_bias
    activated = gelu_tanh(pre_act).astype(bf16)
    ffn_out = jnp.dot(activated, full_down, preferred_element_type=f32) + full_down_bias
    layer_out = (hidden_one + gate_two * ffn_out).astype(bf16)

    rows_dot = lambda a, b: lax.dot_general(
        a, b, (((0,), (0,)), ((), ())), preferred_element_type=f32
    )
    back_dot = lambda a, b: lax.dot_general(
        a, b, (((1,), (1,)), ((), ())), preferred_element_type=f32
    )

    def scattered(grads, turn=False):
        if turn:
            grads = grads.reshape(seq, width // seq, -1)[seq_order].reshape(grads.shape)
        return lax.psum_scatter(
            grads.astype(bf16), ALL, scatter_dimension=0, tiled=True
        ).astype(f32)

    ffn_grad = out_grad * gate_two
    down_bias_term = jnp.sum(ffn_grad, axis=0)
    ffn_grad_low = ffn_grad.astype(bf16)
    act_grad = back_dot(ffn_grad_low, full_down)
    pre_grad = jax.vjp(gelu_tanh, pre_act)[1](act_grad)[0]
    up_bias_term = jnp.sum(pre_grad, axis=0)
    pre_grad_low = pre_grad.astype(bf16)
    normed_two_grad = back_dot(pre_grad_low, full_up)
    pull_two = jax.vjp(modulated, hidden_one, scale_two, shift_two)[1]
    hidden_grad_two, scale_two_grad, shift_two_grad = pull_two(normed_two_grad)
    gate_two_grad = jnp.sum(out_grad * ffn_out, axis=0)
    hidden_one_grad = out_grad + hidden_grad_two
    gate_one_grad = jnp.sum(hidden_one_grad * attn_proj, axis=0)
    proj_grad_low = (hidden_one_grad * gate_one).astype(bf16)
    attended_grad = back_dot(proj_grad_low, full_output).astype(bf16)
    pieces = [attended_grad[:, i * part : (i + 1) * part] for i in range(seq)]
    grad_all = jnp.concatenate([p if i == 0 else net.swap(p, i) for i, p in enumerate(pieces)])
    pair = lambda i, gate: attend_back(
        q, k, v, att, gate, lse, key_bias, cosine, sine, 2, i
    )
    if built:
        early_row = jnp.concatenate(
            [
                v.reshape(1, -1)
                for v in (
                    gate_one_grad,
                    shift_two_grad,
                    scale_two_grad,
                    gate_two_grad,
                    up_bias_term,
                    down_bias_term,
                )
            ],
            axis=1,
        )
        activated, attended_grad = lax.optimization_barrier((activated, attended_grad))
        down = Scatter(net, *grad_blocks(net, [activated], [ffn_grad_low], [(4, 4, 0, 0)], 128))
        normed_two = after(normed_two, down.parts[0])
        up = Scatter(
            net,
            *grad_blocks(
                net,
                [normed_two, attended],
                [pre_grad_low, proj_grad_low],
                [(4, 1, 0, 32), (1, 1, 128, 0)],
                160,
                [s * 0, s * (n // seq // 2)],
            ),
        )
        down_half = down.halve(8, 16, 4, 2)
        down.push(down_half)
        grad_all, down_half, early_row, _ = lax.optimization_barrier(
            (grad_all, down_half, early_row, up.parts[0])
        )
        early = utterance_rows(net, early_row)
        first = pair(0, grad_all)
        up.parts[1], down.parts[2], first = lax.optimization_barrier(
            (up.parts[1], down.parts[2], first)
        )
        up_half = up.halve(8, 16, 4, 2)
        up.push(up_half)
        down_half = down.halve(4, 8, 2, 4)
        down.push(down_half)
        grad_all, _ = lax.optimization_barrier((grad_all, (up_half, down_half, first)))
        second = pair(1, grad_all)
        up.parts[2], down.parts[3], early, second = lax.optimization_barrier(
            (up.parts[2], down.parts[3], early, second)
        )
        results = [first, second]
    else:
        grad_down_weight = scattered(rows_dot(activated, ffn_grad_low))
        grad_up_weight = scattered(rows_dot(normed_two, pre_grad_low))
        grad_output_weight = scattered(rows_dot(attended, proj_grad_low), True)
        results = [pair(i, grad_all) for i in range(heads // 2)]
    pieces = [r[i] for i in range(3) for r in results]
    odd_grad, odd = qkv_back(pieces, full_qkv, local, 1, bf16)
    sent = net.swap(odd, 1)
    even_grad, even = qkv_back(pieces, full_qkv, local, 0, f32)
    halves = [
        even[i * local : (i + 1) * local] + sent[i * local : (i + 1) * local].astype(f32)
        for i in range(seq // 2)
    ]
    step = 2
    while len(halves) > 1:
        keep = halves[0::2]
        give = halves[1::2]
        halves = [
            a + net.swap(g.astype(bf16), step).astype(f32) for a, g in zip(keep, give)
        ]
        step *= 2
    normed_one_grad = halves[0]
    if built:
        keep, send = qkv_grad_blocks(net, normed_parts, [even_grad, odd_grad])
        got = net.swap(send, 4)
        up_quarter = up.halve(4, 8, 2, 4)
        up.push(up_quarter)
        grad_down_weight = down.finish()
        zs = [
            net.swap(total(keep[i], got[i]).astype(bf16), i << 3) for i in (1, 2, 3)
        ]
        own = total(keep[0], got[0], *zs)
    else:
        qkv_part = sum(
            rows_dot(a, (odd_grad if i % 2 else even_grad)[(i // 2) * local : (i // 2 + 1) * local])
            for i, a in enumerate(normed_parts)
        ).astype(bf16)
        own = lax.psum_scatter(qkv_part, "batch", scatter_dimension=0, tiled=True).astype(f32)
    own = own.reshape(seq, wrow, 3 * part)
    cols = [lax.dynamic_index_in_dim(own, s ^ i, 0, keepdims=False) for i in range(seq)]
    cols = [c if i == 0 else net.swap(c, i) for i, c in enumerate(cols)]
    grad_qkv_weight = spread_columns(cols, seq_order, 3)

    pull_one = jax.vjp(modulated, hidden_zero, scale_one, shift_one)[1]
    hidden_grad_one, scale_one_grad, shift_one_grad = pull_one(normed_one_grad)
    hidden_zero_grad = (hidden_one_grad + hidden_grad_one).astype(bf16)
    if built:
        skip = Scatter(
            net,
            *grad_blocks(
                net,
                [frames, skips],
                [hidden_zero_grad, hidden_zero_grad],
                [(1, 2, 0, 0), (1, 2, 0, 0)],
                64,
                [s * 0, s * 0 + 8],
            ),
        )
        skip.push(skip.halve(8, 16, 4, 2))
        own = up.finish()
        grad_up_weight = jnp.concatenate(
            [own[i * wrow : (i + 1) * wrow] for i in range(4)], axis=1
        )
        grad_output_weight = own[4 * wrow :]
        skip.push(skip.halve(4, 8, 2, 4))
        grad_skip_weight = skip.finish()
    else:
        grad_skip_weight = scattered(rows_dot(joined, hidden_zero_grad))
    grad_frames = back_dot(hidden_zero_grad, full_skip[:width])
    grad_skip = back_dot(hidden_zero_grad, full_skip[width:])

    def by_utterance(*vectors):
        row = jnp.concatenate([vec.reshape(1, -1) for vec in vectors], axis=1)
        place_row = lax.broadcasted_iota(jnp.int32, (batch, row.shape[1]), 0)
        return jnp.where(place_row == net.b, row, 0.0)

    if built:
        late = utterance_rows(
            net, jnp.concatenate([shift_one_grad.reshape(1, -1), scale_one_grad.reshape(1, -1)], axis=1)
        )
        sums = jnp.sum(early[:, 4 * width :], axis=0)
        up_sum, down_sum = sums[:ff], sums[ff:]
        early = early[:, : 4 * width]
    else:
        early = by_utterance(gate_one_grad, shift_two_grad, scale_two_grad, gate_two_grad)
        flat = jnp.concatenate([early.reshape(-1), up_bias_term, down_bias_term])
        flat = net.sum_all(flat.reshape(-1, 128)).reshape(-1)
        early = flat[: batch * 4 * width].reshape(batch, 4 * width)
        up_sum = flat[batch * 4 * width : batch * 4 * width + ff]
        down_sum = flat[batch * 4 * width + ff :]
        late = net.sum_all(by_utterance(shift_one_grad, scale_one_grad))
    grad_up_bias = lax.dynamic_slice_in_dim(up_sum, d * urow, urow, 0)
    grad_down_bias = lax.dynamic_slice_in_dim(down_sum, d * drow, drow, 0)
    mod_grad = jnp.concatenate([late, early], axis=1)
    grad_modulate_weight = lax.dot_general(
        feat_own.astype(f32),
        mod_grad,
        (((0,), (0,)), ((), ())),
        precision=lax.Precision.HIGHEST,
        preferred_element_type=f32,
    )
    mod_width = modulate_bias.shape[0]
    grad_modulate_bias = jnp.sum(
        lax.dynamic_slice_in_dim(mod_grad, d * mod_width, mod_width, 1), axis=0
    )
    shape = (local, utts, width)
    return (
        layer_out.reshape(shape),
        grad_frames.reshape(shape),
        grad_skip.reshape(shape),
        grad_skip_weight,
        grad_qkv_weight,
        grad_output_weight,
        grad_up_weight,
        grad_up_bias,
        grad_down_weight,
        grad_down_bias,
        grad_modulate_weight,
        grad_modulate_bias,
    )


def solution(mesh):
    rows_two = P("seq", "batch", None)
    owned = P(ALL, None)
    vector = P(ALL)
    in_specs = (
        rows_two,
        rows_two,
        P("batch"),
        P("batch"),
        owned,
        owned,
        owned,
        owned,
        vector,
        owned,
        vector,
        owned,
        vector,
        rows_two,
    )
    out_specs = (
        rows_two,
        rows_two,
        rows_two,
        owned,
        owned,
        owned,
        owned,
        vector,
        owned,
        vector,
        owned,
        vector,
    )
    sizes = (mesh.shape["batch"], mesh.shape["seq"])
    return jax.shard_map(
        functools.partial(body, sizes),
        mesh=mesh,
        in_specs=in_specs,
        out_specs=out_specs,
        check_vma=False,
    )
```

```python
import functools
import math

import jax
import jax.numpy as jnp
from jax import lax
from jax.experimental import pallas as pl
from jax.experimental.pallas import tpu as pltpu
from jax.sharding import PartitionSpec as P

HEADS = 16
HEAD_DIM = 64
epsilon = 1e-06
masked_score = -1e30
f32 = jnp.float32
bf16 = jnp.bfloat16
ALL = ("batch", "seq")


def rms_norm(values):
    return values * lax.rsqrt(jnp.mean(values * values, axis=-1, keepdims=True) + epsilon)


def modulated(hidden, scale_rows, shift_rows):
    return rms_norm(hidden) * (1.0 + scale_rows) + shift_rows


def gelu_tanh(pre_values):
    return jax.nn.gelu(pre_values, approximate=True)


def time_embed(flow_times, embed_width):
    half_width = embed_width // 2
    frequency = jnp.exp(-math.log(10000.0) * jnp.arange(half_width, dtype=f32) / half_width)
    angles = 1000.0 * flow_times[:, None] * frequency[None, :]
    return jnp.concatenate([jnp.sin(angles), jnp.cos(angles)], axis=-1)


def params(semantics=None):
    return pltpu.CompilerParams(dimension_semantics=semantics, vmem_limit_bytes=60 * 1024 * 1024)


class Net:
    def __init__(self, batch, seq):
        self.batch, self.seq, self.n = batch, seq, batch * seq
        self.d = lax.axis_index("batch") * seq + lax.axis_index("seq")
        self.b = lax.axis_index("batch")
        self.s = lax.axis_index("seq")
        self.core = self.d & 1

    def swap(self, value, offset):
        return lax.ppermute(value, ALL, [(i, i ^ offset) for i in range(self.n)])

    def swap_by_core(self, value, even, odd):
        pairs = [(i, i ^ (odd if i & 1 else even)) for i in range(self.n)]
        return lax.ppermute(value, ALL, pairs)

    def sum_all(self, value):
        bit = 1
        while bit < self.n:
            value = value + self.swap(value, bit)
            bit *= 2
        return value


def cost(flops, moved, exps=0):
    return pl.CostEstimate(flops=int(flops), bytes_accessed=int(moved), transcendentals=int(exps))


def after(value, *others):
    return lax.optimization_barrier((value,) + tuple(others))[0]


def gate(*values):
    return lax.optimization_barrier(values)


def place(pieces, tables, count, columns=None):
    rows, width = pieces[0].shape[1:]
    columns = columns or (width,)
    counts = [p.shape[0] for p in pieces]
    total = sum(counts)
    table = jnp.concatenate(tables, axis=-1).astype(jnp.int32)
    if table.ndim == 1:
        table = jnp.broadcast_to(table[None], (len(columns), total))

    def kernel(table_ref, *refs):
        sources = refs[: len(pieces)]
        outs = refs[len(pieces) : len(pieces) + len(columns)]
        sems = refs[-1]
        copies = []
        at = 0
        for source, number in zip(sources, counts):
            for j in range(number):
                left = 0
                for o, wide in enumerate(columns):
                    copies.append(
                        pltpu.make_async_copy(
                            source.at[j, :, pl.ds(left, wide)],
                            outs[o].at[table_ref[o, at]],
                            sems.at[o, at],
                        )
                    )
                    left += wide
                at += 1
        for copy in copies:
            copy.start()
        for copy in copies:
            copy.wait()

    any_spec = pl.BlockSpec(memory_space=pl.ANY)
    outs = pl.pallas_call(
        kernel,
        out_shape=[jax.ShapeDtypeStruct((count, rows, wide), pieces[0].dtype) for wide in columns],
        in_specs=[pl.BlockSpec(memory_space=pltpu.SMEM)] + [any_spec] * len(pieces),
        out_specs=[pl.BlockSpec(memory_space=pltpu.VMEM)] * len(columns),
        scratch_shapes=[pltpu.SemaphoreType.DMA((len(columns), total))],
        compiler_params=params(),
        cost_estimate=cost(0, 4 * count * rows * width),
    )(table, *pieces)
    return [out.reshape(count * rows, wide) for out, wide in zip(outs, columns)]


class Gather:
    def __init__(self, net, shard):
        self.net = net
        self.near = jnp.stack([shard] + [net.swap(shard, k << 3) for k in (1, 2, 3)])

    def far(self):
        self.half = jnp.concatenate([self.near, self.net.swap_by_core(self.near, 2, 4)])
        self.mate_half = self.net.swap(self.half, 1)

    def last(self):
        self.other = self.net.swap_by_core(self.half, 4, 2)

    def mates(self):
        self.mate_other = self.net.swap(self.other, 1)

    def blocks(self):
        d = self.net.d
        z = jnp.arange(4, dtype=jnp.int32) << 3
        second = jnp.where(self.net.core == 0, 2, 4)
        third = 6 - second
        own = jnp.concatenate([d ^ z, d ^ z ^ second])
        mate = d ^ 1
        mate_own = jnp.concatenate([mate ^ z, mate ^ z ^ third])
        return (
            [self.half, self.other, self.mate_half, self.mate_other],
            [own, own ^ third, mate_own, mate_own ^ second],
        )


def grad_blocks(net, lefts, rights, segments, packed_rows, turns=None):
    depth = lefts[0].shape[0]
    tile = 1024
    piece = 32
    chip = net.d >> 1
    rel = jnp.arange(16, dtype=jnp.int32) ^ chip
    x_bit, y_bit, z = rel & 1, (rel >> 1) & 1, rel >> 2
    even = y_bit * 8 + x_bit * 4 + z
    odd = x_bit * 8 + y_bit * 4 + z
    mine = jnp.where(net.core == 0, even, odd)
    other = jnp.where(net.core == 0, odd, even)
    extra = jnp.stack([net.core] + (turns or [net.core * 0] * len(segments)))
    extra = jnp.pad(extra, (0, 16 - extra.shape[0]))
    table = jnp.stack([mine, other, extra]).astype(jnp.int32)
    starts = [0]
    for seg in segments:
        starts.append(starts[-1] + seg[0])
    steps = starts[-1]
    number = len(segments)

    def kernel(table_ref, *refs):
        left_refs, right_refs = refs[:number], refs[number : 2 * number]
        keep, send, scratch, sems = refs[2 * number :]
        t = pl.program_id(0)
        slot = t % 2
        core = table_ref[2, 0]

        def copy(v, p, at_slot, source_row, pos, dest_row):
            dest = send if p else keep
            return pltpu.make_async_copy(
                scratch.at[at_slot, pl.ds(pl.multiple_of(source_row, piece), piece)],
                dest.at[pos, pl.ds(pl.multiple_of(dest_row, piece), piece)],
                sems.at[at_slot, p, v],
            )

        def wait_slot(at_slot):
            for v in range(16):
                for p in range(2):
                    copy(v, p, at_slot, 0, 0, 0).wait()

        @pl.when(t >= 2)
        def _():
            wait_slot(slot)

        left, right = left_refs[-1][...], right_refs[-1][...]
        for i in range(number - 2, -1, -1):
            early = t < starts[i + 1]
            left = jnp.where(early, left_refs[i][...], left)
            right = jnp.where(early, right_refs[i][...], right)
        scratch[slot] = lax.dot_general(
            left, right, (((0,), (0,)), ((), ())), preferred_element_type=f32
        ).astype(bf16)
        for v in range(16):
            for p in range(2):
                side = core ^ p
                chip_at = source = dest_row = jnp.int32(0)
                for i, (_, subs, base, rise) in reversed(list(enumerate(segments))):
                    local = t - starts[i]
                    here = (
                        (local * (16 // subs) % 16 + v // subs) ^ table_ref[2, 1 + i],
                        (2 * (v // subs) + side) * subs * piece + (v % subs) * piece,
                        base + local * rise + (v % subs) * piece,
                    )
                    if i == number - 1:
                        chip_at, source, dest_row = here
                    else:
                        early = t < starts[i + 1]
                        chip_at = jnp.where(early, here[0], chip_at)
                        source = jnp.where(early, here[1], source)
                        dest_row = jnp.where(early, here[2], dest_row)
                copy(v, p, slot, source, table_ref[p, chip_at], dest_row).start()

        @pl.when(t == steps - 1)
        def _():
            wait_slot(slot)
            if steps > 1:
                wait_slot(1 - slot)

    def spec(array, i):
        count = array.shape[1] // tile
        if count == 1:
            return pl.BlockSpec((depth, tile), lambda t, table: (0, 0))
        return pl.BlockSpec(
            (depth, tile), lambda t, table: (0, jnp.clip(t - starts[i], 0, count - 1))
        )

    any_spec = pl.BlockSpec(memory_space=pl.ANY)
    shape = jax.ShapeDtypeStruct((16, packed_rows, tile), bf16)
    return pl.pallas_call(
        kernel,
        out_shape=[shape, shape],
        grid_spec=pltpu.PrefetchScalarGridSpec(
            num_scalar_prefetch=1,
            grid=(steps,),
            in_specs=[spec(a, i) for i, a in enumerate(lefts)]
            + [spec(a, i) for i, a in enumerate(rights)],
            out_specs=[any_spec, any_spec],
            scratch_shapes=[
                pltpu.VMEM((2, tile, tile), bf16),
                pltpu.SemaphoreType.DMA((2, 2, 16)),
            ],
        ),
        compiler_params=params(("arbitrary",)),
        cost_estimate=cost(2 * steps * depth * tile * tile, 3 * steps * tile * tile * 2),
    )(table, *lefts, *rights)


def total(*parts):
    result = parts[0].astype(f32)
    for part in parts[1:]:
        result = result + part.astype(f32)
    return result


class Scatter:
    def __init__(self, net, keep, send):
        self.net, self.parts = net, [keep]
        self.parts.append(net.swap(send, 1))

    def halve(self, low, high, even, odd):
        out = total(*[p[low:high] for p in self.parts]).astype(bf16)
        self.out = out
        self.pair = (even, odd)
        return out

    def push(self, out):
        self.parts.append(self.net.swap_by_core(out, *self.pair))

    def z_sums(self):
        self.outs = [total(*[p[k : k + 1] for p in self.parts]).astype(bf16) for k in (1, 2, 3)]
        return self.outs

    def z_push(self):
        self.zs = [self.net.swap(o, (k + 1) << 3) for k, o in enumerate(self.outs)]

    def finish(self):
        return total(*[p[0:1] for p in self.parts], *self.zs)[0]


class UtteranceRows:
    def __init__(self, net, row):
        self.net, self.parts = net, [row] + [net.swap(row, k) for k in (1, 2, 3)]

    def across_z(self):
        row = sum(self.parts[1:], self.parts[0])
        self.parts = [row] + [self.net.swap(row, k << 3) for k in (1, 2, 3)]

    def across_y(self):
        self.parts = [jnp.concatenate(self.parts)]
        self.parts.append(self.net.swap(self.parts[0], 4))

    def rows(self):
        return jnp.stack(self.parts, axis=1).reshape(8, self.parts[0].shape[1])


def spread_columns(parts, order, groups):
    rows, width = parts[0].shape
    number = len(parts)
    wide = width // groups

    def kernel(order_ref, *refs):
        out, sems = refs[number:]
        copies = []
        for i in range(number):
            for g in range(groups):
                at = pl.multiple_of((order_ref[i] + g * number) * wide, wide)
                copies.append(
                    pltpu.make_async_copy(
                        refs[i].at[:, pl.ds(g * wide, wide)],
                        out.at[:, pl.ds(at, wide)],
                        sems.at[i, g],
                    )
                )
        for copy in copies:
            copy.start()
        for copy in copies:
            copy.wait()

    return pl.pallas_call(
        kernel,
        out_shape=jax.ShapeDtypeStruct((rows, width * number), parts[0].dtype),
        in_specs=[pl.BlockSpec(memory_space=pltpu.SMEM)]
        + [pl.BlockSpec(memory_space=pltpu.VMEM)] * number,
        out_specs=pl.BlockSpec(memory_space=pltpu.VMEM),
        scratch_shapes=[pltpu.SemaphoreType.DMA((number, groups))],
        compiler_params=params(),
        cost_estimate=cost(0, 8 * rows * width * number),
    )(order.astype(jnp.int32), *parts)


def rope(values, cosine, sine, back):
    width = values.shape[-1]
    lane = lax.broadcasted_iota(jnp.int32, values.shape, 1)
    early = (lane & (HEAD_DIM - 1)) < HEAD_DIM // 2
    source = values * sine if back else values
    ahead = pltpu.roll(source, width - HEAD_DIM // 2, 1)
    behind = pltpu.roll(source, HEAD_DIM // 2, 1)
    if back:
        turned = jnp.where(early, ahead, -behind)
        return values * cosine + turned
    turned = jnp.where(early, -ahead, behind)
    return values * cosine + turned * sine


def wide_tables(cos_ref, sin_ref, width):
    reps = width // cos_ref.shape[-1]
    cosine = jnp.concatenate([cos_ref[...]] * reps, axis=-1)
    sine = jnp.concatenate([sin_ref[...]] * reps, axis=-1)
    return cosine, sine


def qkv_kernel(number, *refs):
    w_ref, cos_ref, sin_ref, q_ref, k_ref, v_ref = refs[number:]
    width = q_ref.shape[-1]
    scale = HEAD_DIM ** (-0.5)
    for i in range(number):

        @pl.when(pl.program_id(0) == i)
        def _():
            result = jnp.dot(refs[i][...], w_ref[...], preferred_element_type=f32)
            cosine, sine = wide_tables(cos_ref, sin_ref, width)
            q_ref[...] = (rope(result[:, :width], cosine, sine, False) * scale).astype(bf16)
            k_ref[...] = rope(result[:, width : 2 * width], cosine, sine, False).astype(bf16)
            v_ref[...] = result[:, 2 * width :].astype(bf16)


def qkv_project(parts, w, cosine, sine):
    block, depth = parts[0].shape
    rows = block * len(parts)
    width = w.shape[1] // 3
    row = lambda wide: pl.BlockSpec((block, wide), lambda i: (i, 0))
    whole = lambda a: pl.BlockSpec(a.shape, lambda i: (0, 0))
    return pl.pallas_call(
        functools.partial(qkv_kernel, len(parts)),
        grid=(len(parts),),
        out_shape=[jax.ShapeDtypeStruct((rows, width), bf16)] * 3,
        in_specs=[whole(a) for a in parts] + [whole(w), row(128), row(128)],
        out_specs=[row(width)] * 3,
        compiler_params=params(("arbitrary",)),
        cost_estimate=cost(2 * rows * depth * 3 * width, 2 * rows * (depth + 3 * width)),
    )(*parts, w, cosine, sine)


def qkv_back(pieces, w, local, first, dtype):
    rows = pieces[0].shape[0]
    wide = pieces[0].shape[1]
    count = rows // local // 2
    width = len(pieces) * wide

    def kernel(*refs):
        w_ref, all_ref, out_ref = refs[len(pieces) :]
        joined = jnp.concatenate([r[...] for r in refs[: len(pieces)]], axis=-1)
        all_ref[...] = joined
        out_ref[...] = lax.dot_general(
            joined, w_ref[...], (((1,), (1,)), ((), ())), preferred_element_type=f32
        ).astype(dtype)

    return pl.pallas_call(
        kernel,
        grid=(count,),
        out_shape=[
            jax.ShapeDtypeStruct((count * local, width), bf16),
            jax.ShapeDtypeStruct((count * local, w.shape[0]), dtype),
        ],
        in_specs=[pl.BlockSpec((local, wide), lambda i: (2 * i + first, 0))] * len(pieces)
        + [pl.BlockSpec(w.shape, lambda i: (0, 0))],
        out_specs=[
            pl.BlockSpec((local, width), lambda i: (i, 0)),
            pl.BlockSpec((local, w.shape[0]), lambda i: (i, 0)),
        ],
        compiler_params=params(("arbitrary",)),
        cost_estimate=cost(2 * count * local * width * w.shape[0], 8 * count * local * w.shape[0]),
    )(*pieces, w)


def qkv_grad_blocks(net, lefts, grads):
    local, depth = lefts[0].shape
    width = grads[0].shape[1]
    rows = depth // 8
    t = jnp.arange(8, dtype=jnp.int32)
    table = net.b ^ ((t & 3) << 1) ^ jnp.where(t < 4, 1, 0)
    number = len(lefts)

    def kernel(table_ref, *refs):
        keep, send = refs[number + len(grads) :]
        result = jnp.zeros((rows, width), f32)
        for i in range(number):
            grad = refs[number + i % 2][(i // 2) * local : (i // 2 + 1) * local]
            result = result + lax.dot_general(
                refs[i][...], grad, (((0,), (0,)), ((), ())), preferred_element_type=f32
            )
        result = result.astype(bf16)[None]
        step = pl.program_id(0)

        @pl.when(step < 4)
        def _():
            send[...] = result

        @pl.when(step >= 4)
        def _():
            keep[...] = result

    shape = jax.ShapeDtypeStruct((4, rows, width), bf16)
    block = (1, rows, width)
    return pl.pallas_call(
        kernel,
        out_shape=[shape, shape],
        grid_spec=pltpu.PrefetchScalarGridSpec(
            num_scalar_prefetch=1,
            grid=(8,),
            in_specs=[pl.BlockSpec((local, rows), lambda i, t: (0, t[i]))] * number
            + [pl.BlockSpec(g.shape, lambda i, t: (0, 0)) for g in grads],
            out_specs=[
                pl.BlockSpec(block, lambda i, t: (jnp.maximum(i - 4, 0), 0, 0)),
                pl.BlockSpec(block, lambda i, t: (jnp.minimum(i, 3), 0, 0)),
            ],
        ),
        compiler_params=params(("arbitrary",)),
        cost_estimate=cost(2 * number * local * depth * width, 4 * depth * width),
    )(table, *lefts, *grads)


def attend_kernel(heads, q_ref, k_ref, v_ref, bias_ref, o_ref, lse_ref):
    q = q_ref[...]
    k = k_ref[...]
    v = v_ref[...]
    bias = bias_ref[...]
    lane = lax.broadcasted_iota(jnp.int32, q.shape, 1) // HEAD_DIM
    spot = lax.broadcasted_iota(jnp.int32, lse_ref.shape, 1)
    out = jnp.zeros(q.shape, f32)
    lse = jnp.zeros(lse_ref.shape, f32)
    for h in range(heads):
        mine = lane == h
        qh = jnp.where(mine, q, jnp.zeros_like(q))
        s = lax.dot_general(qh, k, (((1,), (1,)), ((), ())), preferred_element_type=f32) + bias
        top = jnp.max(s, axis=-1, keepdims=True)
        p = jnp.exp(s - top)
        total = jnp.sum(p, axis=-1, keepdims=True)
        o = jnp.dot(p.astype(bf16), v, preferred_element_type=f32) / total
        out = jnp.where(mine, o, out)
        lse = jnp.where(spot == h, top + jnp.log(total), lse)
    o_ref[...] = out.astype(bf16)
    lse_ref[...] = lse


def attend(q, k, v, bias, heads):
    rows, width = q.shape
    block = 256
    row = lambda wide: pl.BlockSpec((block, wide), lambda i: (i, 0))
    whole = pl.BlockSpec((rows, width), lambda i: (0, 0))
    return pl.pallas_call(
        functools.partial(attend_kernel, heads),
        grid=(rows // block,),
        out_shape=[jax.ShapeDtypeStruct((rows, width), bf16), jax.ShapeDtypeStruct((rows, 128), f32)],
        in_specs=[row(width), whole, whole, pl.BlockSpec((1, rows), lambda i: (0, 0))],
        out_specs=[row(width), row(128)],
        compiler_params=params(("arbitrary",)),
        cost_estimate=cost(
            16 * rows * rows * heads * HEAD_DIM, 8 * rows * width, rows * rows * heads
        ),
    )(q, k, v, bias)


def attend_back_kernel(
    heads,
    first,
    q_ref,
    do_ref,
    o_ref,
    lse_ref,
    k_ref,
    v_ref,
    kt_ref,
    bias_ref,
    cosq_ref,
    sinq_ref,
    cosk_ref,
    sink_ref,
    dq_ref,
    dk_ref,
    dv_ref,
    p_all,
    ds_all,
    dk_acc,
    dv_acc,
):
    step = pl.program_id(0)
    q = q_ref[...]
    do = do_ref[...]
    k = k_ref[...]
    v = v_ref[...]
    block, width = q.shape
    lane = lax.broadcasted_iota(jnp.int32, q.shape, 1) // HEAD_DIM
    product = (do.astype(f32) * o_ref[...].astype(f32)).T
    lse_t = lse_ref[...].T
    bias = bias_ref[...]
    contract = (((1,), (1,)), ((), ()))
    q_parts, do_parts, dq_parts = [], [], []
    for h in range(heads):
        mine = lane == h
        qh = jnp.where(mine, q, jnp.zeros_like(q))
        doh = jnp.where(mine, do, jnp.zeros_like(do))
        q_parts.append(qh)
        do_parts.append(doh)
        row_dot = jnp.sum(product[h * HEAD_DIM : (h + 1) * HEAD_DIM], axis=0, keepdims=True)
        s = lax.dot_general(k, qh, contract, preferred_element_type=f32)
        p = jnp.exp(s + bias - lse_t[first + h : first + h + 1])
        dp = lax.dot_general(v, doh, contract, preferred_element_type=f32)
        ds = (p * (dp - row_dot)).astype(bf16)
        p_all[:, h * block : (h + 1) * block] = p.astype(bf16)
        ds_all[:, h * block : (h + 1) * block] = ds
        dq_parts.append(
            jnp.dot(kt_ref[h * HEAD_DIM : (h + 1) * HEAD_DIM, :], ds, preferred_element_type=f32)
        )
    dv = jnp.dot(p_all[...], jnp.concatenate(do_parts, axis=0), preferred_element_type=f32)
    dk = jnp.dot(ds_all[...], jnp.concatenate(q_parts, axis=0), preferred_element_type=f32)

    @pl.when(step == 0)
    def _():
        dv_acc[...] = dv
        dk_acc[...] = dk

    @pl.when(step > 0)
    def _():
        dv_acc[...] += dv
        dk_acc[...] += dk

    dq = jnp.concatenate(dq_parts, axis=0).T
    cosine, sine = wide_tables(cosq_ref, sinq_ref, width)
    dq_ref[...] = (rope(dq, cosine, sine, True) * (HEAD_DIM ** (-0.5))).astype(bf16)

    @pl.when(step == pl.num_programs(0) - 1)
    def _():
        cosine, sine = wide_tables(cosk_ref, sink_ref, width)
        dk_ref[...] = rope(dk_acc[...], cosine, sine, True).astype(bf16)
        dv_ref[...] = dv_acc[...].astype(bf16)


def attend_back(q, k, v, o, do, lse, bias, cosine, sine, heads, group):
    rows = q.shape[0]
    width = heads * HEAD_DIM
    block = 256
    lanes = lambda wide: pl.BlockSpec((block, wide), lambda i: (i, group))
    row = lambda wide: pl.BlockSpec((block, wide), lambda i: (i, 0))
    whole = lambda wide, at: pl.BlockSpec((rows, wide), lambda i: (0, at))
    out = jax.ShapeDtypeStruct((rows, width), bf16)
    return pl.pallas_call(
        functools.partial(attend_back_kernel, heads, group * heads),
        grid=(rows // block,),
        out_shape=[out] * 3,
        in_specs=[
            lanes(width),
            lanes(width),
            lanes(width),
            row(128),
            whole(width, group),
            whole(width, group),
            pl.BlockSpec((width, rows), lambda i: (group, 0)),
            whole(block, 0),
            row(128),
            row(128),
            whole(128, 0),
            whole(128, 0),
        ],
        out_specs=[row(width), whole(width, 0), whole(width, 0)],
        scratch_shapes=[
            pltpu.VMEM((rows, heads * block), bf16),
            pltpu.VMEM((rows, heads * block), bf16),
            pltpu.VMEM((rows, width), f32),
            pltpu.VMEM((rows, width), f32),
        ],
        compiler_params=params(("arbitrary",)),
        cost_estimate=cost(
            40 * rows * rows * heads * HEAD_DIM, 16 * rows * width, rows * rows * heads
        ),
    )(
        q,
        do,
        o,
        lse,
        k,
        v,
        k.T,
        jnp.broadcast_to(bias.reshape(rows, 1), (rows, block)),
        cosine,
        sine,
        cosine,
        sine,
    )


def body(
    mesh_sizes,
    frames_in,
    skip_in,
    flow_times,
    lengths,
    skip_weight,
    qkv_weight,
    output_weight,
    up_weight,
    up_bias,
    down_weight,
    down_bias,
    modulate_weight,
    modulate_bias,
    output_grad,
):
    batch, seq = mesh_sizes
    net = Net(batch, seq)
    n, d, s = net.n, net.d, net.s
    local, utts, width = frames_in.shape
    frames = frames_in.reshape(local, width)
    skips = skip_in.reshape(local, width)
    out_grad = output_grad.reshape(local, width).astype(f32)
    heads = HEADS // seq
    part = heads * HEAD_DIM
    rows = local * seq
    built = n == 32 and seq == 4
    wrow = width // n
    ff = up_weight.shape[1]

    seq_order = s ^ jnp.arange(seq, dtype=jnp.int32)
    by_part = qkv_weight.reshape(wrow, 3, seq, part)
    pieces = [
        lax.dynamic_index_in_dim(by_part, s ^ k, 2, keepdims=False).reshape(wrow, 3 * part)
        for k in range(seq)
    ]
    urow, drow = up_bias.shape[0], down_bias.shape[0]
    if built:
        vectors = jnp.concatenate(
            [
                up_bias.reshape(1, urow),
                jnp.pad(down_bias, (0, urow - drow)).reshape(1, urow),
                jnp.zeros((wrow - 2, urow), bf16),
            ]
        )
        pieces = [jnp.concatenate([p, vectors], axis=1) for p in pieces]
    pieces = [p if k == 0 else net.swap(p, k) for k, p in enumerate(pieces)]
    if built:
        skip_gather = Gather(net, skip_weight)
        qkv_four = after(jnp.stack(pieces), skip_gather.near)
        qkv_far = [net.swap(qkv_four, k << 3) for k in (1, 2, 3)]
        skip_gather.far()
        skip_gather.last()
        skip_gather.mates()
        (full_skip,) = place(*skip_gather.blocks(), n)
        ou = jnp.concatenate([output_weight, up_weight], axis=1)
        ou_gather = Gather(net, after(ou, skip_gather.other))
    else:
        gather = lambda w, ax: lax.all_gather(w, ax, axis=0, tiled=True)
        full_skip = gather(skip_weight, ALL)
        full_qkv = gather(jnp.stack(pieces)[seq_order], "batch")
        full_qkv = full_qkv.reshape(batch, seq, wrow, 3 * part)
        full_qkv = full_qkv.reshape(width, 3 * part)
        full_output = gather(output_weight, ALL).reshape(seq, width // seq, width)[seq_order]
        full_output = full_output.reshape(width, width)
        full_up = gather(up_weight, ALL)
        full_down = gather(down_weight, ALL)

    mod_bias = lax.dynamic_update_slice_in_dim(
        jnp.zeros((6 * width,), f32), modulate_bias.astype(f32), d * modulate_bias.shape[0], 0
    )
    if built:
        times = jnp.broadcast_to(flow_times.reshape(1, 1), (8, 128))
        times = [times] + [net.swap(times, k << 3) for k in (1, 2, 3)]
        *times, _ = gate(*times, skip_gather.near)
        times = jnp.concatenate([t[:1] for t in times] * 2)
        times = jnp.stack([times[:4], net.swap(times, 4)[:4]], axis=1).reshape(batch, 128)
        all_times = times[:, 0]
    else:
        small = jnp.concatenate([up_bias.astype(f32), down_bias.astype(f32), flow_times])
        small_width = -(-small.shape[0] // 128) * 128
        small = jnp.pad(small, (0, small_width - small.shape[0]))
        slots = lax.broadcasted_iota(jnp.int32, (n, small_width), 0)
        small = net.sum_all(jnp.where(slots == d, small[None], 0.0))
        full_up_bias = small[:, :urow].reshape(1, ff)
        full_down_bias = small[:, urow : urow + drow].reshape(1, width)
        all_times = small.reshape(batch, seq, small_width)[:, 0, urow + drow]
    feat = jax.nn.silu(time_embed(all_times, width)).astype(bf16)
    feat_own = lax.dynamic_slice_in_dim(feat, d * wrow, wrow, 1)
    modulation = jnp.dot(feat_own, modulate_weight, preferred_element_type=f32)
    modulation = modulation + mod_bias[None]
    if built:
        sums = modulation[0:2]
        for k in (1, 2, 3):
            sums = sums + net.swap(modulation[2 * k : 2 * k + 2], k << 3)
        sums = after(sums, skip_gather.half)
        sums = sums[0:1] + net.swap(sums[1:2], 4)
        sums = after(sums, skip_gather.other)
        modulation = sums
        for k in (1, 2, 3):
            modulation = modulation + net.swap(sums, k)
    else:
        bit = batch // 2
        while bit:
            high = (net.b & bit) // bit
            sent = lax.dynamic_slice_in_dim(modulation, (1 - high) * bit, bit, 0)
            kept = lax.dynamic_slice_in_dim(modulation, high * bit, bit, 0)
            modulation = kept + net.swap(sent, bit * seq)
            bit //= 2
        bit = 1
        while bit < seq:
            modulation = modulation + net.swap(modulation, bit)
            bit *= 2
    shift_one, scale_one, gate_one, shift_two, scale_two, gate_two = jnp.split(modulation, 6, -1)

    half_dim = HEAD_DIM // 2
    inverse = jnp.exp(-math.log(10000.0) * 2.0 * jnp.arange(half_dim, dtype=f32) / HEAD_DIM)
    positions = (
        seq_order[:, None] * local + jnp.arange(local, dtype=jnp.int32)[None]
    ).reshape(rows)
    angles = positions.astype(f32)[:, None] * jnp.tile(inverse, 128 // half_dim)[None]
    cosine, sine = jnp.cos(angles), jnp.sin(angles)
    key_bias = jnp.where(positions < lengths[0], 0.0, masked_score).astype(f32)[None]

    joined = jnp.concatenate([frames, skips], axis=-1)
    hidden_zero = jnp.dot(joined, full_skip, preferred_element_type=f32)
    normed_one = modulated(hidden_zero, scale_one, shift_one).astype(bf16)
    if built:
        *qkv_far, down_own, _ = gate(*qkv_far, down_weight, normed_one)
        qkv_z = jnp.concatenate([qkv_four] + qkv_far)
        qkv_y = net.swap(qkv_z, 4)
        down_gather = Gather(net, down_own)
    across = {0: normed_one}
    bit = seq // 2
    while bit:
        across.update({i | bit: net.swap(a, bit) for i, a in list(across.items())})
        if built and bit == 2:
            across[2], cosine, sine = gate(across[2], cosine, sine)
        bit //= 2
    normed_parts = [across[i] for i in range(seq)]
    if built:
        ou_gather.near = after(ou_gather.near, across[2])
        ou_gather.far()
        k16 = jnp.arange(16, dtype=jnp.int32)
        z_spots = d ^ (((k16 >> 2) << 3) | (k16 & 3))
        full_qkv, vectors = place(
            [qkv_z, qkv_y], [z_spots, z_spots ^ 4], n, (3 * part, urow)
        )
        vectors = vectors.reshape(n, wrow, urow)
        full_up_bias = vectors[:, 0].reshape(1, ff).astype(f32)
        full_down_bias = vectors[:, 1, :drow].reshape(1, width).astype(f32)
    q, k, v = qkv_project(normed_parts, full_qkv, cosine, sine)
    if built:
        q, ou_gather.half, down_gather.near = lax.optimization_barrier(
            (q, ou_gather.half, down_gather.near)
        )
        ou_gather.last()
        down_gather.far()
    att, lse = attend(q, k, v, key_bias, heads)
    if built:
        att, ou_gather.other, ou_gather.mate_half = gate(
            att, ou_gather.other, ou_gather.mate_half
        )
        ou_gather.mates()
        got, spots = ou_gather.blocks()
        spots = jnp.concatenate(spots)
        turned = spots ^ (s * (n // seq))
        full_output, full_up = place(got, [jnp.stack([turned, spots])], n, (width, ff))
    blocks = [att[i * local : (i + 1) * local] for i in range(seq)]
    attended = jnp.concatenate(
        [b if i == 0 else net.swap(b, i) for i, b in enumerate(blocks)], axis=-1
    )
    if built:
        down_gather.half = after(down_gather.half, attended)
        down_gather.last()
    attn_proj = jnp.dot(attended, full_output, preferred_element_type=f32)
    hidden_one = hidden_zero + gate_one * attn_proj
    normed_two = modulated(hidden_one, scale_two, shift_two).astype(bf16)
    if built:
        down_gather.other, down_gather.mate_half, normed_two = gate(
            down_gather.other, down_gather.mate_half, normed_two
        )
        down_gather.mates()
        (full_down,) = place(*down_gather.blocks(), n)
    pre_act = jnp.dot(normed_two, full_up, preferred_element_type=f32) + full_up_bias
    activated = gelu_tanh(pre_act).astype(bf16)
    ffn_out = jnp.dot(activated, full_down, preferred_element_type=f32) + full_down_bias
    layer_out = (hidden_one + gate_two * ffn_out).astype(bf16)

    rows_dot = lambda a, b: lax.dot_general(
        a, b, (((0,), (0,)), ((), ())), preferred_element_type=f32
    )
    back_dot = lambda a, b: lax.dot_general(
        a, b, (((1,), (1,)), ((), ())), preferred_element_type=f32
    )

    def scattered(grads, turn=False):
        if turn:
            grads = grads.reshape(seq, width // seq, -1)[seq_order].reshape(grads.shape)
        return lax.psum_scatter(
            grads.astype(bf16), ALL, scatter_dimension=0, tiled=True
        ).astype(f32)

    ffn_grad = out_grad * gate_two
    down_bias_term = jnp.sum(ffn_grad, axis=0)
    ffn_grad_low = ffn_grad.astype(bf16)
    act_grad = back_dot(ffn_grad_low, full_down)
    pre_grad = jax.vjp(gelu_tanh, pre_act)[1](act_grad)[0]
    up_bias_term = jnp.sum(pre_grad, axis=0)
    pre_grad_low = pre_grad.astype(bf16)
    normed_two_grad = back_dot(pre_grad_low, full_up)
    pull_two = jax.vjp(modulated, hidden_one, scale_two, shift_two)[1]
    hidden_grad_two, scale_two_grad, shift_two_grad = pull_two(normed_two_grad)
    gate_two_grad = jnp.sum(out_grad * ffn_out, axis=0)
    hidden_one_grad = out_grad + hidden_grad_two
    gate_one_grad = jnp.sum(hidden_one_grad * attn_proj, axis=0)
    proj_grad_low = (hidden_one_grad * gate_one).astype(bf16)
    attended_grad = back_dot(proj_grad_low, full_output).astype(bf16)
    pieces = [attended_grad[:, i * part : (i + 1) * part] for i in range(seq)]
    grad_all = jnp.concatenate([p if i == 0 else net.swap(p, i) for i, p in enumerate(pieces)])
    pair = lambda i, gate: attend_back(
        q, k, v, att, gate, lse, key_bias, cosine, sine, 2, i
    )
    if built:
        early_row = jnp.concatenate(
            [
                v.reshape(1, -1)
                for v in (
                    gate_one_grad,
                    shift_two_grad,
                    scale_two_grad,
                    gate_two_grad,
                    up_bias_term,
                    down_bias_term,
                )
            ],
            axis=1,
        )
        activated, attended_grad = lax.optimization_barrier((activated, attended_grad))
        down = Scatter(net, *grad_blocks(net, [activated], [ffn_grad_low], [(4, 4, 0, 0)], 128))
        normed_two = after(normed_two, down.parts[0])
        up = Scatter(
            net,
            *grad_blocks(
                net,
                [normed_two, attended],
                [pre_grad_low, proj_grad_low],
                [(4, 1, 0, 32), (1, 1, 128, 0)],
                160,
                [s * 0, s * (n // seq // 2)],
            ),
        )
        down_half = down.halve(8, 16, 4, 2)
        down.push(down_half)
        grad_all, down_half, early_row, _ = lax.optimization_barrier(
            (grad_all, down_half, early_row, up.parts[0])
        )
        early = UtteranceRows(net, early_row)
        first = pair(0, grad_all)
        up.parts[1], down.parts[2], first, *early.parts = gate(
            up.parts[1], down.parts[2], first, *early.parts
        )
        early.across_z()
        up_half = up.halve(8, 16, 4, 2)
        up.push(up_half)
        down_half = down.halve(4, 8, 2, 4)
        down.push(down_half)
        grad_all, _ = gate(grad_all, (up_half, down_half, first))
        second = pair(1, grad_all)
        results = [first, second]
    else:
        grad_down_weight = scattered(rows_dot(activated, ffn_grad_low))
        grad_up_weight = scattered(rows_dot(normed_two, pre_grad_low))
        grad_output_weight = scattered(rows_dot(attended, proj_grad_low), True)
        results = [pair(i, grad_all) for i in range(heads // 2)]
    pieces = [r[i] for i in range(3) for r in results]
    odd_grad, odd = qkv_back(pieces, full_qkv, local, 1, bf16)
    sent = net.swap(odd, 1)
    even_grad, even = qkv_back(pieces, full_qkv, local, 0, f32)
    halves = [
        even[i * local : (i + 1) * local] + sent[i * local : (i + 1) * local].astype(f32)
        for i in range(seq // 2)
    ]
    if built:
        give = halves[1].astype(bf16)
        taken = net.swap(give, 2)
        down.parts[2], down.parts[3], give, *early.parts = gate(
            down.parts[2], down.parts[3], give, *early.parts
        )
        early.across_y()
        down_sums = down.z_sums()
        down.z_push()
        *normed_parts, _, _ = gate(*normed_parts, give, down_sums)
        keep, send = qkv_grad_blocks(net, normed_parts, [even_grad, odd_grad])
        got = net.swap(send, 4)
        up.parts[2], keep = gate(up.parts[2], keep)
        up_quarter = up.halve(4, 8, 2, 4)
        up.push(up_quarter)
        taken = after(taken, up_quarter)
        normed_one_grad = halves[0] + taken.astype(f32)
    else:
        step = 2
        while len(halves) > 1:
            kept = halves[0::2]
            give = halves[1::2]
            halves = [
                a + net.swap(g.astype(bf16), step).astype(f32) for a, g in zip(kept, give)
            ]
            step *= 2
        normed_one_grad = halves[0]
        qkv_part = sum(
            rows_dot(a, (odd_grad if i % 2 else even_grad)[(i // 2) * local : (i // 2 + 1) * local])
            for i, a in enumerate(normed_parts)
        ).astype(bf16)
        own = lax.psum_scatter(qkv_part, "batch", scatter_dimension=0, tiled=True).astype(f32)

    pull_one = jax.vjp(modulated, hidden_zero, scale_one, shift_one)[1]
    hidden_grad_one, scale_one_grad, shift_one_grad = pull_one(normed_one_grad)
    hidden_zero_grad = (hidden_one_grad + hidden_grad_one).astype(bf16)
    if built:
        late = UtteranceRows(
            net, jnp.concatenate([shift_one_grad.reshape(1, -1), scale_one_grad.reshape(1, -1)], axis=1)
        )
        skip = Scatter(
            net,
            *grad_blocks(
                net,
                [frames, skips],
                [hidden_zero_grad, hidden_zero_grad],
                [(1, 2, 0, 0), (1, 2, 0, 0)],
                64,
                [s * 0, s * 0 + 8],
            ),
        )
        got, skip.parts[0] = gate(got, skip.parts[0])
        qkv_sums = [total(keep[i], got[i]).astype(bf16) for i in (1, 2, 3)]
        qkv_zs = [net.swap(v, (i + 1) << 3) for i, v in enumerate(qkv_sums)]
        skip.parts[1] = after(skip.parts[1], qkv_sums)
        skip_half = skip.halve(8, 16, 4, 2)
        skip.push(skip_half)
        up.parts[3], skip_half, *late.parts = gate(up.parts[3], skip_half, *late.parts)
        up_sums = up.z_sums()
        up.z_push()
        late.across_z()
        skip.parts[2] = after(skip.parts[2], up_sums)
        skip_quarter = skip.halve(4, 8, 2, 4)
        skip.push(skip_quarter)
        keep, got, skip_quarter, late.parts[0], *rest = gate(
            keep, got, skip_quarter, late.parts[0], *qkv_zs, *late.parts[1:]
        )
        qkv_zs, late.parts[1:] = rest[:3], rest[3:]
        own = total(keep[0], got[0], *qkv_zs)
        late.across_y()
    own = own.reshape(seq, wrow, 3 * part)
    cols = [lax.dynamic_index_in_dim(own, s ^ i, 0, keepdims=False) for i in range(seq)]
    cols = [c if i == 0 else net.swap(c, i) for i, c in enumerate(cols)]
    if built:
        skip.parts[3] = after(skip.parts[3], own)
        skip_sums = skip.z_sums()
        skip.z_push()
        down.parts[0] = after(down.parts[0], skip_sums)
        up.parts[0] = after(up.parts[0], skip_sums)
        grad_down_weight = down.finish()
        own = up.finish()
        grad_up_weight = jnp.concatenate(
            [own[i * wrow : (i + 1) * wrow] for i in range(4)], axis=1
        )
        grad_output_weight = own[4 * wrow :]
        grad_skip_weight = skip.finish()
    else:
        grad_skip_weight = scattered(rows_dot(joined, hidden_zero_grad))
    grad_qkv_weight = spread_columns(cols, seq_order, 3)
    grad_joined = back_dot(hidden_zero_grad, full_skip)
    grad_frames, grad_skip = grad_joined[:, :width], grad_joined[:, width:]

    def by_utterance(*vectors):
        row = jnp.concatenate([vec.reshape(1, -1) for vec in vectors], axis=1)
        place_row = lax.broadcasted_iota(jnp.int32, (batch, row.shape[1]), 0)
        return jnp.where(place_row == net.b, row, 0.0)

    if built:
        early, late = early.rows(), late.rows()
        sums = jnp.sum(early[:, 4 * width :], axis=0)
        up_sum, down_sum = sums[:ff], sums[ff:]
        early = early[:, : 4 * width]
    else:
        early = by_utterance(gate_one_grad, shift_two_grad, scale_two_grad, gate_two_grad)
        flat = jnp.concatenate([early.reshape(-1), up_bias_term, down_bias_term])
        flat = net.sum_all(flat.reshape(-1, 128)).reshape(-1)
        early = flat[: batch * 4 * width].reshape(batch, 4 * width)
        up_sum = flat[batch * 4 * width : batch * 4 * width + ff]
        down_sum = flat[batch * 4 * width + ff :]
        late = net.sum_all(by_utterance(shift_one_grad, scale_one_grad))
    grad_up_bias = lax.dynamic_slice_in_dim(up_sum, d * urow, urow, 0)
    grad_down_bias = lax.dynamic_slice_in_dim(down_sum, d * drow, drow, 0)
    mod_grad = jnp.concatenate([late, early], axis=1)
    grad_modulate_weight = lax.dot_general(
        feat_own.astype(f32),
        mod_grad,
        (((0,), (0,)), ((), ())),
        precision=lax.Precision.HIGHEST,
        preferred_element_type=f32,
    )
    mod_width = modulate_bias.shape[0]
    grad_modulate_bias = jnp.sum(
        lax.dynamic_slice_in_dim(mod_grad, d * mod_width, mod_width, 1), axis=0
    )
    shape = (local, utts, width)
    return (
        layer_out.reshape(shape),
        grad_frames.reshape(shape),
        grad_skip.reshape(shape),
        grad_skip_weight,
        grad_qkv_weight,
        grad_output_weight,
        grad_up_weight,
        grad_up_bias,
        grad_down_weight,
        grad_down_bias,
        grad_modulate_weight,
        grad_modulate_bias,
    )


def solution(mesh):
    rows_two = P("seq", "batch", None)
    owned = P(ALL, None)
    vector = P(ALL)
    in_specs = (
        rows_two,
        rows_two,
        P("batch"),
        P("batch"),
        owned,
        owned,
        owned,
        owned,
        vector,
        owned,
        vector,
        owned,
        vector,
        rows_two,
    )
    out_specs = (
        rows_two,
        rows_two,
        rows_two,
        owned,
        owned,
        owned,
        owned,
        vector,
        owned,
        vector,
        owned,
        vector,
    )
    sizes = (mesh.shape["batch"], mesh.shape["seq"])
    return jax.shard_map(
        functools.partial(body, sizes),
        mesh=mesh,
        in_specs=in_specs,
        out_specs=out_specs,
        check_vma=False,
    )
```

```python
import functools
import math

import jax
import jax.numpy as jnp
from jax import lax
from jax.experimental import pallas as pl
from jax.experimental.pallas import tpu as pltpu
from jax.sharding import PartitionSpec as P

HEADS = 16
HEAD_DIM = 64
epsilon = 1e-06
masked_score = -1e30
f32 = jnp.float32
bf16 = jnp.bfloat16
ALL = ("batch", "seq")


def rms_norm(values):
    return values * lax.rsqrt(jnp.mean(values * values, axis=-1, keepdims=True) + epsilon)


def modulated(hidden, scale_rows, shift_rows):
    return rms_norm(hidden) * (1.0 + scale_rows) + shift_rows


def gelu_tanh(pre_values):
    return jax.nn.gelu(pre_values, approximate=True)


def time_embed(flow_times, embed_width):
    half_width = embed_width // 2
    frequency = jnp.exp(-math.log(10000.0) * jnp.arange(half_width, dtype=f32) / half_width)
    angles = 1000.0 * flow_times[:, None] * frequency[None, :]
    return jnp.concatenate([jnp.sin(angles), jnp.cos(angles)], axis=-1)


def params(semantics=None):
    return pltpu.CompilerParams(dimension_semantics=semantics, vmem_limit_bytes=60 * 1024 * 1024)


class Net:
    def __init__(self, batch, seq):
        self.batch, self.seq, self.n = batch, seq, batch * seq
        self.d = lax.axis_index("batch") * seq + lax.axis_index("seq")
        self.b = lax.axis_index("batch")
        self.s = lax.axis_index("seq")
        self.core = self.d & 1

    def swap(self, value, offset):
        return lax.ppermute(value, ALL, [(i, i ^ offset) for i in range(self.n)])

    def swap_by_core(self, value, even, odd):
        pairs = [(i, i ^ (odd if i & 1 else even)) for i in range(self.n)]
        return lax.ppermute(value, ALL, pairs)

    def sum_all(self, value):
        bit = 1
        while bit < self.n:
            value = value + self.swap(value, bit)
            bit *= 2
        return value


def cost(flops, moved, exps=0):
    return pl.CostEstimate(flops=int(flops), bytes_accessed=int(moved), transcendentals=int(exps))


def after(value, *others):
    return lax.optimization_barrier((value,) + tuple(others))[0]


def gate(*values):
    return lax.optimization_barrier(values)


def place(pieces, tables, count, columns=None):
    rows, width = pieces[0].shape[1:]
    columns = columns or (width,)
    counts = [p.shape[0] for p in pieces]
    total = sum(counts)
    table = jnp.concatenate(tables, axis=-1).astype(jnp.int32)
    if table.ndim == 1:
        table = jnp.broadcast_to(table[None], (len(columns), total))

    def kernel(table_ref, *refs):
        sources = refs[: len(pieces)]
        outs = refs[len(pieces) : len(pieces) + len(columns)]
        sems = refs[-1]
        copies = []
        at = 0
        for source, number in zip(sources, counts):
            for j in range(number):
                left = 0
                for o, wide in enumerate(columns):
                    copies.append(
                        pltpu.make_async_copy(
                            source.at[j, :, pl.ds(left, wide)],
                            outs[o].at[table_ref[o, at]],
                            sems.at[o, at],
                        )
                    )
                    left += wide
                at += 1
        for copy in copies:
            copy.start()
        for copy in copies:
            copy.wait()

    any_spec = pl.BlockSpec(memory_space=pl.ANY)
    outs = pl.pallas_call(
        kernel,
        out_shape=[jax.ShapeDtypeStruct((count, rows, wide), pieces[0].dtype) for wide in columns],
        in_specs=[pl.BlockSpec(memory_space=pltpu.SMEM)] + [any_spec] * len(pieces),
        out_specs=[pl.BlockSpec(memory_space=pltpu.VMEM)] * len(columns),
        scratch_shapes=[pltpu.SemaphoreType.DMA((len(columns), total))],
        compiler_params=params(),
        cost_estimate=cost(0, 4 * count * rows * width),
    )(table, *pieces)
    return [out.reshape(count * rows, wide) for out, wide in zip(outs, columns)]


class Gather:
    def __init__(self, net, shard):
        self.net = net
        self.near = jnp.stack([shard] + [net.swap(shard, k << 3) for k in (1, 2, 3)])

    def far(self):
        self.half = jnp.concatenate([self.near, self.net.swap_by_core(self.near, 2, 4)])
        self.mate_half = self.net.swap(self.half, 1)

    def last(self):
        self.other = self.net.swap_by_core(self.half, 4, 2)

    def mates(self):
        self.mate_other = self.net.swap(self.other, 1)

    def blocks(self):
        d = self.net.d
        z = jnp.arange(4, dtype=jnp.int32) << 3
        second = jnp.where(self.net.core == 0, 2, 4)
        third = 6 - second
        own = jnp.concatenate([d ^ z, d ^ z ^ second])
        mate = d ^ 1
        mate_own = jnp.concatenate([mate ^ z, mate ^ z ^ third])
        return (
            [self.half, self.other, self.mate_half, self.mate_other],
            [own, own ^ third, mate_own, mate_own ^ second],
        )


def grad_blocks(net, lefts, rights, segments, packed_rows, turns=None):
    depth = lefts[0].shape[0]
    tile = 1024
    piece = 32
    chip = net.d >> 1
    rel = jnp.arange(16, dtype=jnp.int32) ^ chip
    x_bit, y_bit, z = rel & 1, (rel >> 1) & 1, rel >> 2
    even = y_bit * 8 + x_bit * 4 + z
    odd = x_bit * 8 + y_bit * 4 + z
    mine = jnp.where(net.core == 0, even, odd)
    other = jnp.where(net.core == 0, odd, even)
    extra = jnp.stack([net.core] + (turns or [net.core * 0] * len(segments)))
    extra = jnp.pad(extra, (0, 16 - extra.shape[0]))
    table = jnp.stack([mine, other, extra]).astype(jnp.int32)
    starts = [0]
    for seg in segments:
        starts.append(starts[-1] + seg[0])
    steps = starts[-1]
    number = len(segments)

    def kernel(table_ref, *refs):
        left_refs, right_refs = refs[:number], refs[number : 2 * number]
        keep, send, scratch, sems = refs[2 * number :]
        t = pl.program_id(0)
        slot = t % 2
        core = table_ref[2, 0]

        def copy(v, p, at_slot, source_row, pos, dest_row):
            dest = send if p else keep
            return pltpu.make_async_copy(
                scratch.at[at_slot, pl.ds(pl.multiple_of(source_row, piece), piece)],
                dest.at[pos, pl.ds(pl.multiple_of(dest_row, piece), piece)],
                sems.at[at_slot, p, v],
            )

        def wait_slot(at_slot):
            for v in range(16):
                for p in range(2):
                    copy(v, p, at_slot, 0, 0, 0).wait()

        @pl.when(t >= 2)
        def _():
            wait_slot(slot)

        left, right = left_refs[-1][...], right_refs[-1][...]
        for i in range(number - 2, -1, -1):
            early = t < starts[i + 1]
            left = jnp.where(early, left_refs[i][...], left)
            right = jnp.where(early, right_refs[i][...], right)
        scratch[slot] = lax.dot_general(
            left, right, (((0,), (0,)), ((), ())), preferred_element_type=f32
        ).astype(bf16)
        for v in range(16):
            for p in range(2):
                side = core ^ p
                chip_at = source = dest_row = jnp.int32(0)
                for i, (_, subs, base, rise) in reversed(list(enumerate(segments))):
                    local = t - starts[i]
                    here = (
                        (local * (16 // subs) % 16 + v // subs) ^ table_ref[2, 1 + i],
                        (2 * (v // subs) + side) * subs * piece + (v % subs) * piece,
                        base + local * rise + (v % subs) * piece,
                    )
                    if i == number - 1:
                        chip_at, source, dest_row = here
                    else:
                        early = t < starts[i + 1]
                        chip_at = jnp.where(early, here[0], chip_at)
                        source = jnp.where(early, here[1], source)
                        dest_row = jnp.where(early, here[2], dest_row)
                copy(v, p, slot, source, table_ref[p, chip_at], dest_row).start()

        @pl.when(t == steps - 1)
        def _():
            wait_slot(slot)
            if steps > 1:
                wait_slot(1 - slot)

    def spec(array, i):
        count = array.shape[1] // tile
        if count == 1:
            return pl.BlockSpec((depth, tile), lambda t, table: (0, 0))
        return pl.BlockSpec(
            (depth, tile), lambda t, table: (0, jnp.clip(t - starts[i], 0, count - 1))
        )

    any_spec = pl.BlockSpec(memory_space=pl.ANY)
    shape = jax.ShapeDtypeStruct((16, packed_rows, tile), bf16)
    return pl.pallas_call(
        kernel,
        out_shape=[shape, shape],
        grid_spec=pltpu.PrefetchScalarGridSpec(
            num_scalar_prefetch=1,
            grid=(steps,),
            in_specs=[spec(a, i) for i, a in enumerate(lefts)]
            + [spec(a, i) for i, a in enumerate(rights)],
            out_specs=[any_spec, any_spec],
            scratch_shapes=[
                pltpu.VMEM((2, tile, tile), bf16),
                pltpu.SemaphoreType.DMA((2, 2, 16)),
            ],
        ),
        compiler_params=params(("arbitrary",)),
        cost_estimate=cost(2 * steps * depth * tile * tile, 3 * steps * tile * tile * 2),
    )(table, *lefts, *rights)


def total(*parts):
    result = parts[0].astype(f32)
    for part in parts[1:]:
        result = result + part.astype(f32)
    return result


class Scatter:
    def __init__(self, net, keep, send):
        self.net, self.parts = net, [keep]
        self.parts.append(net.swap(send, 1))

    def halve(self, low, high, even, odd):
        out = total(*[p[low:high] for p in self.parts]).astype(bf16)
        self.out = out
        self.pair = (even, odd)
        return out

    def push(self, out):
        self.parts.append(self.net.swap_by_core(out, *self.pair))

    def z_sums(self):
        self.outs = [total(*[p[k : k + 1] for p in self.parts]).astype(bf16) for k in (1, 2, 3)]
        return self.outs

    def z_push(self):
        self.zs = [self.net.swap(o, (k + 1) << 3) for k, o in enumerate(self.outs)]

    def finish(self):
        return total(*[p[0:1] for p in self.parts], *self.zs)[0]


class UtteranceRows:
    def __init__(self, net, row):
        self.net, self.parts = net, [row] + [net.swap(row, k) for k in (1, 2, 3)]

    def across_z(self):
        row = sum(self.parts[1:], self.parts[0])
        self.parts = [row] + [self.net.swap(row, k << 3) for k in (1, 2, 3)]

    def across_y(self):
        self.parts = [jnp.concatenate(self.parts)]
        self.parts.append(self.net.swap(self.parts[0], 4))

    def rows(self):
        return jnp.stack(self.parts, axis=1).reshape(8, self.parts[0].shape[1])


def spread_columns(parts, order, groups):
    rows, width = parts[0].shape
    number = len(parts)
    wide = width // groups

    def kernel(order_ref, *refs):
        out, sems = refs[number:]
        copies = []
        for i in range(number):
            for g in range(groups):
                at = pl.multiple_of((order_ref[i] + g * number) * wide, wide)
                copies.append(
                    pltpu.make_async_copy(
                        refs[i].at[:, pl.ds(g * wide, wide)],
                        out.at[:, pl.ds(at, wide)],
                        sems.at[i, g],
                    )
                )
        for copy in copies:
            copy.start()
        for copy in copies:
            copy.wait()

    return pl.pallas_call(
        kernel,
        out_shape=jax.ShapeDtypeStruct((rows, width * number), parts[0].dtype),
        in_specs=[pl.BlockSpec(memory_space=pltpu.SMEM)]
        + [pl.BlockSpec(memory_space=pltpu.VMEM)] * number,
        out_specs=pl.BlockSpec(memory_space=pltpu.VMEM),
        scratch_shapes=[pltpu.SemaphoreType.DMA((number, groups))],
        compiler_params=params(),
        cost_estimate=cost(0, 8 * rows * width * number),
    )(order.astype(jnp.int32), *parts)


def rope(values, cosine, sine, back):
    width = values.shape[-1]
    lane = lax.broadcasted_iota(jnp.int32, values.shape, 1)
    early = (lane & (HEAD_DIM - 1)) < HEAD_DIM // 2
    source = values * sine if back else values
    ahead = pltpu.roll(source, width - HEAD_DIM // 2, 1)
    behind = pltpu.roll(source, HEAD_DIM // 2, 1)
    if back:
        turned = jnp.where(early, ahead, -behind)
        return values * cosine + turned
    turned = jnp.where(early, -ahead, behind)
    return values * cosine + turned * sine


def wide_tables(cos_ref, sin_ref, width):
    reps = width // cos_ref.shape[-1]
    cosine = jnp.concatenate([cos_ref[...]] * reps, axis=-1)
    sine = jnp.concatenate([sin_ref[...]] * reps, axis=-1)
    return cosine, sine


def qkv_kernel(number, *refs):
    w_ref, cos_ref, sin_ref, q_ref, k_ref, v_ref = refs[number:]
    width = q_ref.shape[-1]
    scale = HEAD_DIM ** (-0.5)
    for i in range(number):

        @pl.when(pl.program_id(0) == i)
        def _():
            result = jnp.dot(refs[i][...], w_ref[...], preferred_element_type=f32)
            cosine, sine = wide_tables(cos_ref, sin_ref, width)
            q_ref[...] = (rope(result[:, :width], cosine, sine, False) * scale).astype(bf16)
            k_ref[...] = rope(result[:, width : 2 * width], cosine, sine, False).astype(bf16)
            v_ref[...] = result[:, 2 * width :].astype(bf16)


def qkv_project(parts, w, cosine, sine):
    block, depth = parts[0].shape
    rows = block * len(parts)
    width = w.shape[1] // 3
    row = lambda wide: pl.BlockSpec((block, wide), lambda i: (i, 0))
    whole = lambda a: pl.BlockSpec(a.shape, lambda i: (0, 0))
    return pl.pallas_call(
        functools.partial(qkv_kernel, len(parts)),
        grid=(len(parts),),
        out_shape=[jax.ShapeDtypeStruct((rows, width), bf16)] * 3,
        in_specs=[whole(a) for a in parts] + [whole(w), row(128), row(128)],
        out_specs=[row(width)] * 3,
        compiler_params=params(("arbitrary",)),
        cost_estimate=cost(2 * rows * depth * 3 * width, 2 * rows * (depth + 3 * width)),
    )(*parts, w, cosine, sine)


def qkv_back(pieces, w, local, first, dtype):
    rows = pieces[0].shape[0]
    wide = pieces[0].shape[1]
    count = rows // local // 2
    width = len(pieces) * wide

    def kernel(*refs):
        w_ref, all_ref, out_ref = refs[len(pieces) :]
        joined = jnp.concatenate([r[...] for r in refs[: len(pieces)]], axis=-1)
        all_ref[...] = joined
        out_ref[...] = lax.dot_general(
            joined, w_ref[...], (((1,), (1,)), ((), ())), preferred_element_type=f32
        ).astype(dtype)

    return pl.pallas_call(
        kernel,
        grid=(count,),
        out_shape=[
            jax.ShapeDtypeStruct((count * local, width), bf16),
            jax.ShapeDtypeStruct((count * local, w.shape[0]), dtype),
        ],
        in_specs=[pl.BlockSpec((local, wide), lambda i: (2 * i + first, 0))] * len(pieces)
        + [pl.BlockSpec(w.shape, lambda i: (0, 0))],
        out_specs=[
            pl.BlockSpec((local, width), lambda i: (i, 0)),
            pl.BlockSpec((local, w.shape[0]), lambda i: (i, 0)),
        ],
        compiler_params=params(("arbitrary",)),
        cost_estimate=cost(2 * count * local * width * w.shape[0], 8 * count * local * w.shape[0]),
    )(*pieces, w)


def qkv_grad_blocks(net, lefts, grads):
    local, depth = lefts[0].shape
    width = grads[0].shape[1]
    rows = depth // 8
    t = jnp.arange(8, dtype=jnp.int32)
    table = net.b ^ ((t & 3) << 1) ^ jnp.where(t < 4, 1, 0)
    number = len(lefts)

    def kernel(table_ref, *refs):
        keep, send = refs[number + len(grads) :]
        result = jnp.zeros((rows, width), f32)
        for i in range(number):
            grad = refs[number + i % 2][(i // 2) * local : (i // 2 + 1) * local]
            result = result + lax.dot_general(
                refs[i][...], grad, (((0,), (0,)), ((), ())), preferred_element_type=f32
            )
        result = result.astype(bf16)[None]
        step = pl.program_id(0)

        @pl.when(step < 4)
        def _():
            send[...] = result

        @pl.when(step >= 4)
        def _():
            keep[...] = result

    shape = jax.ShapeDtypeStruct((4, rows, width), bf16)
    block = (1, rows, width)
    return pl.pallas_call(
        kernel,
        out_shape=[shape, shape],
        grid_spec=pltpu.PrefetchScalarGridSpec(
            num_scalar_prefetch=1,
            grid=(8,),
            in_specs=[pl.BlockSpec((local, rows), lambda i, t: (0, t[i]))] * number
            + [pl.BlockSpec(g.shape, lambda i, t: (0, 0)) for g in grads],
            out_specs=[
                pl.BlockSpec(block, lambda i, t: (jnp.maximum(i - 4, 0), 0, 0)),
                pl.BlockSpec(block, lambda i, t: (jnp.minimum(i, 3), 0, 0)),
            ],
        ),
        compiler_params=params(("arbitrary",)),
        cost_estimate=cost(2 * number * local * depth * width, 4 * depth * width),
    )(table, *lefts, *grads)


def attend_kernel(heads, q_ref, k_ref, v_ref, bias_ref, o_ref, lse_ref):
    q = q_ref[...]
    k = k_ref[...]
    v = v_ref[...]
    bias = bias_ref[...]
    lane = lax.broadcasted_iota(jnp.int32, q.shape, 1) // HEAD_DIM
    spot = lax.broadcasted_iota(jnp.int32, lse_ref.shape, 1)
    out = jnp.zeros(q.shape, f32)
    lse = jnp.zeros(lse_ref.shape, f32)
    for h in range(heads):
        mine = lane == h
        qh = jnp.where(mine, q, jnp.zeros_like(q))
        s = lax.dot_general(qh, k, (((1,), (1,)), ((), ())), preferred_element_type=f32) + bias
        top = jnp.max(s, axis=-1, keepdims=True)
        p = jnp.exp(s - top)
        total = jnp.sum(p, axis=-1, keepdims=True)
        o = jnp.dot(p.astype(bf16), v, preferred_element_type=f32) / total
        out = jnp.where(mine, o, out)
        lse = jnp.where(spot == h, top + jnp.log(total), lse)
    o_ref[...] = out.astype(bf16)
    lse_ref[...] = lse


def attend(q, k, v, bias, heads):
    rows, width = q.shape
    block = 256
    row = lambda wide: pl.BlockSpec((block, wide), lambda i: (i, 0))
    whole = pl.BlockSpec((rows, width), lambda i: (0, 0))
    return pl.pallas_call(
        functools.partial(attend_kernel, heads),
        grid=(rows // block,),
        out_shape=[jax.ShapeDtypeStruct((rows, width), bf16), jax.ShapeDtypeStruct((rows, 128), f32)],
        in_specs=[row(width), whole, whole, pl.BlockSpec((1, rows), lambda i: (0, 0))],
        out_specs=[row(width), row(128)],
        compiler_params=params(("arbitrary",)),
        cost_estimate=cost(
            16 * rows * rows * heads * HEAD_DIM, 8 * rows * width, rows * rows * heads
        ),
    )(q, k, v, bias)


def attend_back_kernel(
    heads,
    first,
    q_ref,
    do_ref,
    o_ref,
    lse_ref,
    k_ref,
    v_ref,
    kt_ref,
    bias_ref,
    cosq_ref,
    sinq_ref,
    cosk_ref,
    sink_ref,
    dq_ref,
    dk_ref,
    dv_ref,
    p_all,
    ds_all,
    dk_acc,
    dv_acc,
):
    step = pl.program_id(0)
    q = q_ref[...]
    do = do_ref[...]
    k = k_ref[...]
    v = v_ref[...]
    block, width = q.shape
    lane = lax.broadcasted_iota(jnp.int32, q.shape, 1) // HEAD_DIM
    product = (do.astype(f32) * o_ref[...].astype(f32)).T
    lse_t = lse_ref[...].T
    bias = bias_ref[...]
    contract = (((1,), (1,)), ((), ()))
    q_parts, do_parts, dq_parts = [], [], []
    for h in range(heads):
        mine = lane == h
        qh = jnp.where(mine, q, jnp.zeros_like(q))
        doh = jnp.where(mine, do, jnp.zeros_like(do))
        q_parts.append(qh)
        do_parts.append(doh)
        row_dot = jnp.sum(product[h * HEAD_DIM : (h + 1) * HEAD_DIM], axis=0, keepdims=True)
        s = lax.dot_general(k, qh, contract, preferred_element_type=f32)
        p = jnp.exp(s + bias - lse_t[first + h : first + h + 1])
        dp = lax.dot_general(v, doh, contract, preferred_element_type=f32)
        ds = (p * (dp - row_dot)).astype(bf16)
        p_all[:, h * block : (h + 1) * block] = p.astype(bf16)
        ds_all[:, h * block : (h + 1) * block] = ds
        dq_parts.append(
            jnp.dot(kt_ref[h * HEAD_DIM : (h + 1) * HEAD_DIM, :], ds, preferred_element_type=f32)
        )
    dv = jnp.dot(p_all[...], jnp.concatenate(do_parts, axis=0), preferred_element_type=f32)
    dk = jnp.dot(ds_all[...], jnp.concatenate(q_parts, axis=0), preferred_element_type=f32)

    @pl.when(step == 0)
    def _():
        dv_acc[...] = dv
        dk_acc[...] = dk

    @pl.when(step > 0)
    def _():
        dv_acc[...] += dv
        dk_acc[...] += dk

    dq = jnp.concatenate(dq_parts, axis=0).T
    cosine, sine = wide_tables(cosq_ref, sinq_ref, width)
    dq_ref[...] = (rope(dq, cosine, sine, True) * (HEAD_DIM ** (-0.5))).astype(bf16)

    @pl.when(step == pl.num_programs(0) - 1)
    def _():
        cosine, sine = wide_tables(cosk_ref, sink_ref, width)
        dk_ref[...] = rope(dk_acc[...], cosine, sine, True).astype(bf16)
        dv_ref[...] = dv_acc[...].astype(bf16)


def attend_back(q, k, v, o, do, lse, k_turned, bias, cosine, sine, heads, group):
    rows = q.shape[0]
    width = heads * HEAD_DIM
    block = 256
    lanes = lambda wide: pl.BlockSpec((block, wide), lambda i: (i, group))
    row = lambda wide: pl.BlockSpec((block, wide), lambda i: (i, 0))
    whole = lambda wide, at: pl.BlockSpec((rows, wide), lambda i: (0, at))
    out = jax.ShapeDtypeStruct((rows, width), bf16)
    return pl.pallas_call(
        functools.partial(attend_back_kernel, heads, group * heads),
        grid=(rows // block,),
        out_shape=[out] * 3,
        in_specs=[
            lanes(width),
            lanes(width),
            lanes(width),
            row(128),
            whole(width, group),
            whole(width, group),
            pl.BlockSpec((width, rows), lambda i: (group, 0)),
            whole(block, 0),
            row(128),
            row(128),
            whole(128, 0),
            whole(128, 0),
        ],
        out_specs=[row(width), whole(width, 0), whole(width, 0)],
        scratch_shapes=[
            pltpu.VMEM((rows, heads * block), bf16),
            pltpu.VMEM((rows, heads * block), bf16),
            pltpu.VMEM((rows, width), f32),
            pltpu.VMEM((rows, width), f32),
        ],
        compiler_params=params(("arbitrary",)),
        cost_estimate=cost(
            40 * rows * rows * heads * HEAD_DIM, 16 * rows * width, rows * rows * heads
        ),
    )(
        q,
        do,
        o,
        lse,
        k,
        v,
        k_turned,
        bias,
        cosine,
        sine,
        cosine,
        sine,
    )


def body(
    mesh_sizes,
    frames_in,
    skip_in,
    flow_times,
    lengths,
    skip_weight,
    qkv_weight,
    output_weight,
    up_weight,
    up_bias,
    down_weight,
    down_bias,
    modulate_weight,
    modulate_bias,
    output_grad,
):
    batch, seq = mesh_sizes
    net = Net(batch, seq)
    n, d, s = net.n, net.d, net.s
    local, utts, width = frames_in.shape
    frames = frames_in.reshape(local, width)
    skips = skip_in.reshape(local, width)
    out_grad = output_grad.reshape(local, width).astype(f32)
    heads = HEADS // seq
    part = heads * HEAD_DIM
    rows = local * seq
    built = n == 32 and seq == 4
    wrow = width // n
    ff = up_weight.shape[1]

    seq_order = s ^ jnp.arange(seq, dtype=jnp.int32)
    by_part = qkv_weight.reshape(wrow, 3, seq, part)
    pieces = [
        lax.dynamic_index_in_dim(by_part, s ^ k, 2, keepdims=False).reshape(wrow, 3 * part)
        for k in range(seq)
    ]
    urow, drow = up_bias.shape[0], down_bias.shape[0]
    if built:
        vectors = jnp.concatenate(
            [
                up_bias.reshape(1, urow),
                jnp.pad(down_bias, (0, urow - drow)).reshape(1, urow),
                jnp.zeros((wrow - 2, urow), bf16),
            ]
        )
        pieces = [jnp.concatenate([p, vectors], axis=1) for p in pieces]
    pieces = [p if k == 0 else net.swap(p, k) for k, p in enumerate(pieces)]
    if built:
        skip_gather = Gather(net, skip_weight)
        skip_gather.far()
        skip_gather.last()
        qkv_four = after(jnp.stack(pieces), skip_gather.other)
        qkv_far = [net.swap(qkv_four, k << 3) for k in (1, 2, 3)]
        skip_gather.mates()
        (full_skip,) = place(*skip_gather.blocks(), n)
        ou = jnp.concatenate([output_weight, up_weight], axis=1)
    else:
        gather = lambda w, ax: lax.all_gather(w, ax, axis=0, tiled=True)
        full_skip = gather(skip_weight, ALL)
        full_qkv = gather(jnp.stack(pieces)[seq_order], "batch")
        full_qkv = full_qkv.reshape(batch, seq, wrow, 3 * part)
        full_qkv = full_qkv.reshape(width, 3 * part)
        full_output = gather(output_weight, ALL).reshape(seq, width // seq, width)[seq_order]
        full_output = full_output.reshape(width, width)
        full_up = gather(up_weight, ALL)
        full_down = gather(down_weight, ALL)

    mod_bias = lax.dynamic_update_slice_in_dim(
        jnp.zeros((6 * width,), f32), modulate_bias.astype(f32), d * modulate_bias.shape[0], 0
    )
    if built:
        times = jnp.broadcast_to(flow_times.reshape(1, 1), (8, 128))
        times = [times] + [net.swap(times, k << 3) for k in (1, 2, 3)]
        *times, _ = gate(*times, skip_gather.half)
        times = jnp.concatenate([t[:1] for t in times] * 2)
        times = jnp.stack([times[:4], net.swap(times, 4)[:4]], axis=1).reshape(batch, 128)
        all_times = times[:, 0]
    else:
        small = jnp.concatenate([up_bias.astype(f32), down_bias.astype(f32), flow_times])
        small_width = -(-small.shape[0] // 128) * 128
        small = jnp.pad(small, (0, small_width - small.shape[0]))
        slots = lax.broadcasted_iota(jnp.int32, (n, small_width), 0)
        small = net.sum_all(jnp.where(slots == d, small[None], 0.0))
        full_up_bias = small[:, :urow].reshape(1, ff)
        full_down_bias = small[:, urow : urow + drow].reshape(1, width)
        all_times = small.reshape(batch, seq, small_width)[:, 0, urow + drow]
    feat = jax.nn.silu(time_embed(all_times, width)).astype(bf16)
    feat_own = lax.dynamic_slice_in_dim(feat, d * wrow, wrow, 1)
    modulation = jnp.dot(feat_own, modulate_weight, preferred_element_type=f32)
    modulation = modulation + mod_bias[None]
    if built:
        sums = modulation[0:2]
        for k in (1, 2, 3):
            sums = sums + net.swap(modulation[2 * k : 2 * k + 2], k << 3)
        sums = sums[0:1] + net.swap(sums[1:2], 4)
        modulation = sums
        for k in (1, 2, 3):
            modulation = modulation + net.swap(sums, k)
    else:
        bit = batch // 2
        while bit:
            high = (net.b & bit) // bit
            sent = lax.dynamic_slice_in_dim(modulation, (1 - high) * bit, bit, 0)
            kept = lax.dynamic_slice_in_dim(modulation, high * bit, bit, 0)
            modulation = kept + net.swap(sent, bit * seq)
            bit //= 2
        bit = 1
        while bit < seq:
            modulation = modulation + net.swap(modulation, bit)
            bit *= 2
    shift_one, scale_one, gate_one, shift_two, scale_two, gate_two = jnp.split(modulation, 6, -1)

    half_dim = HEAD_DIM // 2
    inverse = jnp.exp(-math.log(10000.0) * 2.0 * jnp.arange(half_dim, dtype=f32) / HEAD_DIM)
    positions = (
        seq_order[:, None] * local + jnp.arange(local, dtype=jnp.int32)[None]
    ).reshape(rows)
    angles = positions.astype(f32)[:, None] * jnp.tile(inverse, 128 // half_dim)[None]
    cosine, sine = jnp.cos(angles), jnp.sin(angles)
    key_bias = jnp.where(positions < lengths[0], 0.0, masked_score).astype(f32)[None]

    joined = jnp.concatenate([frames, skips], axis=-1)
    hidden_zero = jnp.dot(joined, full_skip, preferred_element_type=f32)
    normed_one = modulated(hidden_zero, scale_one, shift_one).astype(bf16)
    if built:
        normed_one, ou, *qkv_far = gate(normed_one, ou, *qkv_far)
        qkv_z = jnp.concatenate([qkv_four] + qkv_far)
        qkv_y = net.swap(qkv_z, 4)
        ou_gather = Gather(net, ou)
        k16 = jnp.arange(16, dtype=jnp.int32)
        z_spots = d ^ (((k16 >> 2) << 3) | (k16 & 3))
        full_qkv, vectors = place(
            [qkv_z, qkv_y], [z_spots, z_spots ^ 4], n, (3 * part, urow)
        )
    across = {0: normed_one}
    bit = seq // 2
    while bit:
        across.update({i | bit: net.swap(a, bit) for i, a in list(across.items())})
        if built and bit == 2:
            across[2], cosine, sine, full_qkv, ou_gather.near, down_own = gate(
                across[2], cosine, sine, full_qkv, ou_gather.near, down_weight
            )
            down_gather = Gather(net, down_own)
        bit //= 2
    normed_parts = [across[i] for i in range(seq)]
    if built:
        ou_gather.far()
        vectors = vectors.reshape(n, wrow, urow)
        full_up_bias = vectors[:, 0].reshape(1, ff).astype(f32)
        full_down_bias = vectors[:, 1, :drow].reshape(1, width).astype(f32)
    q, k, v = qkv_project(normed_parts, full_qkv, cosine, sine)
    if built:
        q, ou_gather.half, down_gather.near = lax.optimization_barrier(
            (q, ou_gather.half, down_gather.near)
        )
        ou_gather.last()
        down_gather.far()
    att, lse = attend(q, k, v, key_bias, heads)
    if built:
        att, ou_gather.other, ou_gather.mate_half, down_gather.half = gate(
            att, ou_gather.other, ou_gather.mate_half, down_gather.half
        )
        ou_gather.mates()
        got, spots = ou_gather.blocks()
        spots = jnp.concatenate(spots)
        turned = spots ^ (s * (n // seq))
        full_output, full_up = place(got, [jnp.stack([turned, spots])], n, (width, ff))
    blocks = [att[i * local : (i + 1) * local] for i in range(seq)]
    k_turned = k.T
    bias_wide = jnp.broadcast_to(key_bias.reshape(rows, 1), (rows, 256))
    blocks = [b if i == 0 else net.swap(b, i) for i, b in enumerate(blocks)]
    *blocks, full_output, full_up, k_turned, bias_wide = gate(
        *blocks, full_output, full_up, k_turned, bias_wide
    )
    attended = jnp.concatenate(blocks, axis=-1)
    if built:
        down_gather.half = after(down_gather.half, attended)
        down_gather.last()
    attn_proj = jnp.dot(attended, full_output, preferred_element_type=f32)
    hidden_one = hidden_zero + gate_one * attn_proj
    normed_two = modulated(hidden_one, scale_two, shift_two).astype(bf16)
    pre_act = jnp.dot(normed_two, full_up, preferred_element_type=f32) + full_up_bias
    activated = gelu_tanh(pre_act).astype(bf16)
    if built:
        down_gather.other, down_gather.mate_half, activated = gate(
            down_gather.other, down_gather.mate_half, activated
        )
        down_gather.mates()
        (full_down,) = place(*down_gather.blocks(), n)
    ffn_out = jnp.dot(activated, full_down, preferred_element_type=f32) + full_down_bias
    layer_out = (hidden_one + gate_two * ffn_out).astype(bf16)

    rows_dot = lambda a, b: lax.dot_general(
        a, b, (((0,), (0,)), ((), ())), preferred_element_type=f32
    )
    back_dot = lambda a, b: lax.dot_general(
        a, b, (((1,), (1,)), ((), ())), preferred_element_type=f32
    )

    def scattered(grads, turn=False):
        if turn:
            grads = grads.reshape(seq, width // seq, -1)[seq_order].reshape(grads.shape)
        return lax.psum_scatter(
            grads.astype(bf16), ALL, scatter_dimension=0, tiled=True
        ).astype(f32)

    ffn_grad = out_grad * gate_two
    down_bias_term = jnp.sum(ffn_grad, axis=0)
    ffn_grad_low = ffn_grad.astype(bf16)
    act_grad = back_dot(ffn_grad_low, full_down)
    pre_grad = jax.vjp(gelu_tanh, pre_act)[1](act_grad)[0]
    up_bias_term = jnp.sum(pre_grad, axis=0)
    pre_grad_low = pre_grad.astype(bf16)
    normed_two_grad = back_dot(pre_grad_low, full_up)
    pull_two = jax.vjp(modulated, hidden_one, scale_two, shift_two)[1]
    hidden_grad_two, scale_two_grad, shift_two_grad = pull_two(normed_two_grad)
    gate_two_grad = jnp.sum(out_grad * ffn_out, axis=0)
    hidden_one_grad = out_grad + hidden_grad_two
    gate_one_grad = jnp.sum(hidden_one_grad * attn_proj, axis=0)
    proj_grad_low = (hidden_one_grad * gate_one).astype(bf16)
    attended_grad = back_dot(proj_grad_low, full_output).astype(bf16)
    pieces = [attended_grad[:, i * part : (i + 1) * part] for i in range(seq)]
    grad_all = jnp.concatenate([p if i == 0 else net.swap(p, i) for i, p in enumerate(pieces)])
    pair = lambda i, grad: attend_back(
        q, k, v, att, grad, lse, k_turned, bias_wide, cosine, sine, 2, i
    )
    if built:
        early_row = jnp.concatenate(
            [
                v.reshape(1, -1)
                for v in (
                    gate_one_grad,
                    shift_two_grad,
                    scale_two_grad,
                    gate_two_grad,
                    up_bias_term,
                    down_bias_term,
                )
            ],
            axis=1,
        )
        activated, attended_grad = lax.optimization_barrier((activated, attended_grad))
        down = Scatter(net, *grad_blocks(net, [activated], [ffn_grad_low], [(4, 4, 0, 0)], 128))
        normed_two = after(normed_two, down.parts[0])
        up = Scatter(
            net,
            *grad_blocks(
                net,
                [normed_two, attended],
                [pre_grad_low, proj_grad_low],
                [(4, 1, 0, 32), (1, 1, 128, 0)],
                160,
                [s * 0, s * (n // seq // 2)],
            ),
        )
        down_half = down.halve(8, 16, 4, 2)
        down.push(down_half)
        grad_all, down_half, early_row, _ = lax.optimization_barrier(
            (grad_all, down_half, early_row, up.parts[0])
        )
        early = UtteranceRows(net, early_row)
        first = pair(0, grad_all)
        up.parts[1], down.parts[2], first, *early.parts = gate(
            up.parts[1], down.parts[2], first, *early.parts
        )
        early.across_z()
        up_half = up.halve(8, 16, 4, 2)
        up.push(up_half)
        down_half = down.halve(4, 8, 2, 4)
        down.push(down_half)
        grad_all, _ = gate(grad_all, (up_half, down_half, first))
        second = pair(1, grad_all)
        up.parts[2], down.parts[3], second = gate(up.parts[2], down.parts[3], second)
        results = [first, second]
    else:
        grad_down_weight = scattered(rows_dot(activated, ffn_grad_low))
        grad_up_weight = scattered(rows_dot(normed_two, pre_grad_low))
        grad_output_weight = scattered(rows_dot(attended, proj_grad_low), True)
        results = [pair(i, grad_all) for i in range(heads // 2)]
    pieces = [r[i] for i in range(3) for r in results]
    odd_grad, odd = qkv_back(pieces, full_qkv, local, 1, bf16)
    sent = net.swap(odd, 1)
    even_grad, even = qkv_back(pieces, full_qkv, local, 0, f32)
    halves = [
        even[i * local : (i + 1) * local] + sent[i * local : (i + 1) * local].astype(f32)
        for i in range(seq // 2)
    ]
    if built:
        give = halves[1].astype(bf16)
        taken = net.swap(give, 2)
        down.parts[2], down.parts[3], give, *early.parts = gate(
            down.parts[2], down.parts[3], give, *early.parts
        )
        early.across_y()
        down_sums = down.z_sums()
        down.z_push()
        *normed_parts, _, _ = gate(*normed_parts, give, down_sums)
        keep, send = qkv_grad_blocks(net, normed_parts, [even_grad, odd_grad])
        got = net.swap(send, 4)
        up.parts[2], keep = gate(up.parts[2], keep)
        up_quarter = up.halve(4, 8, 2, 4)
        up.push(up_quarter)
        taken, _, *down.zs = gate(taken, up_quarter, *down.zs)
        normed_one_grad = halves[0] + taken.astype(f32)
    else:
        step = 2
        while len(halves) > 1:
            kept = halves[0::2]
            give = halves[1::2]
            halves = [
                a + net.swap(g.astype(bf16), step).astype(f32) for a, g in zip(kept, give)
            ]
            step *= 2
        normed_one_grad = halves[0]
        qkv_part = sum(
            rows_dot(a, (odd_grad if i % 2 else even_grad)[(i // 2) * local : (i // 2 + 1) * local])
            for i, a in enumerate(normed_parts)
        ).astype(bf16)
        own = lax.psum_scatter(qkv_part, "batch", scatter_dimension=0, tiled=True).astype(f32)

    pull_one = jax.vjp(modulated, hidden_zero, scale_one, shift_one)[1]
    hidden_grad_one, scale_one_grad, shift_one_grad = pull_one(normed_one_grad)
    hidden_zero_grad = (hidden_one_grad + hidden_grad_one).astype(bf16)
    if built:
        hidden_zero_grad, got = gate(hidden_zero_grad, got)
        late = UtteranceRows(
            net, jnp.concatenate([shift_one_grad.reshape(1, -1), scale_one_grad.reshape(1, -1)], axis=1)
        )
        skip = Scatter(
            net,
            *grad_blocks(
                net,
                [frames, skips],
                [hidden_zero_grad, hidden_zero_grad],
                [(1, 2, 0, 0), (1, 2, 0, 0)],
                64,
                [s * 0, s * 0 + 8],
            ),
        )
        got, skip.parts[0] = gate(got, skip.parts[0])
        qkv_sums = [total(keep[i], got[i]).astype(bf16) for i in (1, 2, 3)]
        qkv_zs = [net.swap(v, (i + 1) << 3) for i, v in enumerate(qkv_sums)]
        skip.parts[1] = after(skip.parts[1], qkv_sums)
        skip_half = skip.halve(8, 16, 4, 2)
        skip.push(skip_half)
        up.parts[3], hidden_zero_grad, skip_half, *late.parts = gate(
            up.parts[3], hidden_zero_grad, skip_half, *late.parts
        )
        up_sums = up.z_sums()
        up.z_push()
        late.across_z()
        skip.parts[2] = after(skip.parts[2], up_sums)
        skip_quarter = skip.halve(4, 8, 2, 4)
        skip.push(skip_quarter)
        keep, got, skip_quarter, late.parts[0], *rest = gate(
            keep, got, skip_quarter, late.parts[0], *qkv_zs, *late.parts[1:]
        )
        qkv_zs, late.parts[1:] = rest[:3], rest[3:]
        own = total(keep[0], got[0], *qkv_zs)
        late.across_y()
    own = own.reshape(seq, wrow, 3 * part)
    cols = [lax.dynamic_index_in_dim(own, s ^ i, 0, keepdims=False) for i in range(seq)]
    cols = [c if i == 0 else net.swap(c, i) for i, c in enumerate(cols)]
    if built:
        skip.parts[3] = after(skip.parts[3], own)
        skip_sums = skip.z_sums()
        skip.z_push()
        down.parts[0] = after(down.parts[0], skip_sums)
        up.parts[0] = after(up.parts[0], skip_sums)
        grad_down_weight = down.finish()
        own = up.finish()
        grad_up_weight = jnp.concatenate(
            [own[i * wrow : (i + 1) * wrow] for i in range(4)], axis=1
        )
        grad_output_weight = own[4 * wrow :]
        grad_skip_weight = skip.finish()
    else:
        grad_skip_weight = scattered(rows_dot(joined, hidden_zero_grad))
    grad_qkv_weight = spread_columns(cols, seq_order, 3)
    grad_joined = back_dot(hidden_zero_grad, full_skip)
    grad_frames, grad_skip = grad_joined[:, :width], grad_joined[:, width:]

    def by_utterance(*vectors):
        row = jnp.concatenate([vec.reshape(1, -1) for vec in vectors], axis=1)
        place_row = lax.broadcasted_iota(jnp.int32, (batch, row.shape[1]), 0)
        return jnp.where(place_row == net.b, row, 0.0)

    if built:
        early, late = early.rows(), late.rows()
        sums = jnp.sum(early[:, 4 * width :], axis=0)
        up_sum, down_sum = sums[:ff], sums[ff:]
        early = early[:, : 4 * width]
    else:
        early = by_utterance(gate_one_grad, shift_two_grad, scale_two_grad, gate_two_grad)
        flat = jnp.concatenate([early.reshape(-1), up_bias_term, down_bias_term])
        flat = net.sum_all(flat.reshape(-1, 128)).reshape(-1)
        early = flat[: batch * 4 * width].reshape(batch, 4 * width)
        up_sum = flat[batch * 4 * width : batch * 4 * width + ff]
        down_sum = flat[batch * 4 * width + ff :]
        late = net.sum_all(by_utterance(shift_one_grad, scale_one_grad))
    grad_up_bias = lax.dynamic_slice_in_dim(up_sum, d * urow, urow, 0)
    grad_down_bias = lax.dynamic_slice_in_dim(down_sum, d * drow, drow, 0)
    mod_grad = jnp.concatenate([late, early], axis=1)
    grad_modulate_weight = lax.dot_general(
        feat_own.astype(f32),
        mod_grad,
        (((0,), (0,)), ((), ())),
        precision=lax.Precision.HIGHEST,
        preferred_element_type=f32,
    )
    mod_width = modulate_bias.shape[0]
    grad_modulate_bias = jnp.sum(
        lax.dynamic_slice_in_dim(mod_grad, d * mod_width, mod_width, 1), axis=0
    )
    shape = (local, utts, width)
    return (
        layer_out.reshape(shape),
        grad_frames.reshape(shape),
        grad_skip.reshape(shape),
        grad_skip_weight,
        grad_qkv_weight,
        grad_output_weight,
        grad_up_weight,
        grad_up_bias,
        grad_down_weight,
        grad_down_bias,
        grad_modulate_weight,
        grad_modulate_bias,
    )


def solution(mesh):
    rows_two = P("seq", "batch", None)
    owned = P(ALL, None)
    vector = P(ALL)
    in_specs = (
        rows_two,
        rows_two,
        P("batch"),
        P("batch"),
        owned,
        owned,
        owned,
        owned,
        vector,
        owned,
        vector,
        owned,
        vector,
        rows_two,
    )
    out_specs = (
        rows_two,
        rows_two,
        rows_two,
        owned,
        owned,
        owned,
        owned,
        vector,
        owned,
        vector,
        owned,
        vector,
    )
    sizes = (mesh.shape["batch"], mesh.shape["seq"])
    return jax.shard_map(
        functools.partial(body, sizes),
        mesh=mesh,
        in_specs=in_specs,
        out_specs=out_specs,
        check_vma=False,
    )
```

```python
import functools
import math

import jax
import jax.numpy as jnp
from jax import lax
from jax.experimental import pallas as pl
from jax.experimental.pallas import tpu as pltpu
from jax.sharding import PartitionSpec as P

HEADS = 16
HEAD_DIM = 64
epsilon = 1e-06
masked_score = -1e30
f32 = jnp.float32
bf16 = jnp.bfloat16
ALL = ("batch", "seq")


def rms_norm(values):
    return values * lax.rsqrt(jnp.mean(values * values, axis=-1, keepdims=True) + epsilon)


def modulated(hidden, scale_rows, shift_rows):
    return rms_norm(hidden) * (1.0 + scale_rows) + shift_rows


def gelu_tanh(pre_values):
    return jax.nn.gelu(pre_values, approximate=True)


def time_embed(flow_times, embed_width):
    half_width = embed_width // 2
    frequency = jnp.exp(-math.log(10000.0) * jnp.arange(half_width, dtype=f32) / half_width)
    angles = 1000.0 * flow_times[:, None] * frequency[None, :]
    return jnp.concatenate([jnp.sin(angles), jnp.cos(angles)], axis=-1)


def params(semantics=None):
    return pltpu.CompilerParams(dimension_semantics=semantics, vmem_limit_bytes=60 * 1024 * 1024)


class Net:
    def __init__(self, batch, seq):
        self.batch, self.seq, self.n = batch, seq, batch * seq
        self.d = lax.axis_index("batch") * seq + lax.axis_index("seq")
        self.b = lax.axis_index("batch")
        self.s = lax.axis_index("seq")
        self.core = self.d & 1

    def swap(self, value, offset):
        return lax.ppermute(value, ALL, [(i, i ^ offset) for i in range(self.n)])

    def swap_by_core(self, value, even, odd):
        pairs = [(i, i ^ (odd if i & 1 else even)) for i in range(self.n)]
        return lax.ppermute(value, ALL, pairs)

    def sum_all(self, value):
        bit = 1
        while bit < self.n:
            value = value + self.swap(value, bit)
            bit *= 2
        return value


def cost(flops, moved, exps=0):
    return pl.CostEstimate(flops=int(flops), bytes_accessed=int(moved), transcendentals=int(exps))


def after(value, *others):
    return lax.optimization_barrier((value,) + tuple(others))[0]


def gate(*values):
    return lax.optimization_barrier(values)


def place(pieces, tables, count, columns=None):
    rows, width = pieces[0].shape[1:]
    columns = columns or (width,)
    counts = [p.shape[0] for p in pieces]
    total = sum(counts)
    table = jnp.concatenate(tables, axis=-1).astype(jnp.int32)
    if table.ndim == 1:
        table = jnp.broadcast_to(table[None], (len(columns), total))

    def kernel(table_ref, *refs):
        sources = refs[: len(pieces)]
        outs = refs[len(pieces) : len(pieces) + len(columns)]
        sems = refs[-1]
        copies = []
        at = 0
        for source, number in zip(sources, counts):
            for j in range(number):
                left = 0
                for o, wide in enumerate(columns):
                    copies.append(
                        pltpu.make_async_copy(
                            source.at[j, :, pl.ds(left, wide)],
                            outs[o].at[table_ref[o, at]],
                            sems.at[o, at],
                        )
                    )
                    left += wide
                at += 1
        for copy in copies:
            copy.start()
        for copy in copies:
            copy.wait()

    any_spec = pl.BlockSpec(memory_space=pl.ANY)
    outs = pl.pallas_call(
        kernel,
        out_shape=[jax.ShapeDtypeStruct((count, rows, wide), pieces[0].dtype) for wide in columns],
        in_specs=[pl.BlockSpec(memory_space=pltpu.SMEM)] + [any_spec] * len(pieces),
        out_specs=[pl.BlockSpec(memory_space=pltpu.VMEM)] * len(columns),
        scratch_shapes=[pltpu.SemaphoreType.DMA((len(columns), total))],
        compiler_params=params(),
        cost_estimate=cost(0, 4 * count * rows * width),
    )(table, *pieces)
    return [out.reshape(count * rows, wide) for out, wide in zip(outs, columns)]


class Gather:
    def __init__(self, net, shard, received=None):
        self.net = net
        received = received or [net.swap(shard, k << 3) for k in (1, 2, 3)]
        self.near = jnp.stack([shard] + list(received))

    def far(self):
        self.half = jnp.concatenate([self.near, self.net.swap_by_core(self.near, 2, 4)])
        self.mate_half = self.net.swap(self.half, 1)

    def last(self):
        self.other = self.net.swap_by_core(self.half, 4, 2)

    def mates(self):
        self.mate_other = self.net.swap(self.other, 1)

    def blocks(self):
        d = self.net.d
        z = jnp.arange(4, dtype=jnp.int32) << 3
        second = jnp.where(self.net.core == 0, 2, 4)
        third = 6 - second
        own = jnp.concatenate([d ^ z, d ^ z ^ second])
        mate = d ^ 1
        mate_own = jnp.concatenate([mate ^ z, mate ^ z ^ third])
        return (
            [self.half, self.other, self.mate_half, self.mate_other],
            [own, own ^ third, mate_own, mate_own ^ second],
        )


def grad_blocks(net, lefts, rights, segments, packed_rows, turns=None):
    depth = lefts[0].shape[0]
    tile = 1024
    piece = 32
    chip = net.d >> 1
    rel = jnp.arange(16, dtype=jnp.int32) ^ chip
    x_bit, y_bit, z = rel & 1, (rel >> 1) & 1, rel >> 2
    even = y_bit * 8 + x_bit * 4 + z
    odd = x_bit * 8 + y_bit * 4 + z
    mine = jnp.where(net.core == 0, even, odd)
    other = jnp.where(net.core == 0, odd, even)
    extra = jnp.stack([net.core] + (turns or [net.core * 0] * len(segments)))
    extra = jnp.pad(extra, (0, 16 - extra.shape[0]))
    table = jnp.stack([mine, other, extra]).astype(jnp.int32)
    starts = [0]
    for seg in segments:
        starts.append(starts[-1] + seg[0])
    steps = starts[-1]
    number = len(segments)

    def kernel(table_ref, *refs):
        left_refs, right_refs = refs[:number], refs[number : 2 * number]
        keep, send, scratch, sems = refs[2 * number :]
        t = pl.program_id(0)
        slot = t % 2
        core = table_ref[2, 0]

        def copy(v, p, at_slot, source_row, pos, dest_row):
            dest = send if p else keep
            return pltpu.make_async_copy(
                scratch.at[at_slot, pl.ds(pl.multiple_of(source_row, piece), piece)],
                dest.at[pos, pl.ds(pl.multiple_of(dest_row, piece), piece)],
                sems.at[at_slot, p, v],
            )

        def wait_slot(at_slot):
            for v in range(16):
                for p in range(2):
                    copy(v, p, at_slot, 0, 0, 0).wait()

        @pl.when(t >= 2)
        def _():
            wait_slot(slot)

        left, right = left_refs[-1][...], right_refs[-1][...]
        for i in range(number - 2, -1, -1):
            early = t < starts[i + 1]
            left = jnp.where(early, left_refs[i][...], left)
            right = jnp.where(early, right_refs[i][...], right)
        scratch[slot] = lax.dot_general(
            left, right, (((0,), (0,)), ((), ())), preferred_element_type=f32
        ).astype(bf16)
        for v in range(16):
            for p in range(2):
                side = core ^ p
                chip_at = source = dest_row = jnp.int32(0)
                for i, (_, subs, base, rise) in reversed(list(enumerate(segments))):
                    local = t - starts[i]
                    here = (
                        (local * (16 // subs) % 16 + v // subs) ^ table_ref[2, 1 + i],
                        (2 * (v // subs) + side) * subs * piece + (v % subs) * piece,
                        base + local * rise + (v % subs) * piece,
                    )
                    if i == number - 1:
                        chip_at, source, dest_row = here
                    else:
                        early = t < starts[i + 1]
                        chip_at = jnp.where(early, here[0], chip_at)
                        source = jnp.where(early, here[1], source)
                        dest_row = jnp.where(early, here[2], dest_row)
                copy(v, p, slot, source, table_ref[p, chip_at], dest_row).start()

        @pl.when(t == steps - 1)
        def _():
            wait_slot(slot)
            if steps > 1:
                wait_slot(1 - slot)

    def spec(array, i):
        count = array.shape[1] // tile
        if count == 1:
            return pl.BlockSpec((depth, tile), lambda t, table: (0, 0))
        return pl.BlockSpec(
            (depth, tile), lambda t, table: (0, jnp.clip(t - starts[i], 0, count - 1))
        )

    any_spec = pl.BlockSpec(memory_space=pl.ANY)
    shape = jax.ShapeDtypeStruct((16, packed_rows, tile), bf16)
    return pl.pallas_call(
        kernel,
        out_shape=[shape, shape],
        grid_spec=pltpu.PrefetchScalarGridSpec(
            num_scalar_prefetch=1,
            grid=(steps,),
            in_specs=[spec(a, i) for i, a in enumerate(lefts)]
            + [spec(a, i) for i, a in enumerate(rights)],
            out_specs=[any_spec, any_spec],
            scratch_shapes=[
                pltpu.VMEM((2, tile, tile), bf16),
                pltpu.SemaphoreType.DMA((2, 2, 16)),
            ],
        ),
        compiler_params=params(("arbitrary",)),
        cost_estimate=cost(2 * steps * depth * tile * tile, 3 * steps * tile * tile * 2),
    )(table, *lefts, *rights)


def total(*parts):
    result = parts[0].astype(f32)
    for part in parts[1:]:
        result = result + part.astype(f32)
    return result


class Scatter:
    def __init__(self, net, keep, send):
        self.net, self.parts = net, [keep]
        self.parts.append(net.swap(send, 1))

    def halve(self, low, high, even, odd):
        out = total(*[p[low:high] for p in self.parts]).astype(bf16)
        self.out = out
        self.pair = (even, odd)
        return out

    def push(self, out):
        self.parts.append(self.net.swap_by_core(out, *self.pair))

    def z_sums(self):
        self.outs = [total(*[p[k : k + 1] for p in self.parts]).astype(bf16) for k in (1, 2, 3)]
        return self.outs

    def z_push(self):
        self.zs = [self.net.swap(o, (k + 1) << 3) for k, o in enumerate(self.outs)]

    def finish(self):
        return total(*[p[0:1] for p in self.parts], *self.zs)[0]


class UtteranceRows:
    def __init__(self, net, row):
        self.net, self.parts = net, [row] + [net.swap(row, k) for k in (1, 2, 3)]

    def across_z(self):
        row = sum(self.parts[1:], self.parts[0])
        self.parts = [row] + [self.net.swap(row, k << 3) for k in (1, 2, 3)]

    def across_y(self):
        self.parts = [jnp.concatenate(self.parts)]
        self.parts.append(self.net.swap(self.parts[0], 4))

    def rows(self):
        return jnp.stack(self.parts, axis=1).reshape(8, self.parts[0].shape[1])


def spread_columns(parts, order, groups):
    rows, width = parts[0].shape
    number = len(parts)
    wide = width // groups

    def kernel(order_ref, *refs):
        out, sems = refs[number:]
        copies = []
        for i in range(number):
            for g in range(groups):
                at = pl.multiple_of((order_ref[i] + g * number) * wide, wide)
                copies.append(
                    pltpu.make_async_copy(
                        refs[i].at[:, pl.ds(g * wide, wide)],
                        out.at[:, pl.ds(at, wide)],
                        sems.at[i, g],
                    )
                )
        for copy in copies:
            copy.start()
        for copy in copies:
            copy.wait()

    return pl.pallas_call(
        kernel,
        out_shape=jax.ShapeDtypeStruct((rows, width * number), parts[0].dtype),
        in_specs=[pl.BlockSpec(memory_space=pltpu.SMEM)]
        + [pl.BlockSpec(memory_space=pltpu.VMEM)] * number,
        out_specs=pl.BlockSpec(memory_space=pltpu.VMEM),
        scratch_shapes=[pltpu.SemaphoreType.DMA((number, groups))],
        compiler_params=params(),
        cost_estimate=cost(0, 8 * rows * width * number),
    )(order.astype(jnp.int32), *parts)


def rope(values, cosine, sine, back):
    width = values.shape[-1]
    lane = lax.broadcasted_iota(jnp.int32, values.shape, 1)
    early = (lane & (HEAD_DIM - 1)) < HEAD_DIM // 2
    source = values * sine if back else values
    ahead = pltpu.roll(source, width - HEAD_DIM // 2, 1)
    behind = pltpu.roll(source, HEAD_DIM // 2, 1)
    if back:
        turned = jnp.where(early, ahead, -behind)
        return values * cosine + turned
    turned = jnp.where(early, -ahead, behind)
    return values * cosine + turned * sine


def wide_tables(cos_ref, sin_ref, width):
    reps = width // cos_ref.shape[-1]
    cosine = jnp.concatenate([cos_ref[...]] * reps, axis=-1)
    sine = jnp.concatenate([sin_ref[...]] * reps, axis=-1)
    return cosine, sine


def qkv_kernel(number, *refs):
    w_ref, cos_ref, sin_ref, q_ref, k_ref, v_ref = refs[number:]
    width = q_ref.shape[-1]
    scale = HEAD_DIM ** (-0.5)
    for i in range(number):

        @pl.when(pl.program_id(0) == i)
        def _():
            result = jnp.dot(refs[i][...], w_ref[...], preferred_element_type=f32)
            cosine, sine = wide_tables(cos_ref, sin_ref, width)
            q_ref[...] = (rope(result[:, :width], cosine, sine, False) * scale).astype(bf16)
            k_ref[...] = rope(result[:, width : 2 * width], cosine, sine, False).astype(bf16)
            v_ref[...] = result[:, 2 * width :].astype(bf16)


def qkv_project(parts, w, cosine, sine):
    block, depth = parts[0].shape
    rows = block * len(parts)
    width = w.shape[1] // 3
    row = lambda wide: pl.BlockSpec((block, wide), lambda i: (i, 0))
    whole = lambda a: pl.BlockSpec(a.shape, lambda i: (0, 0))
    return pl.pallas_call(
        functools.partial(qkv_kernel, len(parts)),
        grid=(len(parts),),
        out_shape=[jax.ShapeDtypeStruct((rows, width), bf16)] * 3,
        in_specs=[whole(a) for a in parts] + [whole(w), row(128), row(128)],
        out_specs=[row(width)] * 3,
        compiler_params=params(("arbitrary",)),
        cost_estimate=cost(2 * rows * depth * 3 * width, 2 * rows * (depth + 3 * width)),
    )(*parts, w, cosine, sine)


def qkv_back(pieces, w, local, first, dtype):
    rows = pieces[0].shape[0]
    wide = pieces[0].shape[1]
    count = rows // local // 2
    width = len(pieces) * wide

    def kernel(*refs):
        w_ref, all_ref, out_ref = refs[len(pieces) :]
        joined = jnp.concatenate([r[...] for r in refs[: len(pieces)]], axis=-1)
        all_ref[...] = joined
        out_ref[...] = lax.dot_general(
            joined, w_ref[...], (((1,), (1,)), ((), ())), preferred_element_type=f32
        ).astype(dtype)

    return pl.pallas_call(
        kernel,
        grid=(count,),
        out_shape=[
            jax.ShapeDtypeStruct((count * local, width), bf16),
            jax.ShapeDtypeStruct((count * local, w.shape[0]), dtype),
        ],
        in_specs=[pl.BlockSpec((local, wide), lambda i: (2 * i + first, 0))] * len(pieces)
        + [pl.BlockSpec(w.shape, lambda i: (0, 0))],
        out_specs=[
            pl.BlockSpec((local, width), lambda i: (i, 0)),
            pl.BlockSpec((local, w.shape[0]), lambda i: (i, 0)),
        ],
        compiler_params=params(("arbitrary",)),
        cost_estimate=cost(2 * count * local * width * w.shape[0], 8 * count * local * w.shape[0]),
    )(*pieces, w)


def qkv_grad_blocks(net, lefts, grads):
    local, depth = lefts[0].shape
    width = grads[0].shape[1]
    rows = depth // 8
    t = jnp.arange(8, dtype=jnp.int32)
    table = net.b ^ ((t & 3) << 1) ^ jnp.where(t < 4, 1, 0)
    number = len(lefts)

    def kernel(table_ref, *refs):
        keep, send = refs[number + len(grads) :]
        result = jnp.zeros((rows, width), f32)
        for i in range(number):
            grad = refs[number + i % 2][(i // 2) * local : (i // 2 + 1) * local]
            result = result + lax.dot_general(
                refs[i][...], grad, (((0,), (0,)), ((), ())), preferred_element_type=f32
            )
        result = result.astype(bf16)[None]
        step = pl.program_id(0)

        @pl.when(step < 4)
        def _():
            send[...] = result

        @pl.when(step >= 4)
        def _():
            keep[...] = result

    shape = jax.ShapeDtypeStruct((4, rows, width), bf16)
    block = (1, rows, width)
    return pl.pallas_call(
        kernel,
        out_shape=[shape, shape],
        grid_spec=pltpu.PrefetchScalarGridSpec(
            num_scalar_prefetch=1,
            grid=(8,),
            in_specs=[pl.BlockSpec((local, rows), lambda i, t: (0, t[i]))] * number
            + [pl.BlockSpec(g.shape, lambda i, t: (0, 0)) for g in grads],
            out_specs=[
                pl.BlockSpec(block, lambda i, t: (jnp.maximum(i - 4, 0), 0, 0)),
                pl.BlockSpec(block, lambda i, t: (jnp.minimum(i, 3), 0, 0)),
            ],
        ),
        compiler_params=params(("arbitrary",)),
        cost_estimate=cost(2 * number * local * depth * width, 4 * depth * width),
    )(table, *lefts, *grads)


def attend_kernel(heads, q_ref, k_ref, v_ref, bias_ref, o_ref, lse_ref):
    q = q_ref[...]
    k = k_ref[...]
    v = v_ref[...]
    bias = bias_ref[...]
    lane = lax.broadcasted_iota(jnp.int32, q.shape, 1) // HEAD_DIM
    spot = lax.broadcasted_iota(jnp.int32, lse_ref.shape, 1)
    out = jnp.zeros(q.shape, f32)
    lse = jnp.zeros(lse_ref.shape, f32)
    for h in range(heads):
        mine = lane == h
        qh = jnp.where(mine, q, jnp.zeros_like(q))
        s = lax.dot_general(qh, k, (((1,), (1,)), ((), ())), preferred_element_type=f32) + bias
        top = jnp.max(s, axis=-1, keepdims=True)
        p = jnp.exp(s - top)
        total = jnp.sum(p, axis=-1, keepdims=True)
        o = jnp.dot(p.astype(bf16), v, preferred_element_type=f32) / total
        out = jnp.where(mine, o, out)
        lse = jnp.where(spot == h, top + jnp.log(total), lse)
    o_ref[...] = out.astype(bf16)
    lse_ref[...] = lse


def attend(q, k, v, bias, heads):
    rows, width = q.shape
    block = 256
    row = lambda wide: pl.BlockSpec((block, wide), lambda i: (i, 0))
    whole = pl.BlockSpec((rows, width), lambda i: (0, 0))
    return pl.pallas_call(
        functools.partial(attend_kernel, heads),
        grid=(rows // block,),
        out_shape=[jax.ShapeDtypeStruct((rows, width), bf16), jax.ShapeDtypeStruct((rows, 128), f32)],
        in_specs=[row(width), whole, whole, pl.BlockSpec((1, rows), lambda i: (0, 0))],
        out_specs=[row(width), row(128)],
        compiler_params=params(("arbitrary",)),
        cost_estimate=cost(
            16 * rows * rows * heads * HEAD_DIM, 8 * rows * width, rows * rows * heads
        ),
    )(q, k, v, bias)


def attend_back_kernel(
    heads,
    first,
    q_ref,
    do_ref,
    o_ref,
    lse_ref,
    k_ref,
    v_ref,
    kt_ref,
    bias_ref,
    cosq_ref,
    sinq_ref,
    cosk_ref,
    sink_ref,
    dq_ref,
    dk_ref,
    dv_ref,
    p_all,
    ds_all,
    dk_acc,
    dv_acc,
):
    step = pl.program_id(0)
    q = q_ref[...]
    do = do_ref[...]
    k = k_ref[...]
    v = v_ref[...]
    block, width = q.shape
    lane = lax.broadcasted_iota(jnp.int32, q.shape, 1) // HEAD_DIM
    product = (do.astype(f32) * o_ref[...].astype(f32)).T
    lse_t = lse_ref[...].T
    bias = bias_ref[...]
    contract = (((1,), (1,)), ((), ()))
    q_parts, do_parts, dq_parts = [], [], []
    for h in range(heads):
        mine = lane == h
        qh = jnp.where(mine, q, jnp.zeros_like(q))
        doh = jnp.where(mine, do, jnp.zeros_like(do))
        q_parts.append(qh)
        do_parts.append(doh)
        row_dot = jnp.sum(product[h * HEAD_DIM : (h + 1) * HEAD_DIM], axis=0, keepdims=True)
        s = lax.dot_general(k, qh, contract, preferred_element_type=f32)
        p = jnp.exp(s + bias - lse_t[first + h : first + h + 1])
        dp = lax.dot_general(v, doh, contract, preferred_element_type=f32)
        ds = (p * (dp - row_dot)).astype(bf16)
        p_all[:, h * block : (h + 1) * block] = p.astype(bf16)
        ds_all[:, h * block : (h + 1) * block] = ds
        dq_parts.append(
            jnp.dot(kt_ref[h * HEAD_DIM : (h + 1) * HEAD_DIM, :], ds, preferred_element_type=f32)
        )
    dv = jnp.dot(p_all[...], jnp.concatenate(do_parts, axis=0), preferred_element_type=f32)
    dk = jnp.dot(ds_all[...], jnp.concatenate(q_parts, axis=0), preferred_element_type=f32)

    @pl.when(step == 0)
    def _():
        dv_acc[...] = dv
        dk_acc[...] = dk

    @pl.when(step > 0)
    def _():
        dv_acc[...] += dv
        dk_acc[...] += dk

    dq = jnp.concatenate(dq_parts, axis=0).T
    cosine, sine = wide_tables(cosq_ref, sinq_ref, width)
    dq_ref[...] = (rope(dq, cosine, sine, True) * (HEAD_DIM ** (-0.5))).astype(bf16)

    @pl.when(step == pl.num_programs(0) - 1)
    def _():
        cosine, sine = wide_tables(cosk_ref, sink_ref, width)
        dk_ref[...] = rope(dk_acc[...], cosine, sine, True).astype(bf16)
        dv_ref[...] = dv_acc[...].astype(bf16)


def attend_back(q, k, v, o, do, lse, k_turned, bias, cosine, sine, heads, group):
    rows = q.shape[0]
    width = heads * HEAD_DIM
    block = 256
    lanes = lambda wide: pl.BlockSpec((block, wide), lambda i: (i, group))
    row = lambda wide: pl.BlockSpec((block, wide), lambda i: (i, 0))
    whole = lambda wide, at: pl.BlockSpec((rows, wide), lambda i: (0, at))
    out = jax.ShapeDtypeStruct((rows, width), bf16)
    return pl.pallas_call(
        functools.partial(attend_back_kernel, heads, group * heads),
        grid=(rows // block,),
        out_shape=[out] * 3,
        in_specs=[
            lanes(width),
            lanes(width),
            lanes(width),
            row(128),
            whole(width, group),
            whole(width, group),
            pl.BlockSpec((width, rows), lambda i: (group, 0)),
            whole(block, 0),
            row(128),
            row(128),
            whole(128, 0),
            whole(128, 0),
        ],
        out_specs=[row(width), whole(width, 0), whole(width, 0)],
        scratch_shapes=[
            pltpu.VMEM((rows, heads * block), bf16),
            pltpu.VMEM((rows, heads * block), bf16),
            pltpu.VMEM((rows, width), f32),
            pltpu.VMEM((rows, width), f32),
        ],
        compiler_params=params(("arbitrary",)),
        cost_estimate=cost(
            40 * rows * rows * heads * HEAD_DIM, 16 * rows * width, rows * rows * heads
        ),
    )(
        q,
        do,
        o,
        lse,
        k,
        v,
        k_turned,
        bias,
        cosine,
        sine,
        cosine,
        sine,
    )


def body(
    mesh_sizes,
    frames_in,
    skip_in,
    flow_times,
    lengths,
    skip_weight,
    qkv_weight,
    output_weight,
    up_weight,
    up_bias,
    down_weight,
    down_bias,
    modulate_weight,
    modulate_bias,
    output_grad,
):
    batch, seq = mesh_sizes
    net = Net(batch, seq)
    n, d, s = net.n, net.d, net.s
    local, utts, width = frames_in.shape
    frames = frames_in.reshape(local, width)
    skips = skip_in.reshape(local, width)
    out_grad = output_grad.reshape(local, width).astype(f32)
    heads = HEADS // seq
    part = heads * HEAD_DIM
    rows = local * seq
    built = n == 32 and seq == 4
    wrow = width // n
    ff = up_weight.shape[1]

    seq_order = s ^ jnp.arange(seq, dtype=jnp.int32)
    by_part = qkv_weight.reshape(wrow, 3, seq, part)
    pieces = [
        lax.dynamic_index_in_dim(by_part, s ^ k, 2, keepdims=False).reshape(wrow, 3 * part)
        for k in range(seq)
    ]
    urow, drow = up_bias.shape[0], down_bias.shape[0]
    if built:
        vectors = jnp.concatenate(
            [
                up_bias.reshape(1, urow),
                jnp.pad(down_bias, (0, urow - drow)).reshape(1, urow),
                jnp.zeros((wrow - 2, urow), bf16),
            ]
        )
        pieces = [jnp.concatenate([p, vectors], axis=1) for p in pieces]
    pieces = [p if k == 0 else net.swap(p, k) for k, p in enumerate(pieces)]
    if built:
        skip_gather = Gather(net, skip_weight)
        skip_gather.far()
        skip_gather.last()
        qkv_four = after(jnp.stack(pieces), skip_gather.other)
        qkv_far = [net.swap(qkv_four, k << 3) for k in (1, 2, 3)]
        skip_gather.mates()
        (full_skip,) = place(*skip_gather.blocks(), n)
        ou = jnp.concatenate([output_weight, up_weight], axis=1)
    else:
        gather = lambda w, ax: lax.all_gather(w, ax, axis=0, tiled=True)
        full_skip = gather(skip_weight, ALL)
        full_qkv = gather(jnp.stack(pieces)[seq_order], "batch")
        full_qkv = full_qkv.reshape(batch, seq, wrow, 3 * part)
        full_qkv = full_qkv.reshape(width, 3 * part)
        full_output = gather(output_weight, ALL).reshape(seq, width // seq, width)[seq_order]
        full_output = full_output.reshape(width, width)
        full_up = gather(up_weight, ALL)
        full_down = gather(down_weight, ALL)

    mod_bias = lax.dynamic_update_slice_in_dim(
        jnp.zeros((6 * width,), f32), modulate_bias.astype(f32), d * modulate_bias.shape[0], 0
    )
    if built:
        times = jnp.broadcast_to(flow_times.reshape(1, 1), (8, 128))
        times = [times] + [net.swap(times, k << 3) for k in (1, 2, 3)]
        *times, _ = gate(*times, skip_gather.half)
        times = jnp.concatenate([t[:1] for t in times] * 2)
        times = jnp.stack([times[:4], net.swap(times, 4)[:4]], axis=1).reshape(batch, 128)
        all_times = times[:, 0]
    else:
        small = jnp.concatenate([up_bias.astype(f32), down_bias.astype(f32), flow_times])
        small_width = -(-small.shape[0] // 128) * 128
        small = jnp.pad(small, (0, small_width - small.shape[0]))
        slots = lax.broadcasted_iota(jnp.int32, (n, small_width), 0)
        small = net.sum_all(jnp.where(slots == d, small[None], 0.0))
        full_up_bias = small[:, :urow].reshape(1, ff)
        full_down_bias = small[:, urow : urow + drow].reshape(1, width)
        all_times = small.reshape(batch, seq, small_width)[:, 0, urow + drow]
    feat = jax.nn.silu(time_embed(all_times, width)).astype(bf16)
    feat_own = lax.dynamic_slice_in_dim(feat, d * wrow, wrow, 1)
    modulation = jnp.dot(feat_own, modulate_weight, preferred_element_type=f32)
    modulation = modulation + mod_bias[None]
    if built:
        sums = modulation[0:2]
        for k in (1, 2, 3):
            sums = sums + net.swap(modulation[2 * k : 2 * k + 2], k << 3)
        sums = sums[0:1] + net.swap(sums[1:2], 4)
        modulation = sums
        for k in (1, 2, 3):
            modulation = modulation + net.swap(sums, k)
    else:
        bit = batch // 2
        while bit:
            high = (net.b & bit) // bit
            sent = lax.dynamic_slice_in_dim(modulation, (1 - high) * bit, bit, 0)
            kept = lax.dynamic_slice_in_dim(modulation, high * bit, bit, 0)
            modulation = kept + net.swap(sent, bit * seq)
            bit //= 2
        bit = 1
        while bit < seq:
            modulation = modulation + net.swap(modulation, bit)
            bit *= 2
    shift_one, scale_one, gate_one, shift_two, scale_two, gate_two = jnp.split(modulation, 6, -1)

    half_dim = HEAD_DIM // 2
    inverse = jnp.exp(-math.log(10000.0) * 2.0 * jnp.arange(half_dim, dtype=f32) / HEAD_DIM)
    positions = (
        seq_order[:, None] * local + jnp.arange(local, dtype=jnp.int32)[None]
    ).reshape(rows)
    angles = positions.astype(f32)[:, None] * jnp.tile(inverse, 128 // half_dim)[None]
    cosine, sine = jnp.cos(angles), jnp.sin(angles)
    key_bias = jnp.where(positions < lengths[0], 0.0, masked_score).astype(f32)[None]

    joined = jnp.concatenate([frames, skips], axis=-1)
    hidden_zero = jnp.dot(joined, full_skip, preferred_element_type=f32)
    normed_one = modulated(hidden_zero, scale_one, shift_one).astype(bf16)
    if built:
        normed_one, ou, *qkv_far = gate(normed_one, ou, *qkv_far)
        qkv_z = jnp.concatenate([qkv_four] + qkv_far)
        qkv_y = net.swap(qkv_z, 4)
        ou_gather = Gather(net, ou)
        k16 = jnp.arange(16, dtype=jnp.int32)
        z_spots = d ^ (((k16 >> 2) << 3) | (k16 & 3))
        full_qkv, vectors = place(
            [qkv_z, qkv_y], [z_spots, z_spots ^ 4], n, (3 * part, urow)
        )
    across = {0: normed_one}
    bit = seq // 2
    while bit:
        across.update({i | bit: net.swap(a, bit) for i, a in list(across.items())})
        if built and bit == 2:
            across[2], cosine, sine, full_qkv, ou_gather.near, down_own = gate(
                across[2], cosine, sine, full_qkv, ou_gather.near, down_weight
            )
            down_near = [net.swap(down_own, k << 3) for k in (1, 2, 3)]
        bit //= 2
    normed_parts = [across[i] for i in range(seq)]
    if built:
        ou_gather.far()
        vectors = vectors.reshape(n, wrow, urow)
        full_up_bias = vectors[:, 0].reshape(1, ff).astype(f32)
        full_down_bias = vectors[:, 1, :drow].reshape(1, width).astype(f32)
    q, k, v = qkv_project(normed_parts, full_qkv, cosine, sine)
    if built:
        q, ou_gather.half = gate(q, ou_gather.half)
        ou_gather.last()
    att, lse = attend(q, k, v, key_bias, heads)
    if built:
        att, ou_gather.other, ou_gather.mate_half, *down_near = gate(
            att, ou_gather.other, ou_gather.mate_half, *down_near
        )
        down_gather = Gather(net, down_own, down_near)
        down_gather.far()
        ou_gather.mates()
        got, spots = ou_gather.blocks()
        spots = jnp.concatenate(spots)
        turned = spots ^ (s * (n // seq))
        full_output, full_up = place(got, [jnp.stack([turned, spots])], n, (width, ff))
    blocks = [att[i * local : (i + 1) * local] for i in range(seq)]
    k_turned = k.T
    bias_wide = jnp.broadcast_to(key_bias.reshape(rows, 1), (rows, 256))
    blocks = [b if i == 0 else net.swap(b, i) for i, b in enumerate(blocks)]
    *blocks, full_output, full_up, k_turned, bias_wide = gate(
        *blocks, full_output, full_up, k_turned, bias_wide
    )
    attended = jnp.concatenate(blocks, axis=-1)
    if built:
        down_gather.half = after(down_gather.half, attended)
        down_gather.last()
    attn_proj = jnp.dot(attended, full_output, preferred_element_type=f32)
    hidden_one = hidden_zero + gate_one * attn_proj
    normed_two = modulated(hidden_one, scale_two, shift_two).astype(bf16)
    pre_act = jnp.dot(normed_two, full_up, preferred_element_type=f32) + full_up_bias
    activated = gelu_tanh(pre_act).astype(bf16)
    if built:
        down_gather.other, down_gather.mate_half, activated = gate(
            down_gather.other, down_gather.mate_half, activated
        )
        down_gather.mates()
        (full_down,) = place(*down_gather.blocks(), n)
    ffn_out = jnp.dot(activated, full_down, preferred_element_type=f32) + full_down_bias
    layer_out = (hidden_one + gate_two * ffn_out).astype(bf16)

    rows_dot = lambda a, b: lax.dot_general(
        a, b, (((0,), (0,)), ((), ())), preferred_element_type=f32
    )
    back_dot = lambda a, b: lax.dot_general(
        a, b, (((1,), (1,)), ((), ())), preferred_element_type=f32
    )

    def scattered(grads, turn=False):
        if turn:
            grads = grads.reshape(seq, width // seq, -1)[seq_order].reshape(grads.shape)
        return lax.psum_scatter(
            grads.astype(bf16), ALL, scatter_dimension=0, tiled=True
        ).astype(f32)

    ffn_grad = out_grad * gate_two
    down_bias_term = jnp.sum(ffn_grad, axis=0)
    ffn_grad_low = ffn_grad.astype(bf16)
    act_grad = back_dot(ffn_grad_low, full_down)
    pre_grad = jax.vjp(gelu_tanh, pre_act)[1](act_grad)[0]
    up_bias_term = jnp.sum(pre_grad, axis=0)
    pre_grad_low = pre_grad.astype(bf16)
    normed_two_grad = back_dot(pre_grad_low, full_up)
    pull_two = jax.vjp(modulated, hidden_one, scale_two, shift_two)[1]
    hidden_grad_two, scale_two_grad, shift_two_grad = pull_two(normed_two_grad)
    gate_two_grad = jnp.sum(out_grad * ffn_out, axis=0)
    hidden_one_grad = out_grad + hidden_grad_two
    gate_one_grad = jnp.sum(hidden_one_grad * attn_proj, axis=0)
    proj_grad_low = (hidden_one_grad * gate_one).astype(bf16)
    attended_grad = back_dot(proj_grad_low, full_output).astype(bf16)
    pieces = [attended_grad[:, i * part : (i + 1) * part] for i in range(seq)]
    grad_all = jnp.concatenate([p if i == 0 else net.swap(p, i) for i, p in enumerate(pieces)])
    pair = lambda i, grad: attend_back(
        q, k, v, att, grad, lse, k_turned, bias_wide, cosine, sine, 2, i
    )
    if built:
        early_row = jnp.concatenate(
            [
                v.reshape(1, -1)
                for v in (
                    gate_one_grad,
                    shift_two_grad,
                    scale_two_grad,
                    gate_two_grad,
                    up_bias_term,
                    down_bias_term,
                )
            ],
            axis=1,
        )
        activated, attended_grad = lax.optimization_barrier((activated, attended_grad))
        down = Scatter(net, *grad_blocks(net, [activated], [ffn_grad_low], [(4, 4, 0, 0)], 128))
        normed_two = after(normed_two, down.parts[0])
        up = Scatter(
            net,
            *grad_blocks(
                net,
                [normed_two, attended],
                [pre_grad_low, proj_grad_low],
                [(4, 1, 0, 32), (1, 1, 128, 0)],
                160,
                [s * 0, s * (n // seq // 2)],
            ),
        )
        down_half = down.halve(8, 16, 4, 2)
        down.push(down_half)
        grad_all, down_half, early_row, _ = lax.optimization_barrier(
            (grad_all, down_half, early_row, up.parts[0])
        )
        early = UtteranceRows(net, early_row)
        first = pair(0, grad_all)
        up.parts[1], down.parts[2], first, *early.parts = gate(
            up.parts[1], down.parts[2], first, *early.parts
        )
        early.across_z()
        up_half = up.halve(8, 16, 4, 2)
        up.push(up_half)
        down_half = down.halve(4, 8, 2, 4)
        down.push(down_half)
        grad_all, _ = gate(grad_all, (up_half, down_half, first))
        second = pair(1, grad_all)
        up.parts[2], down.parts[3], second = gate(up.parts[2], down.parts[3], second)
        results = [first, second]
    else:
        grad_down_weight = scattered(rows_dot(activated, ffn_grad_low))
        grad_up_weight = scattered(rows_dot(normed_two, pre_grad_low))
        grad_output_weight = scattered(rows_dot(attended, proj_grad_low), True)
        results = [pair(i, grad_all) for i in range(heads // 2)]
    pieces = [r[i] for i in range(3) for r in results]
    odd_grad, odd = qkv_back(pieces, full_qkv, local, 1, bf16)
    sent = net.swap(odd, 1)
    even_grad, even = qkv_back(pieces, full_qkv, local, 0, f32)
    halves = [
        even[i * local : (i + 1) * local] + sent[i * local : (i + 1) * local].astype(f32)
        for i in range(seq // 2)
    ]
    if built:
        give = halves[1].astype(bf16)
        taken = net.swap(give, 2)
        down.parts[2], down.parts[3], give = gate(down.parts[2], down.parts[3], give)
        down_sums = down.z_sums()
        down.z_push()
        *normed_parts, _, _ = gate(*normed_parts, give, down_sums)
        keep, send = qkv_grad_blocks(net, normed_parts, [even_grad, odd_grad])
        got = net.swap(send, 4)
        up.parts[2], keep = gate(up.parts[2], keep)
        up_quarter = up.halve(4, 8, 2, 4)
        up.push(up_quarter)
        taken, _, *down.zs = gate(taken, up_quarter, *down.zs)
        normed_one_grad = halves[0] + taken.astype(f32)
    else:
        step = 2
        while len(halves) > 1:
            kept = halves[0::2]
            give = halves[1::2]
            halves = [
                a + net.swap(g.astype(bf16), step).astype(f32) for a, g in zip(kept, give)
            ]
            step *= 2
        normed_one_grad = halves[0]
        qkv_part = sum(
            rows_dot(a, (odd_grad if i % 2 else even_grad)[(i // 2) * local : (i // 2 + 1) * local])
            for i, a in enumerate(normed_parts)
        ).astype(bf16)
        own = lax.psum_scatter(qkv_part, "batch", scatter_dimension=0, tiled=True).astype(f32)

    pull_one = jax.vjp(modulated, hidden_zero, scale_one, shift_one)[1]
    hidden_grad_one, scale_one_grad, shift_one_grad = pull_one(normed_one_grad)
    hidden_zero_grad = (hidden_one_grad + hidden_grad_one).astype(bf16)
    if built:
        hidden_zero_grad, got = gate(hidden_zero_grad, got)
        late = UtteranceRows(
            net, jnp.concatenate([shift_one_grad.reshape(1, -1), scale_one_grad.reshape(1, -1)], axis=1)
        )
        skip = Scatter(
            net,
            *grad_blocks(
                net,
                [frames, skips],
                [hidden_zero_grad, hidden_zero_grad],
                [(1, 2, 0, 0), (1, 2, 0, 0)],
                64,
                [s * 0, s * 0 + 8],
            ),
        )
        got, skip.parts[0] = gate(got, skip.parts[0])
        qkv_sums = [total(keep[i], got[i]).astype(bf16) for i in (1, 2, 3)]
        qkv_zs = [net.swap(v, (i + 1) << 3) for i, v in enumerate(qkv_sums)]
        skip.parts[1] = after(skip.parts[1], qkv_sums)
        skip_half = skip.halve(8, 16, 4, 2)
        skip.push(skip_half)
        up.parts[3], hidden_zero_grad, skip_half, *rest = gate(
            up.parts[3], hidden_zero_grad, skip_half, *late.parts, *early.parts
        )
        late.parts, early.parts = rest[:4], rest[4:]
        up_sums = up.z_sums()
        up.z_push()
        late.across_z()
        skip.parts[2] = after(skip.parts[2], up_sums)
        skip_quarter = skip.halve(4, 8, 2, 4)
        skip.push(skip_quarter)
        *early.parts, _ = gate(*early.parts, skip_quarter)
        early.across_y()
        keep, got, skip_quarter, late.parts[0], *rest = gate(
            keep, got, skip_quarter, late.parts[0], *qkv_zs, *late.parts[1:]
        )
        qkv_zs, late.parts[1:] = rest[:3], rest[3:]
        own = total(keep[0], got[0], *qkv_zs)
        late.across_y()
    own = own.reshape(seq, wrow, 3 * part)
    cols = [lax.dynamic_index_in_dim(own, s ^ i, 0, keepdims=False) for i in range(seq)]
    cols = [c if i == 0 else net.swap(c, i) for i, c in enumerate(cols)]
    if built:
        skip.parts[3] = after(skip.parts[3], own)
        skip_sums = skip.z_sums()
        skip.z_push()
        down.parts[0] = after(down.parts[0], skip_sums)
        up.parts[0] = after(up.parts[0], skip_sums)
        grad_down_weight = down.finish()
        own = up.finish()
        grad_up_weight = jnp.concatenate(
            [own[i * wrow : (i + 1) * wrow] for i in range(4)], axis=1
        )
        grad_output_weight = own[4 * wrow :]
        grad_skip_weight = skip.finish()
    else:
        grad_skip_weight = scattered(rows_dot(joined, hidden_zero_grad))
    grad_qkv_weight = spread_columns(cols, seq_order, 3)
    grad_joined = back_dot(hidden_zero_grad, full_skip)
    grad_frames, grad_skip = grad_joined[:, :width], grad_joined[:, width:]

    def by_utterance(*vectors):
        row = jnp.concatenate([vec.reshape(1, -1) for vec in vectors], axis=1)
        place_row = lax.broadcasted_iota(jnp.int32, (batch, row.shape[1]), 0)
        return jnp.where(place_row == net.b, row, 0.0)

    if built:
        early, late = early.rows(), late.rows()
        sums = jnp.sum(early[:, 4 * width :], axis=0)
        up_sum, down_sum = sums[:ff], sums[ff:]
        early = early[:, : 4 * width]
    else:
        early = by_utterance(gate_one_grad, shift_two_grad, scale_two_grad, gate_two_grad)
        flat = jnp.concatenate([early.reshape(-1), up_bias_term, down_bias_term])
        flat = net.sum_all(flat.reshape(-1, 128)).reshape(-1)
        early = flat[: batch * 4 * width].reshape(batch, 4 * width)
        up_sum = flat[batch * 4 * width : batch * 4 * width + ff]
        down_sum = flat[batch * 4 * width + ff :]
        late = net.sum_all(by_utterance(shift_one_grad, scale_one_grad))
    grad_up_bias = lax.dynamic_slice_in_dim(up_sum, d * urow, urow, 0)
    grad_down_bias = lax.dynamic_slice_in_dim(down_sum, d * drow, drow, 0)
    mod_grad = jnp.concatenate([late, early], axis=1)
    grad_modulate_weight = lax.dot_general(
        feat_own.astype(f32),
        mod_grad,
        (((0,), (0,)), ((), ())),
        precision=lax.Precision.HIGHEST,
        preferred_element_type=f32,
    )
    mod_width = modulate_bias.shape[0]
    grad_modulate_bias = jnp.sum(
        lax.dynamic_slice_in_dim(mod_grad, d * mod_width, mod_width, 1), axis=0
    )
    shape = (local, utts, width)
    return (
        layer_out.reshape(shape),
        grad_frames.reshape(shape),
        grad_skip.reshape(shape),
        grad_skip_weight,
        grad_qkv_weight,
        grad_output_weight,
        grad_up_weight,
        grad_up_bias,
        grad_down_weight,
        grad_down_bias,
        grad_modulate_weight,
        grad_modulate_bias,
    )


def solution(mesh):
    rows_two = P("seq", "batch", None)
    owned = P(ALL, None)
    vector = P(ALL)
    in_specs = (
        rows_two,
        rows_two,
        P("batch"),
        P("batch"),
        owned,
        owned,
        owned,
        owned,
        vector,
        owned,
        vector,
        owned,
        vector,
        rows_two,
    )
    out_specs = (
        rows_two,
        rows_two,
        rows_two,
        owned,
        owned,
        owned,
        owned,
        vector,
        owned,
        vector,
        owned,
        vector,
    )
    sizes = (mesh.shape["batch"], mesh.shape["seq"])
    return jax.shard_map(
        functools.partial(body, sizes),
        mesh=mesh,
        in_specs=in_specs,
        out_specs=out_specs,
        check_vma=False,
    )
```

```python
import functools
import math

import jax
import jax.numpy as jnp
from jax import lax
from jax.experimental import pallas as pl
from jax.experimental.pallas import tpu as pltpu
from jax.sharding import PartitionSpec as P

HEADS = 16
HEAD_DIM = 64
epsilon = 1e-06
masked_score = -1e30
f32 = jnp.float32
bf16 = jnp.bfloat16
ALL = ("batch", "seq")


def rms_norm(values):
    return values * lax.rsqrt(jnp.mean(values * values, axis=-1, keepdims=True) + epsilon)


def modulated(hidden, scale_rows, shift_rows):
    return rms_norm(hidden) * (1.0 + scale_rows) + shift_rows


def gelu_tanh(pre_values):
    return jax.nn.gelu(pre_values, approximate=True)


def time_embed(flow_times, embed_width):
    half_width = embed_width // 2
    frequency = jnp.exp(-math.log(10000.0) * jnp.arange(half_width, dtype=f32) / half_width)
    angles = 1000.0 * flow_times[:, None] * frequency[None, :]
    return jnp.concatenate([jnp.sin(angles), jnp.cos(angles)], axis=-1)


def params(semantics=None):
    return pltpu.CompilerParams(dimension_semantics=semantics, vmem_limit_bytes=60 * 1024 * 1024)


class Net:
    def __init__(self, batch, seq):
        self.batch, self.seq, self.n = batch, seq, batch * seq
        self.d = lax.axis_index("batch") * seq + lax.axis_index("seq")
        self.b = lax.axis_index("batch")
        self.s = lax.axis_index("seq")
        self.core = self.d & 1

    def swap(self, value, offset):
        return lax.ppermute(value, ALL, [(i, i ^ offset) for i in range(self.n)])

    def swap_by_core(self, value, even, odd):
        pairs = [(i, i ^ (odd if i & 1 else even)) for i in range(self.n)]
        return lax.ppermute(value, ALL, pairs)

    def sum_all(self, value):
        bit = 1
        while bit < self.n:
            value = value + self.swap(value, bit)
            bit *= 2
        return value


def cost(flops, moved, exps=0):
    return pl.CostEstimate(flops=int(flops), bytes_accessed=int(moved), transcendentals=int(exps))


def after(value, *others):
    return lax.optimization_barrier((value,) + tuple(others))[0]


def gate(*values):
    return lax.optimization_barrier(values)


def place(pieces, tables, count, columns=None):
    rows, width = pieces[0].shape[1:]
    columns = columns or (width,)
    counts = [p.shape[0] for p in pieces]
    total = sum(counts)
    table = jnp.concatenate(tables, axis=-1).astype(jnp.int32)
    if table.ndim == 1:
        table = jnp.broadcast_to(table[None], (len(columns), total))

    def kernel(table_ref, *refs):
        sources = refs[: len(pieces)]
        outs = refs[len(pieces) : len(pieces) + len(columns)]
        sems = refs[-1]
        copies = []
        at = 0
        for source, number in zip(sources, counts):
            for j in range(number):
                left = 0
                for o, wide in enumerate(columns):
                    copies.append(
                        pltpu.make_async_copy(
                            source.at[j, :, pl.ds(left, wide)],
                            outs[o].at[table_ref[o, at]],
                            sems.at[o, at],
                        )
                    )
                    left += wide
                at += 1
        for copy in copies:
            copy.start()
        for copy in copies:
            copy.wait()

    any_spec = pl.BlockSpec(memory_space=pl.ANY)
    outs = pl.pallas_call(
        kernel,
        out_shape=[jax.ShapeDtypeStruct((count, rows, wide), pieces[0].dtype) for wide in columns],
        in_specs=[pl.BlockSpec(memory_space=pltpu.SMEM)] + [any_spec] * len(pieces),
        out_specs=[pl.BlockSpec(memory_space=pltpu.VMEM)] * len(columns),
        scratch_shapes=[pltpu.SemaphoreType.DMA((len(columns), total))],
        compiler_params=params(),
        cost_estimate=cost(0, 4 * count * rows * width),
    )(table, *pieces)
    return [out.reshape(count * rows, wide) for out, wide in zip(outs, columns)]


class Gather:
    def __init__(self, net, shard, received=None):
        self.net = net
        received = received or [net.swap(shard, k << 3) for k in (1, 2, 3)]
        self.near = jnp.stack([shard] + list(received))

    def far(self):
        self.half = jnp.concatenate([self.near, self.net.swap_by_core(self.near, 2, 4)])
        self.mate_half = self.net.swap(self.half, 1)

    def last(self):
        self.other = self.net.swap_by_core(self.half, 4, 2)

    def mates(self):
        self.mate_other = self.net.swap(self.other, 1)

    def blocks(self):
        d = self.net.d
        z = jnp.arange(4, dtype=jnp.int32) << 3
        second = jnp.where(self.net.core == 0, 2, 4)
        third = 6 - second
        own = jnp.concatenate([d ^ z, d ^ z ^ second])
        mate = d ^ 1
        mate_own = jnp.concatenate([mate ^ z, mate ^ z ^ third])
        return (
            [self.half, self.other, self.mate_half, self.mate_other],
            [own, own ^ third, mate_own, mate_own ^ second],
        )


def grad_blocks(net, lefts, rights, segments, packed_rows, turns=None):
    depth = lefts[0].shape[0]
    tile = 1024
    piece = 32
    chip = net.d >> 1
    rel = jnp.arange(16, dtype=jnp.int32) ^ chip
    x_bit, y_bit, z = rel & 1, (rel >> 1) & 1, rel >> 2
    even = y_bit * 8 + x_bit * 4 + z
    odd = x_bit * 8 + y_bit * 4 + z
    mine = jnp.where(net.core == 0, even, odd)
    other = jnp.where(net.core == 0, odd, even)
    extra = jnp.stack([net.core] + (turns or [net.core * 0] * len(segments)))
    extra = jnp.pad(extra, (0, 16 - extra.shape[0]))
    table = jnp.stack([mine, other, extra]).astype(jnp.int32)
    starts = [0]
    for seg in segments:
        starts.append(starts[-1] + seg[0])
    steps = starts[-1]
    number = len(segments)

    def kernel(table_ref, *refs):
        left_refs, right_refs = refs[:number], refs[number : 2 * number]
        keep, send, scratch, sems = refs[2 * number :]
        t = pl.program_id(0)
        slot = t % 2
        core = table_ref[2, 0]

        def copy(v, p, at_slot, source_row, pos, dest_row):
            dest = send if p else keep
            return pltpu.make_async_copy(
                scratch.at[at_slot, pl.ds(pl.multiple_of(source_row, piece), piece)],
                dest.at[pos, pl.ds(pl.multiple_of(dest_row, piece), piece)],
                sems.at[at_slot, p, v],
            )

        def wait_slot(at_slot):
            for v in range(16):
                for p in range(2):
                    copy(v, p, at_slot, 0, 0, 0).wait()

        @pl.when(t >= 2)
        def _():
            wait_slot(slot)

        left, right = left_refs[-1][...], right_refs[-1][...]
        for i in range(number - 2, -1, -1):
            early = t < starts[i + 1]
            left = jnp.where(early, left_refs[i][...], left)
            right = jnp.where(early, right_refs[i][...], right)
        scratch[slot] = lax.dot_general(
            left, right, (((0,), (0,)), ((), ())), preferred_element_type=f32
        ).astype(bf16)
        for v in range(16):
            for p in range(2):
                side = core ^ p
                chip_at = source = dest_row = jnp.int32(0)
                for i, (_, subs, base, rise) in reversed(list(enumerate(segments))):
                    local = t - starts[i]
                    here = (
                        (local * (16 // subs) % 16 + v // subs) ^ table_ref[2, 1 + i],
                        (2 * (v // subs) + side) * subs * piece + (v % subs) * piece,
                        base + local * rise + (v % subs) * piece,
                    )
                    if i == number - 1:
                        chip_at, source, dest_row = here
                    else:
                        early = t < starts[i + 1]
                        chip_at = jnp.where(early, here[0], chip_at)
                        source = jnp.where(early, here[1], source)
                        dest_row = jnp.where(early, here[2], dest_row)
                copy(v, p, slot, source, table_ref[p, chip_at], dest_row).start()

        @pl.when(t == steps - 1)
        def _():
            wait_slot(slot)
            if steps > 1:
                wait_slot(1 - slot)

    def spec(array, i):
        count = array.shape[1] // tile
        if count == 1:
            return pl.BlockSpec((depth, tile), lambda t, table: (0, 0))
        return pl.BlockSpec(
            (depth, tile), lambda t, table: (0, jnp.clip(t - starts[i], 0, count - 1))
        )

    any_spec = pl.BlockSpec(memory_space=pl.ANY)
    shape = jax.ShapeDtypeStruct((16, packed_rows, tile), bf16)
    return pl.pallas_call(
        kernel,
        out_shape=[shape, shape],
        grid_spec=pltpu.PrefetchScalarGridSpec(
            num_scalar_prefetch=1,
            grid=(steps,),
            in_specs=[spec(a, i) for i, a in enumerate(lefts)]
            + [spec(a, i) for i, a in enumerate(rights)],
            out_specs=[any_spec, any_spec],
            scratch_shapes=[
                pltpu.VMEM((2, tile, tile), bf16),
                pltpu.SemaphoreType.DMA((2, 2, 16)),
            ],
        ),
        compiler_params=params(("arbitrary",)),
        cost_estimate=cost(2 * steps * depth * tile * tile, 3 * steps * tile * tile * 2),
    )(table, *lefts, *rights)


def total(*parts):
    result = parts[0].astype(f32)
    for part in parts[1:]:
        result = result + part.astype(f32)
    return result


class Scatter:
    def __init__(self, net, keep, send):
        self.net, self.parts = net, [keep]
        self.parts.append(net.swap(send, 1))

    def halve(self, low, high, even, odd):
        out = total(*[p[low:high] for p in self.parts]).astype(bf16)
        self.out = out
        self.pair = (even, odd)
        return out

    def push(self, out):
        self.parts.append(self.net.swap_by_core(out, *self.pair))

    def z_sums(self):
        self.outs = [total(*[p[k : k + 1] for p in self.parts]).astype(bf16) for k in (1, 2, 3)]
        return self.outs

    def z_push(self):
        self.zs = [self.net.swap(o, (k + 1) << 3) for k, o in enumerate(self.outs)]

    def finish(self):
        return total(*[p[0:1] for p in self.parts], *self.zs)[0]


class UtteranceRows:
    def __init__(self, net, row):
        self.net, self.parts = net, [row] + [net.swap(row, k) for k in (1, 2, 3)]

    def across_z(self):
        row = sum(self.parts[1:], self.parts[0])
        self.parts = [row] + [self.net.swap(row, k << 3) for k in (1, 2, 3)]

    def across_y(self):
        self.parts = [jnp.concatenate(self.parts)]
        self.parts.append(self.net.swap(self.parts[0], 4))

    def rows(self):
        return jnp.stack(self.parts, axis=1).reshape(8, self.parts[0].shape[1])


def spread_columns(parts, order, groups):
    rows, width = parts[0].shape
    number = len(parts)
    wide = width // groups

    def kernel(order_ref, *refs):
        out, sems = refs[number:]
        copies = []
        for i in range(number):
            for g in range(groups):
                at = pl.multiple_of((order_ref[i] + g * number) * wide, wide)
                copies.append(
                    pltpu.make_async_copy(
                        refs[i].at[:, pl.ds(g * wide, wide)],
                        out.at[:, pl.ds(at, wide)],
                        sems.at[i, g],
                    )
                )
        for copy in copies:
            copy.start()
        for copy in copies:
            copy.wait()

    return pl.pallas_call(
        kernel,
        out_shape=jax.ShapeDtypeStruct((rows, width * number), parts[0].dtype),
        in_specs=[pl.BlockSpec(memory_space=pltpu.SMEM)]
        + [pl.BlockSpec(memory_space=pltpu.VMEM)] * number,
        out_specs=pl.BlockSpec(memory_space=pltpu.VMEM),
        scratch_shapes=[pltpu.SemaphoreType.DMA((number, groups))],
        compiler_params=params(),
        cost_estimate=cost(0, 8 * rows * width * number),
    )(order.astype(jnp.int32), *parts)


def rope(values, cosine, sine, back):
    width = values.shape[-1]
    lane = lax.broadcasted_iota(jnp.int32, values.shape, 1)
    early = (lane & (HEAD_DIM - 1)) < HEAD_DIM // 2
    source = values * sine if back else values
    ahead = pltpu.roll(source, width - HEAD_DIM // 2, 1)
    behind = pltpu.roll(source, HEAD_DIM // 2, 1)
    if back:
        turned = jnp.where(early, ahead, -behind)
        return values * cosine + turned
    turned = jnp.where(early, -ahead, behind)
    return values * cosine + turned * sine


def wide_tables(cos_ref, sin_ref, width):
    reps = width // cos_ref.shape[-1]
    cosine = jnp.concatenate([cos_ref[...]] * reps, axis=-1)
    sine = jnp.concatenate([sin_ref[...]] * reps, axis=-1)
    return cosine, sine


def qkv_kernel(number, *refs):
    w_ref, cos_ref, sin_ref, q_ref, k_ref, v_ref = refs[number:]
    width = q_ref.shape[-1]
    scale = HEAD_DIM ** (-0.5)
    for i in range(number):

        @pl.when(pl.program_id(0) == i)
        def _():
            result = jnp.dot(refs[i][...], w_ref[...], preferred_element_type=f32)
            cosine, sine = wide_tables(cos_ref, sin_ref, width)
            q_ref[...] = (rope(result[:, :width], cosine, sine, False) * scale).astype(bf16)
            k_ref[...] = rope(result[:, width : 2 * width], cosine, sine, False).astype(bf16)
            v_ref[...] = result[:, 2 * width :].astype(bf16)


def qkv_project(parts, w, cosine, sine):
    block, depth = parts[0].shape
    rows = block * len(parts)
    width = w.shape[1] // 3
    row = lambda wide: pl.BlockSpec((block, wide), lambda i: (i, 0))
    whole = lambda a: pl.BlockSpec(a.shape, lambda i: (0, 0))
    return pl.pallas_call(
        functools.partial(qkv_kernel, len(parts)),
        grid=(len(parts),),
        out_shape=[jax.ShapeDtypeStruct((rows, width), bf16)] * 3,
        in_specs=[whole(a) for a in parts] + [whole(w), row(128), row(128)],
        out_specs=[row(width)] * 3,
        compiler_params=params(("arbitrary",)),
        cost_estimate=cost(2 * rows * depth * 3 * width, 2 * rows * (depth + 3 * width)),
    )(*parts, w, cosine, sine)


def qkv_back(pieces, w, local, first, dtype):
    rows = pieces[0].shape[0]
    wide = pieces[0].shape[1]
    count = rows // local // 2
    width = len(pieces) * wide

    def kernel(*refs):
        w_ref, all_ref, out_ref = refs[len(pieces) :]
        joined = jnp.concatenate([r[...] for r in refs[: len(pieces)]], axis=-1)
        all_ref[...] = joined
        out_ref[...] = lax.dot_general(
            joined, w_ref[...], (((1,), (1,)), ((), ())), preferred_element_type=f32
        ).astype(dtype)

    return pl.pallas_call(
        kernel,
        grid=(count,),
        out_shape=[
            jax.ShapeDtypeStruct((count * local, width), bf16),
            jax.ShapeDtypeStruct((count * local, w.shape[0]), dtype),
        ],
        in_specs=[pl.BlockSpec((local, wide), lambda i: (2 * i + first, 0))] * len(pieces)
        + [pl.BlockSpec(w.shape, lambda i: (0, 0))],
        out_specs=[
            pl.BlockSpec((local, width), lambda i: (i, 0)),
            pl.BlockSpec((local, w.shape[0]), lambda i: (i, 0)),
        ],
        compiler_params=params(("arbitrary",)),
        cost_estimate=cost(2 * count * local * width * w.shape[0], 8 * count * local * w.shape[0]),
    )(*pieces, w)


def qkv_grad_blocks(net, lefts, grads):
    local, depth = lefts[0].shape
    width = grads[0].shape[1]
    rows = depth // 8
    t = jnp.arange(8, dtype=jnp.int32)
    table = net.b ^ ((t & 3) << 1) ^ jnp.where(t < 4, 1, 0)
    number = len(lefts)

    def kernel(table_ref, *refs):
        keep, send = refs[number + len(grads) :]
        result = jnp.zeros((rows, width), f32)
        for i in range(number):
            grad = refs[number + i % 2][(i // 2) * local : (i // 2 + 1) * local]
            result = result + lax.dot_general(
                refs[i][...], grad, (((0,), (0,)), ((), ())), preferred_element_type=f32
            )
        result = result.astype(bf16)[None]
        step = pl.program_id(0)

        @pl.when(step < 4)
        def _():
            send[...] = result

        @pl.when(step >= 4)
        def _():
            keep[...] = result

    shape = jax.ShapeDtypeStruct((4, rows, width), bf16)
    block = (1, rows, width)
    return pl.pallas_call(
        kernel,
        out_shape=[shape, shape],
        grid_spec=pltpu.PrefetchScalarGridSpec(
            num_scalar_prefetch=1,
            grid=(8,),
            in_specs=[pl.BlockSpec((local, rows), lambda i, t: (0, t[i]))] * number
            + [pl.BlockSpec(g.shape, lambda i, t: (0, 0)) for g in grads],
            out_specs=[
                pl.BlockSpec(block, lambda i, t: (jnp.maximum(i - 4, 0), 0, 0)),
                pl.BlockSpec(block, lambda i, t: (jnp.minimum(i, 3), 0, 0)),
            ],
        ),
        compiler_params=params(("arbitrary",)),
        cost_estimate=cost(2 * number * local * depth * width, 4 * depth * width),
    )(table, *lefts, *grads)


def attend_kernel(heads, q_ref, k_ref, v_ref, bias_ref, o_ref, lse_ref):
    q = q_ref[...]
    k = k_ref[...]
    v = v_ref[...]
    bias = bias_ref[...]
    lane = lax.broadcasted_iota(jnp.int32, q.shape, 1) // HEAD_DIM
    spot = lax.broadcasted_iota(jnp.int32, lse_ref.shape, 1)
    out = jnp.zeros(q.shape, f32)
    lse = jnp.zeros(lse_ref.shape, f32)
    for h in range(heads):
        mine = lane == h
        qh = jnp.where(mine, q, jnp.zeros_like(q))
        s = lax.dot_general(qh, k, (((1,), (1,)), ((), ())), preferred_element_type=f32) + bias
        top = jnp.max(s, axis=-1, keepdims=True)
        p = jnp.exp(s - top)
        total = jnp.sum(p, axis=-1, keepdims=True)
        o = jnp.dot(p.astype(bf16), v, preferred_element_type=f32) / total
        out = jnp.where(mine, o, out)
        lse = jnp.where(spot == h, top + jnp.log(total), lse)
    o_ref[...] = out.astype(bf16)
    lse_ref[...] = lse


def attend(q, k, v, bias, heads):
    rows, width = q.shape
    block = 256
    row = lambda wide: pl.BlockSpec((block, wide), lambda i: (i, 0))
    whole = pl.BlockSpec((rows, width), lambda i: (0, 0))
    return pl.pallas_call(
        functools.partial(attend_kernel, heads),
        grid=(rows // block,),
        out_shape=[jax.ShapeDtypeStruct((rows, width), bf16), jax.ShapeDtypeStruct((rows, 128), f32)],
        in_specs=[row(width), whole, whole, pl.BlockSpec((1, rows), lambda i: (0, 0))],
        out_specs=[row(width), row(128)],
        compiler_params=params(("arbitrary",)),
        cost_estimate=cost(
            16 * rows * rows * heads * HEAD_DIM, 8 * rows * width, rows * rows * heads
        ),
    )(q, k, v, bias)


def attend_back_kernel(
    heads,
    first,
    q_ref,
    do_ref,
    o_ref,
    lse_ref,
    k_ref,
    v_ref,
    kt_ref,
    bias_ref,
    cosq_ref,
    sinq_ref,
    cosk_ref,
    sink_ref,
    dq_ref,
    dk_ref,
    dv_ref,
    p_all,
    ds_all,
    dk_acc,
    dv_acc,
):
    step = pl.program_id(0)
    q = q_ref[...]
    do = do_ref[...]
    k = k_ref[...]
    v = v_ref[...]
    block, width = q.shape
    lane = lax.broadcasted_iota(jnp.int32, q.shape, 1) // HEAD_DIM
    product = (do.astype(f32) * o_ref[...].astype(f32)).T
    lse_t = lse_ref[...].T
    bias = bias_ref[...]
    contract = (((1,), (1,)), ((), ()))
    q_parts, do_parts, dq_parts = [], [], []
    for h in range(heads):
        mine = lane == h
        qh = jnp.where(mine, q, jnp.zeros_like(q))
        doh = jnp.where(mine, do, jnp.zeros_like(do))
        q_parts.append(qh)
        do_parts.append(doh)
        row_dot = jnp.sum(product[h * HEAD_DIM : (h + 1) * HEAD_DIM], axis=0, keepdims=True)
        s = lax.dot_general(k, qh, contract, preferred_element_type=f32)
        p = jnp.exp(s + bias - lse_t[first + h : first + h + 1])
        dp = lax.dot_general(v, doh, contract, preferred_element_type=f32)
        ds = (p * (dp - row_dot)).astype(bf16)
        p_all[:, h * block : (h + 1) * block] = p.astype(bf16)
        ds_all[:, h * block : (h + 1) * block] = ds
        dq_parts.append(
            jnp.dot(kt_ref[h * HEAD_DIM : (h + 1) * HEAD_DIM, :], ds, preferred_element_type=f32)
        )
    dv = jnp.dot(p_all[...], jnp.concatenate(do_parts, axis=0), preferred_element_type=f32)
    dk = jnp.dot(ds_all[...], jnp.concatenate(q_parts, axis=0), preferred_element_type=f32)

    @pl.when(step == 0)
    def _():
        dv_acc[...] = dv
        dk_acc[...] = dk

    @pl.when(step > 0)
    def _():
        dv_acc[...] += dv
        dk_acc[...] += dk

    dq = jnp.concatenate(dq_parts, axis=0).T
    cosine, sine = wide_tables(cosq_ref, sinq_ref, width)
    dq_ref[...] = (rope(dq, cosine, sine, True) * (HEAD_DIM ** (-0.5))).astype(bf16)

    @pl.when(step == pl.num_programs(0) - 1)
    def _():
        cosine, sine = wide_tables(cosk_ref, sink_ref, width)
        dk_ref[...] = rope(dk_acc[...], cosine, sine, True).astype(bf16)
        dv_ref[...] = dv_acc[...].astype(bf16)


def attend_back(q, k, v, o, do, lse, k_turned, bias, cosine, sine, heads, group):
    rows = q.shape[0]
    width = heads * HEAD_DIM
    block = 256
    lanes = lambda wide: pl.BlockSpec((block, wide), lambda i: (i, group))
    row = lambda wide: pl.BlockSpec((block, wide), lambda i: (i, 0))
    whole = lambda wide, at: pl.BlockSpec((rows, wide), lambda i: (0, at))
    out = jax.ShapeDtypeStruct((rows, width), bf16)
    return pl.pallas_call(
        functools.partial(attend_back_kernel, heads, group * heads),
        grid=(rows // block,),
        out_shape=[out] * 3,
        in_specs=[
            lanes(width),
            lanes(width),
            lanes(width),
            row(128),
            whole(width, group),
            whole(width, group),
            pl.BlockSpec((width, rows), lambda i: (group, 0)),
            whole(block, 0),
            row(128),
            row(128),
            whole(128, 0),
            whole(128, 0),
        ],
        out_specs=[row(width), whole(width, 0), whole(width, 0)],
        scratch_shapes=[
            pltpu.VMEM((rows, heads * block), bf16),
            pltpu.VMEM((rows, heads * block), bf16),
            pltpu.VMEM((rows, width), f32),
            pltpu.VMEM((rows, width), f32),
        ],
        compiler_params=params(("arbitrary",)),
        cost_estimate=cost(
            40 * rows * rows * heads * HEAD_DIM, 16 * rows * width, rows * rows * heads
        ),
    )(
        q,
        do,
        o,
        lse,
        k,
        v,
        k_turned,
        bias,
        cosine,
        sine,
        cosine,
        sine,
    )


def body(
    mesh_sizes,
    frames_in,
    skip_in,
    flow_times,
    lengths,
    skip_weight,
    qkv_weight,
    output_weight,
    up_weight,
    up_bias,
    down_weight,
    down_bias,
    modulate_weight,
    modulate_bias,
    output_grad,
):
    batch, seq = mesh_sizes
    net = Net(batch, seq)
    n, d, s = net.n, net.d, net.s
    local, utts, width = frames_in.shape
    frames = frames_in.reshape(local, width)
    skips = skip_in.reshape(local, width)
    out_grad = output_grad.reshape(local, width).astype(f32)
    heads = HEADS // seq
    part = heads * HEAD_DIM
    rows = local * seq
    built = n == 32 and seq == 4
    wrow = width // n
    ff = up_weight.shape[1]

    seq_order = s ^ jnp.arange(seq, dtype=jnp.int32)
    by_part = qkv_weight.reshape(wrow, 3, seq, part)
    pieces = [
        lax.dynamic_index_in_dim(by_part, s ^ k, 2, keepdims=False).reshape(wrow, 3 * part)
        for k in range(seq)
    ]
    urow, drow = up_bias.shape[0], down_bias.shape[0]
    if built:
        vectors = jnp.concatenate(
            [
                up_bias.reshape(1, urow),
                jnp.pad(down_bias, (0, urow - drow)).reshape(1, urow),
                jnp.zeros((wrow - 2, urow), bf16),
            ]
        )
        pieces = [jnp.concatenate([p, vectors], axis=1) for p in pieces]
    pieces = [p if k == 0 else net.swap(p, k) for k, p in enumerate(pieces)]
    if built:
        skip_gather = Gather(net, skip_weight)
        skip_gather.far()
        skip_gather.last()
        qkv_four = after(jnp.stack(pieces), skip_gather.other)
        qkv_far = [net.swap(qkv_four, k << 3) for k in (1, 2, 3)]
        skip_gather.mates()
        (full_skip,) = place(*skip_gather.blocks(), n)
        ou = jnp.concatenate([output_weight, up_weight], axis=1)
    else:
        gather = lambda w, ax: lax.all_gather(w, ax, axis=0, tiled=True)
        full_skip = gather(skip_weight, ALL)
        full_qkv = gather(jnp.stack(pieces)[seq_order], "batch")
        full_qkv = full_qkv.reshape(batch, seq, wrow, 3 * part)
        full_qkv = full_qkv.reshape(width, 3 * part)
        full_output = gather(output_weight, ALL).reshape(seq, width // seq, width)[seq_order]
        full_output = full_output.reshape(width, width)
        full_up = gather(up_weight, ALL)
        full_down = gather(down_weight, ALL)

    mod_bias = lax.dynamic_update_slice_in_dim(
        jnp.zeros((6 * width,), f32), modulate_bias.astype(f32), d * modulate_bias.shape[0], 0
    )
    if built:
        times = jnp.broadcast_to(flow_times.reshape(1, 1), (8, 128))
        times = [times] + [net.swap(times, k << 3) for k in (1, 2, 3)]
        *times, _ = gate(*times, skip_gather.half)
        times = jnp.concatenate([t[:1] for t in times] * 2)
        times = jnp.stack([times[:4], net.swap(times, 4)[:4]], axis=1).reshape(batch, 128)
        all_times = times[:, 0]
    else:
        small = jnp.concatenate([up_bias.astype(f32), down_bias.astype(f32), flow_times])
        small_width = -(-small.shape[0] // 128) * 128
        small = jnp.pad(small, (0, small_width - small.shape[0]))
        slots = lax.broadcasted_iota(jnp.int32, (n, small_width), 0)
        small = net.sum_all(jnp.where(slots == d, small[None], 0.0))
        full_up_bias = small[:, :urow].reshape(1, ff)
        full_down_bias = small[:, urow : urow + drow].reshape(1, width)
        all_times = small.reshape(batch, seq, small_width)[:, 0, urow + drow]
    feat = jax.nn.silu(time_embed(all_times, width)).astype(bf16)
    feat_own = lax.dynamic_slice_in_dim(feat, d * wrow, wrow, 1)
    modulation = jnp.dot(feat_own, modulate_weight, preferred_element_type=f32)
    modulation = modulation + mod_bias[None]
    if built:
        sums = modulation[0:2]
        for k in (1, 2, 3):
            sums = sums + net.swap(modulation[2 * k : 2 * k + 2], k << 3)
        sums = sums[0:1] + net.swap(sums[1:2], 4)
        modulation = sums
        for k in (1, 2, 3):
            modulation = modulation + net.swap(sums, k)
    else:
        bit = batch // 2
        while bit:
            high = (net.b & bit) // bit
            sent = lax.dynamic_slice_in_dim(modulation, (1 - high) * bit, bit, 0)
            kept = lax.dynamic_slice_in_dim(modulation, high * bit, bit, 0)
            modulation = kept + net.swap(sent, bit * seq)
            bit //= 2
        bit = 1
        while bit < seq:
            modulation = modulation + net.swap(modulation, bit)
            bit *= 2
    shift_one, scale_one, gate_one, shift_two, scale_two, gate_two = jnp.split(modulation, 6, -1)

    half_dim = HEAD_DIM // 2
    inverse = jnp.exp(-math.log(10000.0) * 2.0 * jnp.arange(half_dim, dtype=f32) / HEAD_DIM)
    positions = (
        seq_order[:, None] * local + jnp.arange(local, dtype=jnp.int32)[None]
    ).reshape(rows)
    angles = positions.astype(f32)[:, None] * jnp.tile(inverse, 128 // half_dim)[None]
    cosine, sine = jnp.cos(angles), jnp.sin(angles)
    key_bias = jnp.where(positions < lengths[0], 0.0, masked_score).astype(f32)[None]

    joined = jnp.concatenate([frames, skips], axis=-1)
    hidden_zero = jnp.dot(joined, full_skip, preferred_element_type=f32)
    normed_one = modulated(hidden_zero, scale_one, shift_one).astype(bf16)
    if built:
        normed_one, ou, *qkv_far = gate(normed_one, ou, *qkv_far)
        qkv_z = jnp.concatenate([qkv_four] + qkv_far)
        qkv_y = net.swap(qkv_z, 4)
        ou_gather = Gather(net, ou)
        k16 = jnp.arange(16, dtype=jnp.int32)
        z_spots = d ^ (((k16 >> 2) << 3) | (k16 & 3))
        full_qkv, vectors = place(
            [qkv_z, qkv_y], [z_spots, z_spots ^ 4], n, (3 * part, urow)
        )
    across = {0: normed_one}
    bit = seq // 2
    while bit:
        across.update({i | bit: net.swap(a, bit) for i, a in list(across.items())})
        if built and bit == 2:
            across[2], cosine, sine, full_qkv, ou_gather.near, down_own = gate(
                across[2], cosine, sine, full_qkv, ou_gather.near, down_weight
            )
            down_near = [net.swap(down_own, k << 3) for k in (1, 2, 3)]
        bit //= 2
    normed_parts = [across[i] for i in range(seq)]
    if built:
        ou_gather.far()
        vectors = vectors.reshape(n, wrow, urow)
        full_up_bias = vectors[:, 0].reshape(1, ff).astype(f32)
        full_down_bias = vectors[:, 1, :drow].reshape(1, width).astype(f32)
    q, k, v = qkv_project(normed_parts, full_qkv, cosine, sine)
    if built:
        q, ou_gather.half = gate(q, ou_gather.half)
        ou_gather.last()
    att, lse = attend(q, k, v, key_bias, heads)
    if built:
        att, ou_gather.other, ou_gather.mate_half, *down_near = gate(
            att, ou_gather.other, ou_gather.mate_half, *down_near
        )
        down_gather = Gather(net, down_own, down_near)
        down_gather.far()
        ou_gather.mates()
        got, spots = ou_gather.blocks()
        spots = jnp.concatenate(spots)
        turned = spots ^ (s * (n // seq))
        full_output, full_up = place(got, [jnp.stack([turned, spots])], n, (width, ff))
    blocks = [att[i * local : (i + 1) * local] for i in range(seq)]
    k_turned = k.T
    bias_wide = jnp.broadcast_to(key_bias.reshape(rows, 1), (rows, 256))
    blocks = [b if i == 0 else net.swap(b, i) for i, b in enumerate(blocks)]
    if built:
        *blocks, down_gather.half = gate(*blocks, down_gather.half)
        down_gather.last()
    *blocks, full_output, full_up, k_turned, bias_wide = gate(
        *blocks, full_output, full_up, k_turned, bias_wide
    )
    attended = jnp.concatenate(blocks, axis=-1)
    attn_proj = jnp.dot(attended, full_output, preferred_element_type=f32)
    hidden_one = hidden_zero + gate_one * attn_proj
    normed_two = modulated(hidden_one, scale_two, shift_two).astype(bf16)
    pre_act = jnp.dot(normed_two, full_up, preferred_element_type=f32) + full_up_bias
    activated = gelu_tanh(pre_act).astype(bf16)
    if built:
        down_gather.other, down_gather.mate_half, activated = gate(
            down_gather.other, down_gather.mate_half, activated
        )
        down_gather.mates()
        (full_down,) = place(*down_gather.blocks(), n)
    ffn_out = jnp.dot(activated, full_down, preferred_element_type=f32) + full_down_bias
    layer_out = (hidden_one + gate_two * ffn_out).astype(bf16)

    rows_dot = lambda a, b: lax.dot_general(
        a, b, (((0,), (0,)), ((), ())), preferred_element_type=f32
    )
    back_dot = lambda a, b: lax.dot_general(
        a, b, (((1,), (1,)), ((), ())), preferred_element_type=f32
    )

    def scattered(grads, turn=False):
        if turn:
            grads = grads.reshape(seq, width // seq, -1)[seq_order].reshape(grads.shape)
        return lax.psum_scatter(
            grads.astype(bf16), ALL, scatter_dimension=0, tiled=True
        ).astype(f32)

    ffn_grad = out_grad * gate_two
    down_bias_term = jnp.sum(ffn_grad, axis=0)
    ffn_grad_low = ffn_grad.astype(bf16)
    act_grad = back_dot(ffn_grad_low, full_down)
    pre_grad = jax.vjp(gelu_tanh, pre_act)[1](act_grad)[0]
    up_bias_term = jnp.sum(pre_grad, axis=0)
    pre_grad_low = pre_grad.astype(bf16)
    normed_two_grad = back_dot(pre_grad_low, full_up)
    pull_two = jax.vjp(modulated, hidden_one, scale_two, shift_two)[1]
    hidden_grad_two, scale_two_grad, shift_two_grad = pull_two(normed_two_grad)
    gate_two_grad = jnp.sum(out_grad * ffn_out, axis=0)
    hidden_one_grad = out_grad + hidden_grad_two
    gate_one_grad = jnp.sum(hidden_one_grad * attn_proj, axis=0)
    proj_grad_low = (hidden_one_grad * gate_one).astype(bf16)
    attended_grad = back_dot(proj_grad_low, full_output).astype(bf16)
    pieces = [attended_grad[:, i * part : (i + 1) * part] for i in range(seq)]
    grad_all = jnp.concatenate([p if i == 0 else net.swap(p, i) for i, p in enumerate(pieces)])
    pair = lambda i, grad: attend_back(
        q, k, v, att, grad, lse, k_turned, bias_wide, cosine, sine, 2, i
    )
    if built:
        early_row = jnp.concatenate(
            [
                v.reshape(1, -1)
                for v in (
                    gate_one_grad,
                    shift_two_grad,
                    scale_two_grad,
                    gate_two_grad,
                    up_bias_term,
                    down_bias_term,
                )
            ],
            axis=1,
        )
        activated, attended_grad = lax.optimization_barrier((activated, attended_grad))
        down = Scatter(net, *grad_blocks(net, [activated], [ffn_grad_low], [(4, 4, 0, 0)], 128))
        normed_two = after(normed_two, down.parts[0])
        up = Scatter(
            net,
            *grad_blocks(
                net,
                [normed_two, attended],
                [pre_grad_low, proj_grad_low],
                [(4, 1, 0, 32), (1, 1, 128, 0)],
                160,
                [s * 0, s * (n // seq // 2)],
            ),
        )
        down_half = down.halve(8, 16, 4, 2)
        down.push(down_half)
        grad_all, down_half, early_row, _ = lax.optimization_barrier(
            (grad_all, down_half, early_row, up.parts[0])
        )
        early = UtteranceRows(net, early_row)
        first = pair(0, grad_all)
        up.parts[1], down.parts[2], first, *early.parts = gate(
            up.parts[1], down.parts[2], first, *early.parts
        )
        early.across_z()
        up_half = up.halve(8, 16, 4, 2)
        up.push(up_half)
        down_half = down.halve(4, 8, 2, 4)
        down.push(down_half)
        grad_all, _ = gate(grad_all, (up_half, down_half, first))
        second = pair(1, grad_all)
        up.parts[2], down.parts[3], second = gate(up.parts[2], down.parts[3], second)
        results = [first, second]
    else:
        grad_down_weight = scattered(rows_dot(activated, ffn_grad_low))
        grad_up_weight = scattered(rows_dot(normed_two, pre_grad_low))
        grad_output_weight = scattered(rows_dot(attended, proj_grad_low), True)
        results = [pair(i, grad_all) for i in range(heads // 2)]
    pieces = [r[i] for i in range(3) for r in results]
    odd_grad, odd = qkv_back(pieces, full_qkv, local, 1, bf16)
    sent = net.swap(odd, 1)
    even_grad, even = qkv_back(pieces, full_qkv, local, 0, f32)
    halves = [
        even[i * local : (i + 1) * local] + sent[i * local : (i + 1) * local].astype(f32)
        for i in range(seq // 2)
    ]
    if built:
        give = halves[1].astype(bf16)
        taken = net.swap(give, 2)
        down.parts[2], down.parts[3], give = gate(down.parts[2], down.parts[3], give)
        down_sums = down.z_sums()
        down.z_push()
        *normed_parts, _, _ = gate(*normed_parts, give, down_sums)
        keep, send = qkv_grad_blocks(net, normed_parts, [even_grad, odd_grad])
        got = net.swap(send, 4)
        up.parts[2], keep = gate(up.parts[2], keep)
        up_quarter = up.halve(4, 8, 2, 4)
        up.push(up_quarter)
        taken, _, *down.zs = gate(taken, up_quarter, *down.zs)
        normed_one_grad = halves[0] + taken.astype(f32)
    else:
        step = 2
        while len(halves) > 1:
            kept = halves[0::2]
            give = halves[1::2]
            halves = [
                a + net.swap(g.astype(bf16), step).astype(f32) for a, g in zip(kept, give)
            ]
            step *= 2
        normed_one_grad = halves[0]
        qkv_part = sum(
            rows_dot(a, (odd_grad if i % 2 else even_grad)[(i // 2) * local : (i // 2 + 1) * local])
            for i, a in enumerate(normed_parts)
        ).astype(bf16)
        own = lax.psum_scatter(qkv_part, "batch", scatter_dimension=0, tiled=True).astype(f32)

    pull_one = jax.vjp(modulated, hidden_zero, scale_one, shift_one)[1]
    hidden_grad_one, scale_one_grad, shift_one_grad = pull_one(normed_one_grad)
    hidden_zero_grad = (hidden_one_grad + hidden_grad_one).astype(bf16)
    if built:
        hidden_zero_grad, got = gate(hidden_zero_grad, got)
        late = UtteranceRows(
            net, jnp.concatenate([shift_one_grad.reshape(1, -1), scale_one_grad.reshape(1, -1)], axis=1)
        )
        skip = Scatter(
            net,
            *grad_blocks(
                net,
                [frames, skips],
                [hidden_zero_grad, hidden_zero_grad],
                [(1, 2, 0, 0), (1, 2, 0, 0)],
                64,
                [s * 0, s * 0 + 8],
            ),
        )
        got, skip.parts[0] = gate(got, skip.parts[0])
        qkv_sums = [total(keep[i], got[i]).astype(bf16) for i in (1, 2, 3)]
        qkv_zs = [net.swap(v, (i + 1) << 3) for i, v in enumerate(qkv_sums)]
        skip.parts[1] = after(skip.parts[1], qkv_sums)
        skip_half = skip.halve(8, 16, 4, 2)
        skip.push(skip_half)
        up.parts[3], hidden_zero_grad, skip_half, *rest = gate(
            up.parts[3], hidden_zero_grad, skip_half, *late.parts, *early.parts
        )
        late.parts, early.parts = rest[:4], rest[4:]
        up_sums = up.z_sums()
        up.z_push()
        late.across_z()
        skip.parts[2] = after(skip.parts[2], up_sums)
        skip_quarter = skip.halve(4, 8, 2, 4)
        skip.push(skip_quarter)
        *early.parts, _ = gate(*early.parts, skip_quarter)
        early.across_y()
        keep, got, skip_quarter, late.parts[0], *rest = gate(
            keep, got, skip_quarter, late.parts[0], *qkv_zs, *late.parts[1:]
        )
        qkv_zs, late.parts[1:] = rest[:3], rest[3:]
        own = total(keep[0], got[0], *qkv_zs)
        late.across_y()
    own = own.reshape(seq, wrow, 3 * part)
    cols = [lax.dynamic_index_in_dim(own, s ^ i, 0, keepdims=False) for i in range(seq)]
    cols = [c if i == 0 else net.swap(c, i) for i, c in enumerate(cols)]
    if built:
        skip.parts[3] = after(skip.parts[3], own)
        skip_sums = skip.z_sums()
        skip.z_push()
        down.parts[0] = after(down.parts[0], skip_sums)
        up.parts[0] = after(up.parts[0], skip_sums)
        grad_down_weight = down.finish()
        own = up.finish()
        grad_up_weight = jnp.concatenate(
            [own[i * wrow : (i + 1) * wrow] for i in range(4)], axis=1
        )
        grad_output_weight = own[4 * wrow :]
        grad_skip_weight = skip.finish()
    else:
        grad_skip_weight = scattered(rows_dot(joined, hidden_zero_grad))
    grad_qkv_weight = spread_columns(cols, seq_order, 3)
    grad_joined = back_dot(hidden_zero_grad, full_skip)
    grad_frames, grad_skip = grad_joined[:, :width], grad_joined[:, width:]

    def by_utterance(*vectors):
        row = jnp.concatenate([vec.reshape(1, -1) for vec in vectors], axis=1)
        place_row = lax.broadcasted_iota(jnp.int32, (batch, row.shape[1]), 0)
        return jnp.where(place_row == net.b, row, 0.0)

    if built:
        early, late = early.rows(), late.rows()
        sums = jnp.sum(early[:, 4 * width :], axis=0)
        up_sum, down_sum = sums[:ff], sums[ff:]
        early = early[:, : 4 * width]
    else:
        early = by_utterance(gate_one_grad, shift_two_grad, scale_two_grad, gate_two_grad)
        flat = jnp.concatenate([early.reshape(-1), up_bias_term, down_bias_term])
        flat = net.sum_all(flat.reshape(-1, 128)).reshape(-1)
        early = flat[: batch * 4 * width].reshape(batch, 4 * width)
        up_sum = flat[batch * 4 * width : batch * 4 * width + ff]
        down_sum = flat[batch * 4 * width + ff :]
        late = net.sum_all(by_utterance(shift_one_grad, scale_one_grad))
    grad_up_bias = lax.dynamic_slice_in_dim(up_sum, d * urow, urow, 0)
    grad_down_bias = lax.dynamic_slice_in_dim(down_sum, d * drow, drow, 0)
    mod_grad = jnp.concatenate([late, early], axis=1)
    grad_modulate_weight = lax.dot_general(
        feat_own.astype(f32),
        mod_grad,
        (((0,), (0,)), ((), ())),
        precision=lax.Precision.HIGHEST,
        preferred_element_type=f32,
    )
    mod_width = modulate_bias.shape[0]
    grad_modulate_bias = jnp.sum(
        lax.dynamic_slice_in_dim(mod_grad, d * mod_width, mod_width, 1), axis=0
    )
    shape = (local, utts, width)
    return (
        layer_out.reshape(shape),
        grad_frames.reshape(shape),
        grad_skip.reshape(shape),
        grad_skip_weight,
        grad_qkv_weight,
        grad_output_weight,
        grad_up_weight,
        grad_up_bias,
        grad_down_weight,
        grad_down_bias,
        grad_modulate_weight,
        grad_modulate_bias,
    )


def solution(mesh):
    rows_two = P("seq", "batch", None)
    owned = P(ALL, None)
    vector = P(ALL)
    in_specs = (
        rows_two,
        rows_two,
        P("batch"),
        P("batch"),
        owned,
        owned,
        owned,
        owned,
        vector,
        owned,
        vector,
        owned,
        vector,
        rows_two,
    )
    out_specs = (
        rows_two,
        rows_two,
        rows_two,
        owned,
        owned,
        owned,
        owned,
        vector,
        owned,
        vector,
        owned,
        vector,
    )
    sizes = (mesh.shape["batch"], mesh.shape["seq"])
    return jax.shard_map(
        functools.partial(body, sizes),
        mesh=mesh,
        in_specs=in_specs,
        out_specs=out_specs,
        check_vma=False,
    )
```
